32 devices in a mesh: dp: 4 (over y, x), seq: 8 (over z, core).
Axes of the slice: x: 2, y: 2, z: 4, core: 2. Of those that a mesh axis runs over, the one named last changes fastest.
Arguments:
- tokens: bfloat16 [4, 16, 16, 4, 512], P('dp', 'seq'), may hold values from -6 to 6
- conv_first: bfloat16 [27, 512, 128], replicated, may hold values from -0.0546875 to 0.0546875
- bias_first: float32 [128], replicated, may hold values from -3 to 3
- conv_second: bfloat16 [27, 128, 384], replicated, may hold values from -0.109375 to 0.109375
- bias_second: float32 [384], replicated, may hold values from -3 to 3
- pixels: bfloat16 [4, 16, 16, 4, 1536], P('dp', None, 'seq'), may hold values from 0 to 1
- mask_index: int32 [4, 57], P('dp'), may hold values from 0 to 63, as said below
Outputs:
- grad_first: float32 [27, 512, 128], P(None, 'seq', 'dp')
- grad_second: float32 [27, 128, 384], P(None, 'seq', 'dp')
The draws below stay inside these ranges and needn't reach their ends.
Inputs may be any that keep to these rules, and one draw needn't show every extreme that they name: `mask_index`: each row holds 57 distinct positions of the 16 x 4 token grid.
All inputs are finite; a program needn't handle non-finite values.
Results may differ from the reference program's by a relative error of at most 0.003.
Values may be sent and summed in bfloat16 or wider, within the bound.
A program may use at most 128 MiB of HBM per device.

```python
from functools import partial
import jax
import jax.numpy as jnp
from jax import lax

D = 512
C1 = 128
CO = 384
T_SIZE = 16
W = 4
H = 16
CLIPS = 4
MASKED = 57


def draw_mask_index(key, part):
    clip_keys = jax.random.split(jax.random.fold_in(key, 17), CLIPS)
    orders = jax.vmap(lambda one_key: jax.random.permutation(one_key, H * W))(clip_keys)
    return orders[:, :MASKED].astype(jnp.int32)


def level_of(own_key, shape, cuts, low, high):
    loudness, own = 1.0, jax.random.fold_in(own_key, 6)
    for position, blocks in cuts:
        heights = jnp.exp(jax.random.uniform(jax.random.fold_in(own, position), (blocks,), jnp.float32, low / len(cuts), high / len(cuts)))
        loudness = loudness * jnp.repeat(heights, shape[position] // blocks).reshape([-1 if axis == position else 1 for axis in range(len(shape))])
    return loudness


def gaussian(own_key, extent, scale, limit, cuts=(), kind=jnp.bfloat16):
    level = level_of(own_key, extent, cuts, -0.22, 0.18) if cuts else 1.0
    drawn = jax.random.normal(own_key, extent, jnp.float32) * scale * level
    return jnp.minimum(jnp.maximum(drawn, -limit), limit).astype(kind)


def setup_inputs(seed: int = 0) -> dict:
    key_list = jax.random.split(jax.random.key(seed), 8)
    return {
        "tokens": gaussian(key_list[0], (CLIPS, T_SIZE, H, W, D), 1.0, 6.0, ((0, 4), (1, 8))),
        "conv_first": gaussian(key_list[1], (27, D, C1), (27 * D) ** -0.5, 0.0546875),
        "bias_first": gaussian(key_list[2], (C1,), 0.5, 3.0, (), jnp.float32),
        "conv_second": gaussian(key_list[3], (27, C1, CO), (27 * C1) ** -0.5, 0.109375),
        "bias_second": gaussian(key_list[4], (CO,), 0.5, 3.0, (), jnp.float32),
        "pixels": jnp.clip(1.0 * jax.random.uniform(key_list[5], (CLIPS, T_SIZE, H, W, 4 * CO), jnp.float32) ** level_of(key_list[5], (CLIPS, T_SIZE, H, W, 4 * CO), ((0, 4), (2, 8)), -0.2, 0.2), 0.0, 1.0).astype(jnp.bfloat16),
        "mask_index": draw_mask_index(jax.random.fold_in(key_list[7], 71), 0),
    }


def shifts_of(tap_index):
    return (tap_index // 9, tap_index // 3 % 3, tap_index % 3)

def pad_full(field):
    return jnp.pad(field, ((1, 1), (1, 1), (1, 1), (0, 0)))

def conv_taps(padded, weight):
    frames = padded.shape[0] - 2
    rows = padded.shape[1] - 2
    cols = padded.shape[2] - 2
    summed = jnp.zeros((frames * rows * cols, weight.shape[2]), jnp.float32)
    for tap_index in range(27):
        shift_time, shift_row, shift_col = shifts_of(tap_index)
        window = padded[shift_time:shift_time + frames, shift_row:shift_row + rows, shift_col:shift_col + cols]
        summed = summed + jnp.dot(window.reshape(-1, padded.shape[3]), weight[tap_index], preferred_element_type=jnp.float32)
    return summed.reshape(frames, rows, cols, weight.shape[2])

def tap_grads(padded, cotangent):
    frames, rows, cols, width = cotangent.shape
    flat = cotangent.reshape(-1, width)
    result = []
    for tap_index in range(27):
        shift_time, shift_row, shift_col = shifts_of(tap_index)
        window = padded[shift_time:shift_time + frames, shift_row:shift_row + rows, shift_col:shift_col + cols]
        result.append(lax.dot_general(window.reshape(-1, padded.shape[3]), flat, (((0,), (0,)), ((), ())), preferred_element_type=jnp.float32))
    return jnp.stack(result)

def conv_back(padded, weight):
    frames = padded.shape[0] - 2
    rows = padded.shape[1] - 2
    cols = padded.shape[2] - 2
    summed = jnp.zeros((frames * rows * cols, weight.shape[1]), jnp.float32)
    for tap_index in range(27):
        shift_time, shift_row, shift_col = shifts_of(tap_index)
        window = padded[2 - shift_time:2 - shift_time + frames, 2 - shift_row:2 - shift_row + rows, 2 - shift_col:2 - shift_col + cols]
        summed = summed + lax.dot_general(window.reshape(-1, padded.shape[3]), weight[tap_index], (((1,), (1,)), ((), ())), preferred_element_type=jnp.float32)
    return summed.reshape(frames, rows, cols, weight.shape[1])

def reference(tokens, conv_first, bias_first, conv_second, bias_second, pixels, mask_index):
    gelu_tanh = partial(jax.nn.gelu, approximate=True)

    def per_clip(carry, inputs):
        clip_tokens, clip_pixels, clip_index = inputs
        frames, rows, cols, width = clip_tokens.shape
        tokens_padded = pad_full(clip_tokens)
        zsum = conv_taps(tokens_padded, conv_first) + bias_first
        hidden = gelu_tanh(zsum).astype(jnp.bfloat16)
        upsampled = jnp.repeat(jnp.repeat(hidden, 2, axis=1), 2, axis=2)
        up_padded = pad_full(upsampled)
        predict = conv_taps(up_padded, conv_second) + bias_second
        values = predict.shape[3]
        pix = clip_pixels.astype(jnp.float32)
        center = pix - lax.optimization_barrier(jnp.mean(pix, axis=-1, keepdims=True))
        spread = lax.optimization_barrier(jnp.mean(center * center, axis=-1, keepdims=True))
        normed = center * lax.rsqrt(spread + 1e-06)
        normed = normed.reshape(frames, rows, cols, 2, 2, values).transpose(0, 1, 3, 2, 4, 5).reshape(frames, 2 * rows, 2 * cols, values)
        positions = jnp.arange(rows * cols, dtype=jnp.int32)
        hits = lax.optimization_barrier(jnp.sum((positions[:, None] == clip_index[None, :]).astype(jnp.float32), axis=1)).reshape(rows, cols)
        cell_mask = jnp.repeat(jnp.repeat(hits, 2, axis=0), 2, axis=1)
        cotangent = (2.0 / (4 * values) * cell_mask[None, :, :, None] * (predict - normed)).astype(jnp.bfloat16)
        grad_second = tap_grads(up_padded, cotangent)
        grad_up = conv_back(pad_full(cotangent), conv_second)
        grad_hidden = grad_up.reshape(frames, rows, 2, cols, 2, grad_up.shape[3]).sum(axis=(2, 4))
        grad_z = jax.vjp(gelu_tanh, zsum)[1](grad_hidden)[0].astype(jnp.bfloat16)
        grad_first = tap_grads(tokens_padded, grad_z)
        return ((carry[0] + grad_first, carry[1] + grad_second), None)
    start = (jnp.zeros(conv_first.shape, jnp.float32), jnp.zeros(conv_second.shape, jnp.float32))
    final, unused = lax.scan(per_clip, start, (tokens, pixels, mask_index))
    return (final[0], final[1])
```

```python
import jax
import jax.numpy as jnp
import numpy as np
from jax import lax
from jax.experimental import pallas as pl
from jax.experimental.pallas import tpu as pltpu
from jax.sharding import PartitionSpec as P

F32 = jnp.float32
BF16 = jnp.bfloat16
NT = (((1,), (1,)), ((), ()))
GELU_ROOT = 0.7978845608028654
GELU_CUBE = 0.044715


def floor_half(v):
    return v // 2 if v >= 0 else -1


def make_kernel(dims):
    ndp, nseq, tf, rows, cols, width, mid, values = dims
    n = tf * cols * rows
    plane = cols * rows
    frames = tf * nseq
    hb = rows // nseq
    he = hb + 2
    line = frames * cols
    ext = he * line
    chunk = tf * cols
    dblk = width // nseq
    cblk = mid // ndp
    vblk = values // ndp
    mblk = mid // nseq
    ndev = ndp * nseq
    nz = nseq // 2
    clip_lanes = nseq * n

    def kernel(tok, w1_hbm, b1, w2_hbm, b2, pix_hbm, marks, place_of, tperm, spread_of, gather_of,
               colv, o1, o2,
               w1, w2, w2b, pixv, xbuf, xall, xs, thalo, tfield, im1, slope_of,
               hsend, hraw, vfield, tgt, cell, psend, praw,
               htsend, htall, lhs, csend, call_, stack, qsend, qrecv, rsend, rall, gsend, gall,
               acc1, acc2,
               wsem, th_s, th_r, h_s, h_r, p_s, p_r, xz_s, xz_r, xd_s, xd_r, ht_s, ht_r,
               c_s, c_r, g_s, g_r, q_s, q_r, r_s, r_r):
        dp = lax.axis_index("dp")
        seq = lax.axis_index("seq")
        me = dp * nseq + seq
        chip, core = seq // 2, lax.rem(seq, 2)

        def remote(src, dst, ss, rs, d, s):
            return pltpu.make_async_remote_copy(
                src_ref=src, dst_ref=dst, send_sem=ss, recv_sem=rs,
                device_id=(d, s), device_id_type=pl.DeviceIdType.MESH)

        def drain(ref, sem):
            pltpu.make_async_copy(ref, ref, sem).wait()

        def each(low, count, act):
            def body(o, c):
                act(o)
                return c
            lax.fori_loop(low, count, body, 0)

        cp1 = pltpu.make_async_copy(w1_hbm, w1, wsem.at[0])
        cp2 = pltpu.make_async_copy(w2_hbm, w2, wsem.at[1])
        cpx = pltpu.make_async_copy(pix_hbm, pixv, wsem.at[2])
        cp1.start()
        cpx.start()
        cp2.start()

        barrier = pltpu.get_barrier_semaphore()

        def greet(o):
            t = lax.rem(me + o, ndev)
            pl.semaphore_signal(barrier, inc=1, device_id=(t // nseq, lax.rem(t, nseq)),
                                device_id_type=pl.DeviceIdType.MESH)

        each(1, ndev, greet)

        for k in range(27):
            a, b, c = k // 9, k // 3 % 3, k % 3
            pltpu.make_async_copy(
                w2_hbm.at[pl.ds(k * mid, mid)],
                w2b.at[b, pl.ds(a * mid, mid), pl.ds(c * values, values)], wsem.at[3]).start()

        def ordered(frame):
            raw = frame.astype(F32).reshape(plane, width).astype(BF16)
            return jnp.dot(tperm[...], raw, preferred_element_type=F32)

        flat = jnp.concatenate([ordered(tok[t]) for t in range(tf)], axis=0)
        xt = flat.T
        for s in range(nseq):
            xbuf[s] = xt[s * dblk:(s + 1) * dblk].astype(BF16)
        pl.semaphore_wait(barrier, ndev - 1)

        up = remote(tok.at[tf - 1], thalo.at[0], th_s.at[0], th_r.at[0], dp,
                    jnp.minimum(seq + 1, nseq - 1))
        down = remote(tok.at[0], thalo.at[1], th_s.at[1], th_r.at[1], dp,
                      jnp.maximum(seq - 1, 0))

        @pl.when(seq < nseq - 1)
        def _():
            up.start()

        @pl.when(seq > 0)
        def _():
            down.start()

        @pl.when(seq == 0)
        def _():
            thalo[0] = jnp.zeros((rows, cols, width), BF16)

        @pl.when(seq == nseq - 1)
        def _():
            thalo[1] = jnp.zeros((rows, cols, width), BF16)

        h_low, h_high = colv[:, 0:1], colv[:, 1:2]

        def row_shift(v, d):
            m = v.shape[0]
            if d == 0:
                return v
            rolled = pltpu.roll(v, 1 if d < 0 else m - 1, axis=0)
            return rolled * (h_low if d < 0 else h_high)[:m]

        def place(field, frame, v, count):
            for d in (-1, 0, 1):
                field[d + 1, frame:frame + count, 1:cols + 1] = (
                    row_shift(v, d).astype(BF16).reshape(count, cols, rows, v.shape[1]))

        zero = jnp.zeros((3, tf + 2, 1, rows, width), BF16)
        tfield[:, :, 0:1] = zero
        tfield[:, :, cols + 1:cols + 2] = zero
        place(tfield, 1, flat, tf)

        def taps_first(a):
            for bc in range(9):
                k = a * 9 + bc
                im1[:, k * width:(k + 1) * width] = (
                    tfield[bc // 3, a:a + tf, bc % 3:bc % 3 + cols].reshape(n, width))
            span = slice(a * 9 * width, (a + 1) * 9 * width)
            return jnp.dot(im1[:, span], w1[span], preferred_element_type=F32)

        cp1.wait()
        z = taps_first(1) + b1[...]

        cpx.wait()
        raw = [pixv[:, h].astype(F32).reshape(line, 4 * values) for h in range(hb)]
        px = jnp.concatenate(raw, axis=0)
        center = px - jnp.mean(px, axis=-1, keepdims=True)
        spread = jnp.mean(center * center, axis=-1, keepdims=True)
        normed = center * lax.rsqrt(spread + 1e-06)
        for ij in range(4):
            tgt[ij] = normed[:, ij * values:(ij + 1) * values] - b2[...].reshape(1, values)
        matches = (place_of[...] + seq * (hb * cols) == marks[...]).astype(F32)
        scale = 2.0 / (4 * values) * jnp.sum(matches, axis=1, keepdims=True)

        @pl.when(seq > 0)
        def _():
            up.wait_recv()

        @pl.when(seq < nseq - 1)
        def _():
            down.wait_recv()

        place(tfield, 0, ordered(thalo[0]), 1)
        place(tfield, tf + 1, ordered(thalo[1]), 1)
        z = z + taps_first(0) + taps_first(2)
        th_ = jnp.tanh(GELU_ROOT * (z + GELU_CUBE * z * z * z))
        hid = (0.5 * z * (1.0 + th_)).astype(BF16)
        hsend[...] = jnp.dot(spread_of[...], hid, preferred_element_type=F32).reshape(
            nseq, he, chunk, mid).astype(BF16)

        def h_copy(o):
            s = lax.rem(seq + o, nseq)
            return remote(hsend.at[s], hraw.at[seq], h_s.at[0], h_r.at[0], dp, s)

        each(1, nseq, lambda o: h_copy(o).start())
        hraw[seq] = hsend[seq]
        slope_of[...] = 0.5 * (1.0 + th_) + 0.5 * z * (1.0 - th_ * th_) * GELU_ROOT * (
            1.0 + 3.0 * GELU_CUBE * z * z)

        def band(size):
            li = lax.broadcasted_iota(jnp.int32, (line, size), 0)
            lw = lax.rem(li, cols)
            return ((lw > 0).astype(F32), (lw < cols - 1).astype(F32),
                    (li >= cols).astype(F32), (li < line - cols).astype(F32))

        w_low, w_high, t_low, t_high = band(mid)
        p_low, p_high, _, _ = band(values)
        le = lax.broadcasted_iota(jnp.int32, (1, ext), 1)
        lw = lax.rem(le, cols)
        lt = lax.rem(le, line)
        e_low, e_high = (lw > 0).astype(F32), (lw < cols - 1).astype(F32)
        s_low, s_high = (lt >= cols).astype(F32), (lt < line - cols).astype(F32)

        def shifted(v, by, mask):
            m = v.shape[0]
            rolled = pltpu.roll(v, (-by) % m, axis=0)
            return (rolled.reshape(m // line, line, v.shape[1]) * mask[None]).reshape(v.shape)

        drain(hraw.at[pl.ds(0, nseq - 1)], h_r.at[0])

        def xz_copy(o):
            s = lax.rem(seq + o, nseq)
            return remote(xbuf.at[s], xall.at[dp, seq], xz_s.at[0], xz_r.at[0], dp, s)

        each(1, nseq, lambda o: xz_copy(o).start())
        xall[dp, seq] = xbuf[seq]

        hin = hraw[...].astype(F32)
        hext = jnp.concatenate(
            [hin[:, hh].reshape(line, mid) for hh in range(he)], axis=0)
        for a in range(3):
            late = hext if a == 1 else shifted(
                hext, cols * (a - 1), t_low if a == 0 else t_high)
            for e in range(3):
                v = late if e == 1 else shifted(late, e - 1, w_low if e == 0 else w_high)
                vfield[a * 3 + e] = v.astype(BF16)
        htsend[...] = hext.T.astype(BF16)

        def ht_copy(o):
            d = lax.rem(dp + o, ndp)
            return remote(htsend, htall.at[dp], ht_s.at[0], ht_r.at[0], d, seq)

        each(1, ndp, lambda o: ht_copy(o).start())
        htall[dp] = htsend[...]

        def taps_second(a):
            parts = []
            for ij in range(4):
                i, j = ij // 2, ij % 2
                cells = []
                for bc in range(9):
                    dh, dw = floor_half(i + bc // 3 - 1), floor_half(j + bc % 3 - 1)
                    low = (1 + dh) * line
                    cells.append(vfield[a * 3 + dw + 1, low:low + hb * line])
                parts.append(jnp.concatenate(cells, axis=1))
            return jnp.dot(jnp.concatenate(parts, axis=0), w2[a * 9 * mid:(a + 1) * 9 * mid],
                           preferred_element_type=F32)

        cp2.wait()
        predict = taps_second(0) + taps_second(1) + taps_second(2)
        cots = []
        for ij in range(4):
            cot = (scale * (predict[ij * n:(ij + 1) * n] - tgt[ij])).astype(BF16).astype(F32)
            cots.append(cot)
            turned = cot.T
            for d in range(ndp):
                csend[d, ij] = turned[d * vblk:(d + 1) * vblk].astype(BF16)

        def c_copy(o):
            d = lax.rem(dp + o, ndp)
            return remote(csend.at[d], call_.at[dp], c_s.at[0], c_r.at[dp], d, seq)

        each(1, ndp, lambda o: c_copy(o).start())
        call_[dp] = csend[dp]

        def pair_sums(low, high, after, before):
            return (high + after(low), low + high, before(high) + low)

        def after_row(v):
            return shifted(v, 1, p_high)

        def before_row(v):
            return shifted(v, -1, p_low)

        for u, (low, high) in enumerate((
                (cots[0], cots[1]), (cots[2], cots[3]),
                (cots[0] + cots[2], cots[1] + cots[3]))):
            for c, s in enumerate(pair_sums(low, high, after_row, before_row)):
                cell[u * n:(u + 1) * n, c * values:(c + 1) * values] = s.astype(BF16)

        drain(w2b, wsem.at[3])
        both = cell[0:2 * n]
        first = lax.dot_general(both, w2b[0], NT, preferred_element_type=F32)
        third = lax.dot_general(both, w2b[2], NT, preferred_element_type=F32)
        second = lax.dot_general(cell[2 * n:3 * n], w2b[1], NT, preferred_element_type=F32)
        same = first[n:] + second + third[:n]
        pieces = []
        for hh in range(he):
            total = None
            for v, dh in ((first[:n], -1), (same, 0), (third[n:], 1)):
                h = hh - 1 - dh
                if 0 <= h < hb:
                    part = v[h * line:(h + 1) * line]
                    total = part if total is None else total + part
            back = total[:, mid:2 * mid]
            back = back + shifted(total[:, :mid], cols, t_high)
            back = back + shifted(total[:, 2 * mid:], -cols, t_low)
            pieces.append(back)
        for hh in range(he):
            psend[:, hh] = pieces[hh].reshape(nseq, chunk, mid).astype(BF16)

        def p_copy(o):
            s = lax.rem(seq + o, nseq)
            return remote(psend.at[s], praw.at[seq], p_s.at[0], p_r.at[0], dp, s)

        each(1, nseq, lambda o: p_copy(o).start())
        praw[seq] = psend[seq]

        drain(xall.at[0, pl.ds(0, nseq - 1)], xz_r.at[0])

        def xd_copy(o):
            d = lax.rem(dp + o, ndp)
            return remote(xall.at[dp], xall.at[dp], xd_s.at[0], xd_r.at[0], d, seq)

        each(1, ndp, lambda o: xd_copy(o).start())

        drain(htall.at[pl.ds(0, ndp - 1)], ht_r.at[0])
        for q in range(ndp):
            turned = htall[q].astype(F32)
            for a in range(3):
                v = turned
                if a != 1:
                    v = pltpu.roll(turned, (cols if a == 0 else ext - cols), axis=1)
                    v = v * (s_low if a == 0 else s_high)
                lhs[:, a, :, q * ext:(q + 1) * ext] = v.reshape(nseq, mblk, ext).astype(BF16)

        def lane_after(v):
            return pltpu.roll(v, ext - 1, axis=1) * e_high

        def lane_before(v):
            return pltpu.roll(v, 1, axis=1) * e_low

        pad = jnp.zeros((vblk, ext - hb * line), F32)

        def clip_stack(q):
            by_col = []
            for j in range(2):
                low, high = [jnp.concatenate([call_[q, i * 2 + j].astype(F32), pad], axis=1)
                             for i in range(2)]
                low_in, high_in = pltpu.roll(low, line, axis=1), pltpu.roll(high, line, axis=1)
                high_out = pltpu.roll(high, 2 * line, axis=1)
                by_col.append((low + high_in, low_in + high_in, low_in + high_out))
            at = pl.ds(pl.multiple_of(q * ext, 128), ext)
            k = 0
            for b in range(3):
                for s in pair_sums(by_col[0][b], by_col[1][b], lane_after, lane_before):
                    stack[k * vblk:(k + 1) * vblk, at] = s.astype(BF16)
                    k += 1

        clip_stack(dp)

        drain(praw.at[pl.ds(0, nseq - 1)], p_r.at[0])
        got = praw[...].astype(F32).reshape(nseq * he * chunk, mid).astype(BF16)
        grad_h = jnp.dot(gather_of[...], got, preferred_element_type=F32)
        grad_z = (grad_h * slope_of[...]).astype(BF16).astype(F32).T
        for d in range(ndp):
            gsend[d] = grad_z[d * cblk:(d + 1) * cblk].astype(BF16)

        def g_copy(o):
            t = lax.rem(me + o, ndev)
            d = t // nseq
            return remote(gsend.at[d], gall.at[dp, seq], g_s.at[0], g_r.at[dp], d,
                          lax.rem(t, nseq))

        each(1, ndev, lambda o: g_copy(o).start())
        gall[dp, seq] = gsend[dp]

        def other_clip(o):
            q = lax.rem(dp + o, ndp)
            drain(call_.at[q], c_r.at[q])
            clip_stack(q)

        each(1, ndp, other_clip)

        def half(k):
            block = jnp.concatenate(
                [lhs[2 * s + k].reshape(3 * mblk, ndp * ext) for s in range(nz)], axis=0)
            return lax.dot_general(block, stack[...], NT, preferred_element_type=F32)

        sent = half(1 - core)
        for s in range(nz):
            qsend[s] = sent[s * 3 * mblk:(s + 1) * 3 * mblk].astype(BF16)
        swap = remote(qsend, qrecv, q_s.at[0], q_r.at[0], dp, 2 * chip + 1 - core)
        swap.start()
        acc2[...] = half(core)

        drain(xall.at[pl.ds(0, ndp - 1)], xd_r.at[0])
        lx = lax.broadcasted_iota(jnp.int32, (1, clip_lanes), 1)
        x_low, x_high = (lx >= plane).astype(F32), (lx < clip_lanes - plane).astype(F32)

        def turn_clip(q):
            x = jnp.concatenate([xall[q, s] for s in range(nseq)], axis=1)
            xf = x.astype(F32)
            xs[q, 0:dblk] = (pltpu.roll(xf, plane, axis=1) * x_low).astype(BF16)
            xs[q, dblk:2 * dblk] = x
            xs[q, 2 * dblk:3 * dblk] = (
                pltpu.roll(xf, clip_lanes - plane, axis=1) * x_high).astype(BF16)

        swap.wait_recv()
        for s in range(nz):
            rsend[s] = (acc2[s * 3 * mblk:(s + 1) * 3 * mblk] + qrecv[s].astype(F32)).astype(BF16)

        def r_copy(o):
            s = lax.rem(chip + o, nz)
            return remote(rsend.at[s], rall.at[chip], r_s.at[0], r_r.at[0], dp, s * 2 + core)

        each(1, nz, lambda o: r_copy(o).start())
        rall[chip] = rsend[chip]
        each(0, ndp, turn_clip)

        lh = lax.rem(lx, rows)
        lc = lax.rem(lx, plane)
        g_h = ((lh < rows - 1).astype(F32), None, (lh > 0).astype(F32))
        g_w = ((lc < plane - rows).astype(F32), None, (lc >= rows).astype(F32))
        acc1[...] = jnp.zeros_like(acc1)

        def one_first(q):
            g = jnp.concatenate([gall[q, s].astype(F32) for s in range(nseq)], axis=1)
            grid = []
            for b in range(3):
                v = g if b == 1 else pltpu.roll(g, (b - 1) % clip_lanes, axis=1) * g_h[b]
                for c in range(3):
                    u = v if c == 1 else pltpu.roll(
                        v, ((c - 1) * rows) % clip_lanes, axis=1) * g_w[c]
                    grid.append(u.astype(BF16))
            acc1[...] += lax.dot_general(jnp.concatenate(grid, axis=0), xs[q], NT,
                                         preferred_element_type=F32)

        drain(gall.at[0, pl.ds(0, nseq - 1)], g_r.at[dp])
        one_first(dp)

        def other_first(o):
            q = lax.rem(dp + o, ndp)
            drain(gall.at[q], g_r.at[q])
            one_first(q)

        each(1, ndp, other_first)
        for a in range(3):
            o1[a * 9 * cblk:(a + 1) * 9 * cblk] = acc1[:, a * dblk:(a + 1) * dblk]

        @pl.when(seq < nseq - 1)
        def _():
            up.wait_send()

        @pl.when(seq > 0)
        def _():
            down.wait_send()

        drain(hsend.at[pl.ds(0, nseq - 1)], h_s.at[0])
        drain(xbuf.at[pl.ds(0, nseq - 1)], xz_s.at[0])
        drain(htall.at[pl.ds(0, ndp - 1)], ht_s.at[0])
        drain(csend.at[pl.ds(0, ndp - 1)], c_s.at[0])
        drain(psend.at[pl.ds(0, nseq - 1)], p_s.at[0])
        drain(xall.at[pl.ds(0, ndp - 1)], xd_s.at[0])
        swap.wait_send()
        for o in range(ndp):
            drain(gall.at[0, pl.ds(0, nseq - 1)] if o == 0 else gall.at[0], g_s.at[0])
        drain(rall.at[pl.ds(0, nz - 1)], r_r.at[0])
        total = rall[0].astype(F32)
        for s in range(1, nz):
            total = total + rall[s].astype(F32)
        for a in range(3):
            for bc in range(9):
                o2[a * 9 + bc] = total[a * mblk:(a + 1) * mblk, bc * vblk:(bc + 1) * vblk]
        drain(rsend.at[pl.ds(0, nz - 1)], r_s.at[0])

    return kernel


def flush(a, b, oa, ob, sem):
    moves = (pltpu.make_async_copy(a, oa, sem.at[0]), pltpu.make_async_copy(b, ob, sem.at[1]))
    for m in moves:
        m.start()
    for m in moves:
        m.wait()


def per_device(tokens, conv_first, bias_first, conv_second, bias_second, pixels, mask_index):
    ndp, nseq = lax.axis_size("dp"), lax.axis_size("seq")
    tf, rows, cols, width = tokens.shape[1:]
    frames = tf * nseq
    mid, values = conv_second.shape[1], conv_second.shape[2]
    n = tf * rows * cols
    hb = rows // nseq
    he = hb + 2
    line = frames * cols
    ext = he * line
    chunk = tf * cols
    dims = (ndp, nseq, tf, rows, cols, width, mid, values)
    plane = rows * cols
    dblk, cblk, vblk, mblk = width // nseq, mid // ndp, values // ndp, mid // nseq
    nz = nseq // 2

    idx = np.arange(n, dtype=np.int32)
    t_of, w_of, h_of = idx // plane, idx // rows % cols, idx % rows
    flat_place = (h_of * cols + w_of)[:plane]
    tperm = jnp.asarray(flat_place[:, None] == idx[None, :plane], BF16)
    msg = np.arange(nseq * he * chunk, dtype=np.int32)
    m_s, m_h = msg // (he * chunk), msg // chunk % he
    m_t, m_w = msg % chunk // cols, msg % cols
    m_row = m_s * hb + m_h - 1
    same = ((m_row[:, None] == h_of[None]) & (m_t[:, None] == t_of[None])
            & (m_w[:, None] == w_of[None]))
    spread_of = jnp.asarray(same, BF16)
    gather_of = jnp.asarray(same.T, BF16)
    own = np.arange(hb * line, dtype=np.int32)
    place_of = jnp.asarray((own // line * cols + own % cols)[:, None])
    colv = jnp.asarray(np.stack([h_of > 0, h_of < rows - 1], axis=1), F32)

    vm = pl.BlockSpec(memory_space=pltpu.VMEM)
    hbm = pl.BlockSpec(memory_space=pl.ANY)

    def dma(k):
        return pltpu.SemaphoreType.DMA((k,))

    scratch = [
        pltpu.VMEM((27 * width, mid), BF16),
        pltpu.VMEM((27 * mid, values), BF16),
        pltpu.VMEM((3, 3 * mid, 3 * values), BF16),
        pltpu.VMEM((frames, hb, cols, 4 * values), BF16),
        pltpu.VMEM((nseq, dblk, n), BF16),
        pltpu.VMEM((ndp, nseq, dblk, n), BF16),
        pltpu.VMEM((ndp, 3 * dblk, nseq * n), BF16),
        pltpu.VMEM((2, rows, cols, width), BF16),
        pltpu.VMEM((3, tf + 2, cols + 2, rows, width), BF16),
        pltpu.VMEM((n, 27 * width), BF16),
        pltpu.VMEM((n, mid), F32),
        pltpu.VMEM((nseq, he, chunk, mid), BF16),
        pltpu.VMEM((nseq, he, chunk, mid), BF16),
        pltpu.VMEM((9, ext, mid), BF16),
        pltpu.VMEM((4, n, values), F32),
        pltpu.VMEM((3 * n, 3 * values), BF16),
        pltpu.VMEM((nseq, he, chunk, mid), BF16),
        pltpu.VMEM((nseq, he, chunk, mid), BF16),
        pltpu.VMEM((mid, ext), BF16),
        pltpu.VMEM((ndp, mid, ext), BF16),
        pltpu.VMEM((nseq, 3, mblk, ndp * ext), BF16),
        pltpu.VMEM((ndp, 4, vblk, n), BF16),
        pltpu.VMEM((ndp, 4, vblk, n), BF16),
        pltpu.VMEM((9 * vblk, ndp * ext), BF16),
        pltpu.VMEM((nz, 3 * mblk, 9 * vblk), BF16),
        pltpu.VMEM((nz, 3 * mblk, 9 * vblk), BF16),
        pltpu.VMEM((nz, 3 * mblk, 9 * vblk), BF16),
        pltpu.VMEM((nz, 3 * mblk, 9 * vblk), BF16),
        pltpu.VMEM((ndp, cblk, n), BF16),
        pltpu.VMEM((ndp, nseq, cblk, n), BF16),
        pltpu.VMEM((9 * cblk, 3 * dblk), F32),
        pltpu.VMEM((nz * 3 * mblk, 9 * vblk), F32),
        dma(4), dma(2), dma(2), dma(1), dma(1), dma(1), dma(1), dma(1), dma(1), dma(1), dma(1),
        dma(1), dma(1), dma(1), dma(ndp), dma(1), dma(ndp), dma(1), dma(1), dma(1), dma(1),
    ]
    first, second = pl.pallas_call(
        make_kernel(dims),
        out_shape=(pltpu.VMEM((27 * cblk, dblk), F32), pltpu.VMEM((27, mblk, vblk), F32)),
        in_specs=[vm, hbm, vm, hbm, vm, hbm, vm, vm, vm, vm, vm, vm],
        out_specs=(vm, vm),
        scratch_shapes=scratch,
        compiler_params=pltpu.CompilerParams(
            collective_id=0, has_side_effects=True, vmem_limit_bytes=60 * 1024 * 1024),
        name="step",
    )(tokens[0], conv_first.reshape(27 * width, mid), bias_first.reshape(1, mid),
      conv_second.reshape(27 * mid, values), bias_second,
      pixels[0], mask_index, place_of, tperm, spread_of, gather_of, colv)
    first, second = pl.pallas_call(
        flush,
        out_shape=(jax.ShapeDtypeStruct(first.shape, F32), jax.ShapeDtypeStruct(second.shape, F32)),
        in_specs=[vm, vm],
        out_specs=(hbm, hbm),
        scratch_shapes=[dma(2)],
        compiler_params=pltpu.CompilerParams(vmem_limit_bytes=4 * 1024 * 1024),
        name="flush",
    )(pltpu.with_memory_space_constraint(first, pltpu.VMEM),
      pltpu.with_memory_space_constraint(second, pltpu.VMEM))
    first = first.reshape(27, cblk, dblk).transpose(0, 2, 1)
    return (first, second)


def solution(mesh):
    return jax.shard_map(
        per_device,
        mesh=mesh,
        in_specs=(
            P("dp", "seq", None, None, None),
            P(),
            P(),
            P(),
            P(),
            P("dp", None, "seq", None, None),
            P("dp", None),
        ),
        out_specs=(P(None, "seq", "dp"), P(None, "seq", "dp")),
        check_vma=False,
    )
```

```python
import jax
import jax.numpy as jnp
import numpy as np
from jax import lax
from jax.experimental import pallas as pl
from jax.experimental.pallas import tpu as pltpu
from jax.sharding import PartitionSpec as P

F32 = jnp.float32
BF16 = jnp.bfloat16
NT = (((1,), (1,)), ((), ()))
GELU_ROOT = 0.7978845608028654
GELU_CUBE = 0.044715


def floor_half(v):
    return v // 2 if v >= 0 else -1


def make_kernel(dims):
    ndp, nseq, tf, rows, cols, width, mid, values = dims
    n = tf * cols * rows
    plane = cols * rows
    frames = tf * nseq
    hb = rows // nseq
    he = hb + 2
    line = frames * cols
    ext = he * line
    chunk = tf * cols
    dblk = width // nseq
    cblk = mid // ndp
    vblk = values // ndp
    mblk = mid // nseq
    ndev = ndp * nseq
    nz = nseq // 2
    clip_lanes = nseq * n

    def kernel(tok_hbm, w1_hbm, b1_hbm, w2_hbm, b2_hbm, pix_hbm, marks_hbm, tperm_hbm, spread_hbm,
               gather_hbm, o1, o2,
               tok, b1, b2, marks, tperm, spread_of, gather_of,
               w1, w2, w2b, weff, pixv, xbuf, xall, xs, tsend, thalo, tfield, im1, slope_of,
               hsend, hraw, vfield, tgt, cell, psend, praw,
               htsend, htall, lhs, csend, call_, stack, qsend, qrecv, rsend, rall, gsend, gall,
               acc1, acc2,
               wsem, th_s, th_r, h_s, h_r, p_s, p_r, xz_s, xz_r, xd_s, xd_r, ht_s, ht_r,
               c_s, c_r, g_s, g_r, f_s, f_r, q_s, q_r, r_s, r_r):
        dp = lax.axis_index("dp")
        seq = lax.axis_index("seq")
        me = dp * nseq + seq
        chip, core = seq // 2, lax.rem(seq, 2)

        def remote(src, dst, ss, rs, d, s):
            return pltpu.make_async_remote_copy(
                src_ref=src, dst_ref=dst, send_sem=ss, recv_sem=rs,
                device_id=(d, s), device_id_type=pl.DeviceIdType.MESH)

        def drain(ref, sem):
            pltpu.make_async_copy(ref, ref, sem).wait()

        def each(low, count, act):
            def body(o, c):
                act(o)
                return c
            lax.fori_loop(low, count, body, 0)

        barrier = pltpu.get_barrier_semaphore()

        def greet(o):
            t = lax.rem(me + o, ndev)
            pl.semaphore_signal(barrier, inc=1, device_id=(t // nseq, lax.rem(t, nseq)),
                                device_id_type=pl.DeviceIdType.MESH)

        loads = [pltpu.make_async_copy(src, dst, wsem.at[k]) for k, (src, dst) in enumerate((
            (tok_hbm, tok), (tperm_hbm, tperm), (b1_hbm, b1), (b2_hbm, b2), (marks_hbm, marks),
            (spread_hbm, spread_of), (gather_hbm, gather_of), (pix_hbm, pixv), (w2_hbm, w2)))]
        loads[0].start()
        loads[1].start()
        for a in range(3):
            pltpu.make_async_copy(w1_hbm.at[pl.ds(a * 9 * width, 9 * width)],
                                  w1.at[:, pl.ds(a * mid, mid)], wsem.at[9]).start()
        for m in loads[2:]:
            m.start()
        each(1, ndev, greet)
        for k in range(27):
            a, b, c = k // 9, k // 3 % 3, k % 3
            pltpu.make_async_copy(
                w2_hbm.at[pl.ds(k * mid, mid)],
                w2b.at[b, pl.ds(a * mid, mid), pl.ds(c * values, values)], wsem.at[10]).start()

        def ordered(frame):
            raw = frame.astype(F32).reshape(plane, width).astype(BF16)
            return jnp.dot(tperm[...], raw, preferred_element_type=F32)

        loads[0].wait()
        loads[1].wait()
        flat = jnp.concatenate([ordered(tok[t]) for t in range(tf)], axis=0)
        xt = flat.T
        for s in range(nseq):
            xbuf[s] = xt[s * dblk:(s + 1) * dblk].astype(BF16)

        lr = lax.broadcasted_iota(jnp.int32, (rows, width), 0)
        edge = ((lr > 0).astype(F32), None, (lr < rows - 1).astype(F32))
        zero = jnp.zeros((3, tf, 1, rows, width), BF16)
        tfield[:, :, 0:1] = zero
        tfield[:, :, cols + 1:cols + 2] = zero
        for b in range(3):
            v = flat.reshape(tf, cols, rows, width)
            if b != 1:
                v = pltpu.roll(flat, 1 if b == 0 else n - 1, axis=0).reshape(
                    tf * cols, rows, width) * edge[b][None]
            tfield[b, :, 1:cols + 1] = v.reshape(tf, cols, rows, width).astype(BF16)
        for bc in range(9):
            im1[:, bc * width:(bc + 1) * width] = (
                tfield[bc // 3, :, bc % 3:bc % 3 + cols].reshape(n, width))
        drain(w1, wsem.at[9])
        parts = jnp.dot(im1[...], w1[...], preferred_element_type=F32)
        to_next, here, to_prev = [parts[:, a * mid:(a + 1) * mid] for a in range(3)]
        tsend[0] = to_next[n - plane:]
        tsend[1] = to_prev[:plane]
        pl.semaphore_wait(barrier, ndev - 1)

        up = remote(tsend.at[0], thalo.at[0], th_s.at[0], th_r.at[0], dp,
                    jnp.minimum(seq + 1, nseq - 1))
        down = remote(tsend.at[1], thalo.at[1], th_s.at[1], th_r.at[1], dp,
                      jnp.maximum(seq - 1, 0))

        @pl.when(seq < nseq - 1)
        def _():
            up.start()

        @pl.when(seq > 0)
        def _():
            down.start()

        @pl.when(seq == 0)
        def _():
            thalo[0] = jnp.zeros((plane, mid), F32)

        @pl.when(seq == nseq - 1)
        def _():
            thalo[1] = jnp.zeros((plane, mid), F32)

        for m in loads[2:]:
            m.wait()
        raw = [pixv[:, h].astype(F32).reshape(line, 4 * values) for h in range(hb)]
        px = jnp.concatenate(raw, axis=0)
        center = px - jnp.mean(px, axis=-1, keepdims=True)
        spread = jnp.mean(center * center, axis=-1, keepdims=True)
        normed = center * lax.rsqrt(spread + 1e-06)
        for ij in range(4):
            tgt[ij] = normed[:, ij * values:(ij + 1) * values] - b2[...].reshape(1, values)
        le = lax.broadcasted_iota(jnp.int32, (n, 1), 0)
        spot = lax.div(le, line) * cols + lax.rem(le, cols) + seq * (hb * cols)
        matches = (spot == marks[...]).astype(F32)
        scale = 2.0 / (4 * values) * jnp.sum(matches, axis=1, keepdims=True)

        step = 16 if mid % 16 == 0 else mid

        def sum_taps(o):
            a, r = lax.div(o, mid // step), lax.rem(o, mid // step)
            w = [w2[pl.ds(pl.multiple_of((a * 9 + bc) * mid + r * step, step), step)].astype(F32)
                 for bc in range(9)]
            wide = []
            for b in range(3):
                x, y, z_ = w[b * 3:b * 3 + 3]
                wide.append((x, y + z_, x + y, z_))
            for i in range(2):
                for e in range(4):
                    x, y, z_ = wide[0][e], wide[1][e], wide[2][e]
                    for rh, v in enumerate((x, y + z_) if i == 0 else (x + y, z_)):
                        at = (a * 4 + rh * 2 + e % 2) * mid + r * step
                        weff[i * 2 + e // 2, pl.ds(pl.multiple_of(at, step), step)] = v.astype(BF16)

        each(0, 3 * (mid // step), sum_taps)

        @pl.when(seq > 0)
        def _():
            up.wait_recv()

        @pl.when(seq < nseq - 1)
        def _():
            down.wait_recv()

        if tf > 1:
            late = jnp.concatenate([thalo[0], to_next[:n - plane]], axis=0)
            early = jnp.concatenate([to_prev[plane:], thalo[1]], axis=0)
        else:
            late, early = thalo[0], thalo[1]
        z = here + late + early + b1[...]
        th_ = jnp.tanh(GELU_ROOT * (z + GELU_CUBE * z * z * z))
        hid = (0.5 * z * (1.0 + th_)).astype(BF16)
        hsend[...] = jnp.dot(spread_of[...], hid, preferred_element_type=F32).reshape(
            nseq, he, chunk, mid).astype(BF16)

        def h_copy(o):
            s = lax.rem(seq + o, nseq)
            return remote(hsend.at[s], hraw.at[seq], h_s.at[0], h_r.at[0], dp, s)

        each(1, nseq, lambda o: h_copy(o).start())
        hraw[seq] = hsend[seq]
        slope_of[...] = 0.5 * (1.0 + th_) + 0.5 * z * (1.0 - th_ * th_) * GELU_ROOT * (
            1.0 + 3.0 * GELU_CUBE * z * z)

        def band(size):
            li = lax.broadcasted_iota(jnp.int32, (line, size), 0)
            lw = lax.rem(li, cols)
            return ((lw > 0).astype(F32), (lw < cols - 1).astype(F32),
                    (li >= cols).astype(F32), (li < line - cols).astype(F32))

        w_low, w_high, t_low, t_high = band(mid)
        p_low, p_high, _, _ = band(values)
        le = lax.broadcasted_iota(jnp.int32, (1, ext), 1)
        lw = lax.rem(le, cols)
        lt = lax.rem(le, line)
        e_low, e_high = (lw > 0).astype(F32), (lw < cols - 1).astype(F32)
        s_low, s_high = (lt >= cols).astype(F32), (lt < line - cols).astype(F32)

        def shifted(v, by, mask):
            m = v.shape[0]
            rolled = pltpu.roll(v, (-by) % m, axis=0)
            return (rolled.reshape(m // line, line, v.shape[1]) * mask[None]).reshape(v.shape)

        drain(hraw.at[pl.ds(0, nseq - 1)], h_r.at[0])

        def xz_copy(o):
            s = lax.rem(seq + o, nseq)
            return remote(xbuf.at[s], xall.at[dp, seq], xz_s.at[0], xz_r.at[0], dp, s)

        each(1, nseq, lambda o: xz_copy(o).start())
        xall[dp, seq] = xbuf[seq]

        hin = hraw[...].astype(F32)
        hext = jnp.concatenate(
            [hin[:, hh].reshape(line, mid) for hh in range(he)], axis=0)
        for a in range(3):
            late = hext if a == 1 else shifted(
                hext, cols * (a - 1), t_low if a == 0 else t_high)
            for e in range(3):
                v = late if e == 1 else shifted(late, e - 1, w_low if e == 0 else w_high)
                vfield[a * 3 + e] = v.astype(BF16)
        htsend[...] = hext.T.astype(BF16)

        def ht_copy(o):
            d = lax.rem(dp + o, ndp)
            return remote(htsend, htall.at[dp], ht_s.at[0], ht_r.at[0], d, seq)

        each(1, ndp, lambda o: ht_copy(o).start())
        htall[dp] = htsend[...]

        cots = []
        for ij in range(4):
            i, j = ij // 2, ij % 2
            near = []
            for k in range(12):
                low = (i + k // 2 % 2) * line
                near.append(vfield[k // 4 * 3 + j + k % 2, low:low + hb * line])
            predict = jnp.dot(jnp.concatenate(near, axis=1), weff[ij], preferred_element_type=F32)
            cot = (scale * (predict - tgt[ij])).astype(BF16).astype(F32)
            cots.append(cot)
            turned = cot.T
            for d in range(ndp):
                csend[d, ij] = turned[d * vblk:(d + 1) * vblk].astype(BF16)

        def c_copy(o):
            d = lax.rem(dp + o, ndp)
            return remote(csend.at[d], call_.at[dp], c_s.at[0], c_r.at[dp], d, seq)

        each(1, ndp, lambda o: c_copy(o).start())
        call_[dp] = csend[dp]

        def pair_sums(low, high, after, before):
            return (high + after(low), low + high, before(high) + low)

        def after_row(v):
            return shifted(v, 1, p_high)

        def before_row(v):
            return shifted(v, -1, p_low)

        for u, (low, high) in enumerate((
                (cots[0], cots[1]), (cots[2], cots[3]),
                (cots[0] + cots[2], cots[1] + cots[3]))):
            for c, s in enumerate(pair_sums(low, high, after_row, before_row)):
                cell[u * n:(u + 1) * n, c * values:(c + 1) * values] = s.astype(BF16)

        drain(w2b, wsem.at[10])
        both = cell[0:2 * n]
        first = lax.dot_general(both, w2b[0], NT, preferred_element_type=F32)
        third = lax.dot_general(both, w2b[2], NT, preferred_element_type=F32)
        second = lax.dot_general(cell[2 * n:3 * n], w2b[1], NT, preferred_element_type=F32)
        same = first[n:] + second + third[:n]
        pieces = []
        for hh in range(he):
            total = None
            for v, dh in ((first[:n], -1), (same, 0), (third[n:], 1)):
                h = hh - 1 - dh
                if 0 <= h < hb:
                    part = v[h * line:(h + 1) * line]
                    total = part if total is None else total + part
            back = total[:, mid:2 * mid]
            back = back + shifted(total[:, :mid], cols, t_high)
            back = back + shifted(total[:, 2 * mid:], -cols, t_low)
            pieces.append(back)
        for hh in range(he):
            psend[:, hh] = pieces[hh].reshape(nseq, chunk, mid)

        def p_copy(o):
            s = lax.rem(seq + o, nseq)
            return remote(psend.at[s], praw.at[seq], p_s.at[0], p_r.at[0], dp, s)

        each(1, nseq, lambda o: p_copy(o).start())
        praw[seq] = psend[seq]

        drain(xall.at[0, pl.ds(0, nseq - 1)], xz_r.at[0])

        def xd_copy(o):
            d = lax.rem(dp + o, ndp)
            return remote(xall.at[dp], xall.at[dp], xd_s.at[0], xd_r.at[0], d, seq)

        each(1, ndp, lambda o: xd_copy(o).start())

        drain(htall.at[pl.ds(0, ndp - 1)], ht_r.at[0])
        for q in range(ndp):
            turned = htall[q].astype(F32)
            for a in range(3):
                v = turned
                if a != 1:
                    v = pltpu.roll(turned, (cols if a == 0 else ext - cols), axis=1)
                    v = v * (s_low if a == 0 else s_high)
                lhs[:, a, :, q * ext:(q + 1) * ext] = v.reshape(nseq, mblk, ext).astype(BF16)

        def lane_after(v):
            return pltpu.roll(v, ext - 1, axis=1) * e_high

        def lane_before(v):
            return pltpu.roll(v, 1, axis=1) * e_low

        pad = jnp.zeros((vblk, ext - hb * line), F32)

        def clip_stack(q):
            by_col = []
            for j in range(2):
                low, high = [jnp.concatenate([call_[q, i * 2 + j].astype(F32), pad], axis=1)
                             for i in range(2)]
                low_in, high_in = pltpu.roll(low, line, axis=1), pltpu.roll(high, line, axis=1)
                high_out = pltpu.roll(high, 2 * line, axis=1)
                by_col.append((low + high_in, low_in + high_in, low_in + high_out))
            at = pl.ds(pl.multiple_of(q * ext, 128), ext)
            k = 0
            for b in range(3):
                for s in pair_sums(by_col[0][b], by_col[1][b], lane_after, lane_before):
                    stack[k * vblk:(k + 1) * vblk, at] = s.astype(BF16)
                    k += 1

        clip_stack(dp)

        drain(praw.at[pl.ds(0, nseq - 1)], p_r.at[0])
        got = praw[...].reshape(nseq * he * chunk, mid)
        major = got.astype(BF16)
        minor = (got - major.astype(F32)).astype(BF16)
        grad_h = (jnp.dot(gather_of[...], major, preferred_element_type=F32)
                  + jnp.dot(gather_of[...], minor, preferred_element_type=F32))
        grad_z = (grad_h * slope_of[...]).astype(BF16).astype(F32).T
        for d in range(ndp):
            gsend[d] = grad_z[d * cblk:(d + 1) * cblk].astype(BF16)

        def g_copy(o):
            t = lax.rem(dp * nz + chip + o, ndp * nz)
            d = t // nz
            return remote(gsend.at[d], gall.at[dp, core, chip], g_s.at[0], g_r.at[dp], d,
                          2 * lax.rem(t, nz) + core)

        each(1, ndp * nz, lambda o: g_copy(o).start())
        gall[dp, core, chip] = gsend[dp]

        def other_clip(o):
            q = lax.rem(dp + o, ndp)
            drain(call_.at[q], c_r.at[q])
            clip_stack(q)

        each(1, ndp, other_clip)

        def half(k):
            block = jnp.concatenate(
                [lhs[2 * s + k].reshape(3 * mblk, ndp * ext) for s in range(nz)], axis=0)
            return lax.dot_general(block, stack[...], NT, preferred_element_type=F32)

        sent = half(1 - core)
        for s in range(nz):
            qsend[s] = sent[s * 3 * mblk:(s + 1) * 3 * mblk].astype(BF16)
        swap = remote(qsend, qrecv, q_s.at[0], q_r.at[0], dp, 2 * chip + 1 - core)
        swap.start()
        acc2[...] = half(core)

        lx = lax.broadcasted_iota(jnp.int32, (1, clip_lanes), 1)
        x_low, x_high = (lx >= plane).astype(F32), (lx < clip_lanes - plane).astype(F32)

        def turn_clip(q):
            x = jnp.concatenate([xall[q, s] for s in range(nseq)], axis=1)
            xf = x.astype(F32)
            xs[q, 0:dblk] = (pltpu.roll(xf, plane, axis=1) * x_low).astype(BF16)
            xs[q, dblk:2 * dblk] = x
            xs[q, 2 * dblk:3 * dblk] = (
                pltpu.roll(xf, clip_lanes - plane, axis=1) * x_high).astype(BF16)

        swap.wait_recv()
        for s in range(nz):
            rsend[s] = (acc2[s * 3 * mblk:(s + 1) * 3 * mblk] + qrecv[s].astype(F32)).astype(BF16)

        def r_copy(o):
            s = lax.rem(chip + o, nz)
            return remote(rsend.at[s], rall.at[chip], r_s.at[0], r_r.at[0], dp, s * 2 + core)

        each(1, nz, lambda o: r_copy(o).start())
        rall[chip] = rsend[chip]

        def g_forward(q):
            return remote(gall.at[q, core], gall.at[q, core], f_s.at[0], f_r.at[q], dp,
                          2 * chip + 1 - core)

        def pass_on(o):
            q = lax.rem(dp + o, ndp)
            drain(gall.at[0, 0], g_r.at[q])
            g_forward(q).start()

        drain(gall.at[0, 0, pl.ds(0, nz - 1)], g_r.at[dp])
        g_forward(dp).start()
        each(1, ndp, pass_on)
        drain(xall.at[pl.ds(0, ndp - 1)], xd_r.at[0])
        each(0, ndp, turn_clip)

        lh = lax.rem(lx, rows)
        lc = lax.rem(lx, plane)
        g_h = ((lh < rows - 1).astype(F32), None, (lh > 0).astype(F32))
        g_w = ((lc < plane - rows).astype(F32), None, (lc >= rows).astype(F32))
        acc1[...] = jnp.zeros_like(acc1)

        def one_first(q):
            g = jnp.concatenate([gall[q, s % 2, s // 2].astype(F32) for s in range(nseq)], axis=1)
            grid = []
            for b in range(3):
                v = g if b == 1 else pltpu.roll(g, (b - 1) % clip_lanes, axis=1) * g_h[b]
                for c in range(3):
                    u = v if c == 1 else pltpu.roll(
                        v, ((c - 1) * rows) % clip_lanes, axis=1) * g_w[c]
                    grid.append(u.astype(BF16))
            acc1[...] += lax.dot_general(jnp.concatenate(grid, axis=0), xs[q], NT,
                                         preferred_element_type=F32)

        def arrived_first(o):
            q = lax.rem(dp + o, ndp)
            drain(gall.at[0, 0], f_r.at[q])
            one_first(q)

        each(0, ndp, arrived_first)
        for a in range(3):
            o1[a * 9 * cblk:(a + 1) * 9 * cblk] = acc1[:, a * dblk:(a + 1) * dblk]

        @pl.when(seq < nseq - 1)
        def _():
            up.wait_send()

        @pl.when(seq > 0)
        def _():
            down.wait_send()

        drain(hsend.at[pl.ds(0, nseq - 1)], h_s.at[0])
        drain(xbuf.at[pl.ds(0, nseq - 1)], xz_s.at[0])
        drain(htall.at[pl.ds(0, ndp - 1)], ht_s.at[0])
        drain(csend.at[pl.ds(0, ndp - 1)], c_s.at[0])
        drain(psend.at[pl.ds(0, nseq - 1)], p_s.at[0])
        drain(xall.at[pl.ds(0, ndp - 1)], xd_s.at[0])
        swap.wait_send()
        for o in range(ndp):
            drain(gall.at[0, 0, pl.ds(0, nz - 1)] if o == 0 else gall.at[0, 0], g_s.at[0])
        drain(gall.at[:, 0], f_s.at[0])
        drain(rall.at[pl.ds(0, nz - 1)], r_r.at[0])
        total = rall[0].astype(F32)
        for s in range(1, nz):
            total = total + rall[s].astype(F32)
        for a in range(3):
            for bc in range(9):
                o2[a * 9 + bc] = total[a * mblk:(a + 1) * mblk, bc * vblk:(bc + 1) * vblk]
        drain(rsend.at[pl.ds(0, nz - 1)], r_s.at[0])

    return kernel


def flush(a, b, oa, ob, sem):
    moves = (pltpu.make_async_copy(a, oa, sem.at[0]), pltpu.make_async_copy(b, ob, sem.at[1]))
    for m in moves:
        m.start()
    for m in moves:
        m.wait()


def per_device(tokens, conv_first, bias_first, conv_second, bias_second, pixels, mask_index):
    ndp, nseq = lax.axis_size("dp"), lax.axis_size("seq")
    tf, rows, cols, width = tokens.shape[1:]
    frames = tf * nseq
    mid, values = conv_second.shape[1], conv_second.shape[2]
    n = tf * rows * cols
    hb = rows // nseq
    he = hb + 2
    line = frames * cols
    ext = he * line
    chunk = tf * cols
    dims = (ndp, nseq, tf, rows, cols, width, mid, values)
    plane = rows * cols
    dblk, cblk, vblk, mblk = width // nseq, mid // ndp, values // ndp, mid // nseq
    nz = nseq // 2

    idx = np.arange(n, dtype=np.int32)
    t_of, w_of, h_of = idx // plane, idx // rows % cols, idx % rows
    flat_place = (h_of * cols + w_of)[:plane]
    tperm = jnp.asarray(flat_place[:, None] == idx[None, :plane], BF16)
    msg = np.arange(nseq * he * chunk, dtype=np.int32)
    m_s, m_h = msg // (he * chunk), msg // chunk % he
    m_t, m_w = msg % chunk // cols, msg % cols
    m_row = m_s * hb + m_h - 1
    same = ((m_row[:, None] == h_of[None]) & (m_t[:, None] == t_of[None])
            & (m_w[:, None] == w_of[None]))
    spread_of = jnp.asarray(same, BF16)
    gather_of = jnp.asarray(same.T, BF16)
    vm = pl.BlockSpec(memory_space=pltpu.VMEM)
    hbm = pl.BlockSpec(memory_space=pl.ANY)

    def dma(k):
        return pltpu.SemaphoreType.DMA((k,))

    scratch = [
        pltpu.VMEM((tf, rows, cols, width), BF16),
        pltpu.VMEM((1, mid), F32),
        pltpu.VMEM((values,), F32),
        pltpu.VMEM(mask_index.shape, jnp.int32),
        pltpu.VMEM((plane, plane), BF16),
        pltpu.VMEM((nseq * he * chunk, n), BF16),
        pltpu.VMEM((n, nseq * he * chunk), BF16),
        pltpu.VMEM((9 * width, 3 * mid), BF16),
        pltpu.VMEM((27 * mid, values), BF16),
        pltpu.VMEM((3, 3 * mid, 3 * values), BF16),
        pltpu.VMEM((4, 12 * mid, values), BF16),
        pltpu.VMEM((frames, hb, cols, 4 * values), BF16),
        pltpu.VMEM((nseq, dblk, n), BF16),
        pltpu.VMEM((ndp, nseq, dblk, n), BF16),
        pltpu.VMEM((ndp, 3 * dblk, nseq * n), BF16),
        pltpu.VMEM((2, plane, mid), F32),
        pltpu.VMEM((2, plane, mid), F32),
        pltpu.VMEM((3, tf, cols + 2, rows, width), BF16),
        pltpu.VMEM((n, 9 * width), BF16),
        pltpu.VMEM((n, mid), F32),
        pltpu.VMEM((nseq, he, chunk, mid), BF16),
        pltpu.VMEM((nseq, he, chunk, mid), BF16),
        pltpu.VMEM((9, ext, mid), BF16),
        pltpu.VMEM((4, n, values), F32),
        pltpu.VMEM((3 * n, 3 * values), BF16),
        pltpu.VMEM((nseq, he, chunk, mid), F32),
        pltpu.VMEM((nseq, he, chunk, mid), F32),
        pltpu.VMEM((mid, ext), BF16),
        pltpu.VMEM((ndp, mid, ext), BF16),
        pltpu.VMEM((nseq, 3, mblk, ndp * ext), BF16),
        pltpu.VMEM((ndp, 4, vblk, n), BF16),
        pltpu.VMEM((ndp, 4, vblk, n), BF16),
        pltpu.VMEM((9 * vblk, ndp * ext), BF16),
        pltpu.VMEM((nz, 3 * mblk, 9 * vblk), BF16),
        pltpu.VMEM((nz, 3 * mblk, 9 * vblk), BF16),
        pltpu.VMEM((nz, 3 * mblk, 9 * vblk), BF16),
        pltpu.VMEM((nz, 3 * mblk, 9 * vblk), BF16),
        pltpu.VMEM((ndp, cblk, n), BF16),
        pltpu.VMEM((ndp, 2, nz, cblk, n), BF16),
        pltpu.VMEM((9 * cblk, 3 * dblk), F32),
        pltpu.VMEM((nz * 3 * mblk, 9 * vblk), F32),
        dma(11), dma(2), dma(2), dma(1), dma(1), dma(1), dma(1), dma(1), dma(1), dma(1), dma(1),
        dma(1), dma(1), dma(1), dma(ndp), dma(1), dma(ndp), dma(1), dma(ndp), dma(1), dma(1),
        dma(1), dma(1),
    ]
    first, second = pl.pallas_call(
        make_kernel(dims),
        out_shape=(pltpu.VMEM((27 * cblk, dblk), F32), pltpu.VMEM((27, mblk, vblk), F32)),
        in_specs=[hbm] * 10,
        out_specs=(vm, vm),
        scratch_shapes=scratch,
        compiler_params=pltpu.CompilerParams(
            collective_id=0, has_side_effects=True, vmem_limit_bytes=60 * 1024 * 1024),
        name="step",
    )(tokens[0], conv_first.reshape(27 * width, mid), bias_first.reshape(1, mid),
      conv_second.reshape(27 * mid, values), bias_second,
      pixels[0], mask_index, tperm, spread_of, gather_of)
    first, second = pl.pallas_call(
        flush,
        out_shape=(jax.ShapeDtypeStruct(first.shape, F32), jax.ShapeDtypeStruct(second.shape, F32)),
        in_specs=[vm, vm],
        out_specs=(hbm, hbm),
        scratch_shapes=[dma(2)],
        compiler_params=pltpu.CompilerParams(vmem_limit_bytes=4 * 1024 * 1024),
        name="flush",
    )(pltpu.with_memory_space_constraint(first, pltpu.VMEM),
      pltpu.with_memory_space_constraint(second, pltpu.VMEM))
    first = first.reshape(27, cblk, dblk).transpose(0, 2, 1)
    return (first, second)


def solution(mesh):
    return jax.shard_map(
        per_device,
        mesh=mesh,
        in_specs=(
            P("dp", "seq", None, None, None),
            P(),
            P(),
            P(),
            P(),
            P("dp", None, "seq", None, None),
            P("dp", None),
        ),
        out_specs=(P(None, "seq", "dp"), P(None, "seq", "dp")),
        check_vma=False,
    )
```

```python
import jax
import jax.numpy as jnp
import numpy as np
from jax import lax
from jax.experimental import pallas as pl
from jax.experimental.pallas import tpu as pltpu
from jax.sharding import PartitionSpec as P

F32 = jnp.float32
BF16 = jnp.bfloat16
NT = (((1,), (1,)), ((), ()))
GELU_ROOT = 0.7978845608028654
GELU_CUBE = 0.044715


def floor_half(v):
    return v // 2 if v >= 0 else -1


def columns(total):
    half = -(-total // 512) * 256
    return [(0, half), (half, total - half)] if total > half else [(0, total)]


def make_kernel(dims):
    ndp, nseq, tf, rows, cols, width, mid, values = dims
    n = tf * cols * rows
    plane = cols * rows
    frames = tf * nseq
    hb = rows // nseq
    he = hb + 2
    line = frames * cols
    ext = he * line
    chunk = tf * cols
    dblk = width // nseq
    cblk = mid // ndp
    vblk = values // ndp
    mblk = mid // nseq
    ndev = ndp * nseq
    nz = nseq // 2
    clip_lanes = nseq * n
    nk = nz // 2
    cuts = columns(9 * vblk)

    def kernel(tok_hbm, w1_hbm, b1_hbm, w2_hbm, b2_hbm, pix_hbm, marks_hbm, tperm_hbm, spread_hbm,
               gather_hbm, o1, o2,
               tok, b1, b2, marks, tperm, spread_of, gather_of,
               w1, w2, w2b, weff, pixv, xbuf, xall, xs, tsend, thalo, tfield, im1, slope_of,
               hsend, hraw, vfield, tgt, cell, psend, praw,
               hrow, lhs, csend, call_, stack, gsend, gall, acc1, chunks,
               wsem, th_s, th_r, h_s, h_r, p_s, p_r, xz_s, xz_r, xd_s, xd_r, ht_s, ht_r, e_s, e_r,
               c_s, c_r, g_s, g_r, f_s, f_r, q_s, q_r, a_s, a_r, b_s, b_r):
        dp = lax.axis_index("dp")
        seq = lax.axis_index("seq")
        me = dp * nseq + seq
        chip, core = seq // 2, lax.rem(seq, 2)
        qsend, qrecv, asend, arecv, bsend, brecv, acc2 = chunks

        def remote(src, dst, ss, rs, d, s):
            return pltpu.make_async_remote_copy(
                src_ref=src, dst_ref=dst, send_sem=ss, recv_sem=rs,
                device_id=(d, s), device_id_type=pl.DeviceIdType.MESH)

        def drain(ref, sem):
            pltpu.make_async_copy(ref, ref, sem).wait()

        def each(low, count, act):
            def body(o, c):
                act(o)
                return c
            lax.fori_loop(low, count, body, 0)

        def peer(o):
            d, bit = 0, 1
            while bit < ndp:
                mine_, other = lax.rem(dp // bit, 2), (o // bit) % 2
                d = d + bit * (mine_ + other - 2 * mine_ * other)
                bit = bit * 2
            return d

        barrier = pltpu.get_barrier_semaphore()

        def greet(o):
            s, d = lax.div(o, ndp), lax.rem(o, ndp)

            @pl.when(jnp.logical_or(s != seq, d != dp))
            def _():
                pl.semaphore_signal(barrier, inc=1, device_id=(d, s),
                                    device_id_type=pl.DeviceIdType.MESH)

        loads = [pltpu.make_async_copy(src, dst, wsem.at[k]) for k, (src, dst) in enumerate((
            (tok_hbm, tok), (tperm_hbm, tperm), (b1_hbm, b1), (b2_hbm, b2), (marks_hbm, marks),
            (spread_hbm, spread_of), (gather_hbm, gather_of), (pix_hbm, pixv), (w2_hbm, w2)))]
        loads[0].start()
        loads[1].start()
        def w1_part(b, a, at):
            rows_ = 3 * width
            return pltpu.make_async_copy(
                w1_hbm.at[pl.ds((a * 9 + b * 3) * width, rows_)],
                w1.at[pl.ds(b * rows_, rows_), pl.ds(at * mid, mid)],
                wsem.at[13 if at == 2 else 9 + b])

        for b in range(3):
            w1_part(b, 0, 0).start()
            w1_part(b, 2, 1).start()
        for b in range(3):
            w1_part(b, 1, 2).start()
        each(0, ndev, greet)
        for m in loads[2:]:
            m.start()
        def ordered(frame):
            raw = frame.astype(F32).reshape(plane, width).astype(BF16)
            return jnp.dot(tperm[...], raw, preferred_element_type=F32)

        loads[0].wait()
        loads[1].wait()
        flat = jnp.concatenate([ordered(tok[t]) for t in range(tf)], axis=0)
        lr = lax.broadcasted_iota(jnp.int32, (rows, width), 0)
        edge = ((lr > 0).astype(F32), None, (lr < rows - 1).astype(F32))
        zero = jnp.zeros((3, tf, 1, rows, width), BF16)
        tfield[:, :, 0:1] = zero
        tfield[:, :, cols + 1:cols + 2] = zero
        for b in range(3):
            v = flat.reshape(tf, cols, rows, width)
            if b != 1:
                v = pltpu.roll(flat, 1 if b == 0 else n - 1, axis=0).reshape(
                    tf * cols, rows, width) * edge[b][None]
            tfield[b, :, 1:cols + 1] = v.reshape(tf, cols, rows, width).astype(BF16)
        for bc in range(9):
            im1[:, bc * width:(bc + 1) * width] = (
                tfield[bc // 3, :, bc % 3:bc % 3 + cols].reshape(n, width))
        parts = None
        for b in range(3):
            span = slice(b * 3 * width, (b + 1) * 3 * width)
            drain(w1.at[pl.ds(b * 3 * width, 3 * width), pl.ds(0, 2 * mid)], wsem.at[9 + b])
            part = jnp.dot(im1[:, span], w1[span, 0:2 * mid], preferred_element_type=F32)
            parts = part if parts is None else parts + part
        to_next, to_prev = parts[:, :mid], parts[:, mid:]
        tsend[0] = to_next[n - plane:]
        tsend[1] = to_prev[:plane]
        pl.semaphore_wait(barrier, ndev - 1)

        up = remote(tsend.at[0], thalo.at[0], th_s.at[0], th_r.at[0], dp,
                    jnp.minimum(seq + 1, nseq - 1))
        down = remote(tsend.at[1], thalo.at[1], th_s.at[1], th_r.at[1], dp,
                      jnp.maximum(seq - 1, 0))

        @pl.when(seq < nseq - 1)
        def _():
            up.start()

        @pl.when(seq > 0)
        def _():
            down.start()

        @pl.when(seq == 0)
        def _():
            thalo[0] = jnp.zeros((plane, mid), F32)

        @pl.when(seq == nseq - 1)
        def _():
            thalo[1] = jnp.zeros((plane, mid), F32)

        for m in loads[2:7]:
            m.wait()
        drain(w1.at[:, pl.ds(2 * mid, mid)], wsem.at[13])
        slope_of[...] = jnp.dot(im1[...], w1[:, 2 * mid:3 * mid],
                                preferred_element_type=F32) + b1[...]
        xt = flat.T
        for s in range(nseq):
            xbuf[s] = xt[s * dblk:(s + 1) * dblk].astype(BF16)

        @pl.when(seq > 0)
        def _():
            up.wait_recv()

        @pl.when(seq < nseq - 1)
        def _():
            down.wait_recv()

        if tf > 1:
            late = jnp.concatenate([thalo[0], to_next[:n - plane]], axis=0)
            early = jnp.concatenate([to_prev[plane:], thalo[1]], axis=0)
        else:
            late, early = thalo[0], thalo[1]
        z = slope_of[...] + late + early
        th_ = jnp.tanh(GELU_ROOT * (z + GELU_CUBE * z * z * z))
        hid = (0.5 * z * (1.0 + th_)).astype(BF16)
        hsend[...] = jnp.dot(spread_of[...], hid, preferred_element_type=F32).reshape(
            nseq, he, chunk, mid).astype(BF16)

        def h_copy(o):
            s = lax.rem(seq + o, nseq)
            return remote(hsend.at[s], hraw.at[seq], h_s.at[0], h_r.at[0], dp, s)

        each(1, nseq, lambda o: h_copy(o).start())
        hraw[seq] = hsend[seq]
        slope_of[...] = 0.5 * (1.0 + th_) + 0.5 * z * (1.0 - th_ * th_) * GELU_ROOT * (
            1.0 + 3.0 * GELU_CUBE * z * z)

        for m in loads[7:]:
            m.wait()
        raw = [pixv[:, h].astype(F32).reshape(line, 4 * values) for h in range(hb)]
        px = jnp.concatenate(raw, axis=0)
        center = px - jnp.mean(px, axis=-1, keepdims=True)
        spread = jnp.mean(center * center, axis=-1, keepdims=True)
        normed = center * lax.rsqrt(spread + 1e-06)
        for ij in range(4):
            tgt[ij] = normed[:, ij * values:(ij + 1) * values] - b2[...].reshape(1, values)
        le = lax.broadcasted_iota(jnp.int32, (n, 1), 0)
        spot = lax.div(le, line) * cols + lax.rem(le, cols) + seq * (hb * cols)
        matches = (spot == marks[...]).astype(F32)
        scale = 2.0 / (4 * values) * jnp.sum(matches, axis=1, keepdims=True)

        step = 16 if mid % 16 == 0 else mid

        def sum_taps(o):
            a, r = lax.div(o, mid // step), lax.rem(o, mid // step)
            w = []
            for bc in range(9):
                part = w2[pl.ds(pl.multiple_of((a * 9 + bc) * mid + r * step, step), step)]
                w2b[bc // 3, pl.ds(pl.multiple_of(a * mid + r * step, step), step),
                    (bc % 3) * values:(bc % 3 + 1) * values] = part
                w.append(part.astype(F32))
            wide = []
            for b in range(3):
                x, y, z_ = w[b * 3:b * 3 + 3]
                wide.append((x, y + z_, x + y, z_))
            for i in range(2):
                for e in range(4):
                    x, y, z_ = wide[0][e], wide[1][e], wide[2][e]
                    for rh, v in enumerate((x, y + z_) if i == 0 else (x + y, z_)):
                        at = (a * 4 + rh * 2 + e % 2) * mid + r * step
                        weff[i * 2 + e // 2, pl.ds(pl.multiple_of(at, step), step)] = v.astype(BF16)

        each(0, 3 * (mid // step), sum_taps)

        def band(size):
            li = lax.broadcasted_iota(jnp.int32, (line, size), 0)
            lw = lax.rem(li, cols)
            return ((lw > 0).astype(F32), (lw < cols - 1).astype(F32),
                    (li >= cols).astype(F32), (li < line - cols).astype(F32))

        w_low, w_high, t_low, t_high = band(mid)
        p_low, p_high, _, _ = band(values)
        le = lax.broadcasted_iota(jnp.int32, (1, ext), 1)
        lw = lax.rem(le, cols)
        lt = lax.rem(le, line)
        s_low, s_high = (lt >= cols).astype(F32), (lt < line - cols).astype(F32)

        def shifted(v, by, mask):
            m = v.shape[0]
            rolled = pltpu.roll(v, (-by) % m, axis=0)
            return (rolled.reshape(m // line, line, v.shape[1]) * mask[None]).reshape(v.shape)

        drain(hraw.at[pl.ds(0, nseq - 1)], h_r.at[0])

        def xz_copy(o):
            s = lax.rem(seq + o, nseq)
            return remote(xbuf.at[s], xall.at[dp, seq], xz_s.at[0], xz_r.at[0], dp, s)

        each(1, nseq, lambda o: xz_copy(o).start())
        xall[dp, seq] = xbuf[seq]

        hin = hraw[...].astype(F32)
        hext = jnp.concatenate(
            [hin[:, hh].reshape(line, mid) for hh in range(he)], axis=0)
        for a in range(3):
            late = hext if a == 1 else shifted(
                hext, cols * (a - 1), t_low if a == 0 else t_high)
            for e in range(3):
                v = late if e == 1 else shifted(late, e - 1, w_low if e == 0 else w_high)
                vfield[a * 3 + e] = v.astype(BF16)
        hrow[dp, 0:hb * line] = hext[line:(hb + 1) * line].astype(BF16)
        hrow[dp, hb * line:(hb + 1) * line] = hext[0:line].astype(BF16)
        hrow[dp, (hb + 1) * line:ext] = hext[(hb + 1) * line:ext].astype(BF16)
        mine = hrow.at[dp, pl.ds(0, hb * line)]

        def ht_copy(o):
            d = peer(o)
            return remote(mine, mine, ht_s.at[0], ht_r.at[0], d, seq)

        each(1, ndp, lambda o: ht_copy(o).start())

        cots = []
        for ij in range(4):
            i, j = ij // 2, ij % 2
            near = []
            for k in range(12):
                low = (i + k // 2 % 2) * line
                near.append(vfield[k // 4 * 3 + j + k % 2, low:low + hb * line])
            predict = jnp.dot(jnp.concatenate(near, axis=1), weff[ij], preferred_element_type=F32)
            cot = (scale * (predict - tgt[ij])).astype(BF16).astype(F32)
            cots.append(cot)
            turned = cot.T
            for d in range(ndp):
                csend[d, ij] = turned[d * vblk:(d + 1) * vblk].astype(BF16)

        def c_copy(o):
            d = peer(o)
            return remote(csend.at[d], call_.at[dp], c_s.at[0], c_r.at[dp], d, seq)

        each(1, ndp, lambda o: c_copy(o).start())
        call_[dp] = csend[dp]

        def pair_sums(low, high, after, before):
            return (high + after(low), low + high, before(high) + low)

        def after_row(v):
            return shifted(v, 1, p_high)

        def before_row(v):
            return shifted(v, -1, p_low)

        for u, (low, high) in enumerate((
                (cots[0], cots[1]), (cots[2], cots[3]),
                (cots[0] + cots[2], cots[1] + cots[3]))):
            for c, s in enumerate(pair_sums(low, high, after_row, before_row)):
                cell[u * n:(u + 1) * n, c * values:(c + 1) * values] = s.astype(BF16)

        both = cell[0:2 * n]
        first = lax.dot_general(both, w2b[0], NT, preferred_element_type=F32)
        third = lax.dot_general(both, w2b[2], NT, preferred_element_type=F32)
        second = lax.dot_general(cell[2 * n:3 * n], w2b[1], NT, preferred_element_type=F32)
        same = first[n:] + second + third[:n]
        pieces = []
        for hh in range(he):
            total = None
            for v, dh in ((first[:n], -1), (same, 0), (third[n:], 1)):
                h = hh - 1 - dh
                if 0 <= h < hb:
                    part = v[h * line:(h + 1) * line]
                    total = part if total is None else total + part
            back = total[:, mid:2 * mid]
            back = back + shifted(total[:, :mid], cols, t_high)
            back = back + shifted(total[:, 2 * mid:], -cols, t_low)
            pieces.append(back)
        for hh in range(he):
            psend[:, hh] = pieces[hh].reshape(nseq, chunk, mid)

        def p_copy(o):
            s = lax.rem(seq + o, nseq)
            return remote(psend.at[s], praw.at[seq], p_s.at[0], p_r.at[0], dp, s)

        each(1, nseq, lambda o: p_copy(o).start())
        praw[seq] = psend[seq]

        drain(hrow.at[pl.ds(0, ndp - 1), pl.ds(0, hb * line)], ht_r.at[0])
        others = pl.ds(0, ndp - 1)

        def edge_copy(o, k):
            q = peer(o)
            if k == 0:
                return remote(hrow.at[q, pl.ds((hb - 1) * line, line)],
                              hrow.at[q, pl.ds(hb * line, line)], e_s.at[0], e_r.at[0], dp,
                              jnp.minimum(seq + 1, nseq - 1))
            return remote(hrow.at[q, pl.ds(0, line)],
                          hrow.at[q, pl.ds((hb + 1) * line, line)], e_s.at[1], e_r.at[1], dp,
                          jnp.maximum(seq - 1, 0))

        def no_edge(k):
            def put(o):
                q = peer(o)
                hrow[q, (hb + k) * line:(hb + k + 1) * line] = jnp.zeros((line, mid), BF16)
            each(1, ndp, put)

        @pl.when(seq < nseq - 1)
        def _():
            each(1, ndp, lambda o: edge_copy(o, 0).start())

        @pl.when(seq > 0)
        def _():
            each(1, ndp, lambda o: edge_copy(o, 1).start())

        @pl.when(seq == 0)
        def _():
            no_edge(0)

        @pl.when(seq == nseq - 1)
        def _():
            no_edge(1)

        lo = lax.broadcasted_iota(jnp.int32, (1, hb * line), 1)
        lw = lax.rem(lo, cols)
        e_low, e_high = (lw > 0).astype(F32), (lw < cols - 1).astype(F32)
        early_rows, late_rows = (lo < (hb - 1) * line).astype(F32), (lo >= line).astype(F32)

        def lane_after(v):
            return pltpu.roll(v, hb * line - 1, axis=1) * e_high

        def lane_before(v):
            return pltpu.roll(v, 1, axis=1) * e_low

        stack[3 * vblk:6 * vblk] = jnp.zeros((3 * vblk, ndp * ext), BF16)

        def clip_stack(q):
            by_col, by_edge = [], []
            for j in range(2):
                low, high = call_[q, j].astype(F32), call_[q, 2 + j].astype(F32)
                by_col.append((high + pltpu.roll(low, (hb - 1) * line, axis=1) * early_rows,
                               low + high, low + pltpu.roll(high, line, axis=1) * late_rows))
                by_edge.append((low * early_rows, None, high * late_rows))
            base = q * ext
            at = pl.ds(pl.multiple_of(base, 128), hb * line)
            rim = pl.ds(pl.multiple_of(base + hb * line, 128), 2 * line)
            k = 0
            for b in range(3):
                inner = pair_sums(by_col[0][b], by_col[1][b], lane_after, lane_before)
                outer = (None,) * 3 if b == 1 else pair_sums(
                    by_edge[0][b], by_edge[1][b], lane_after, lane_before)
                for s, r in zip(inner, outer):
                    stack[k * vblk:(k + 1) * vblk, at] = s.astype(BF16)
                    if r is not None:
                        stack[k * vblk:(k + 1) * vblk, rim] = r.astype(BF16)
                    k += 1

        clip_stack(dp)

        def clip_lhs(low, high):
            size = high - low
            for q in range(ndp):
                turned = hrow[q, low:high].astype(F32).T
                for a in range(3):
                    v = turned
                    if a != 1:
                        v = pltpu.roll(turned, (cols if a == 0 else size - cols), axis=1)
                        v = v * (s_low if a == 0 else s_high)[:, low:high]
                    lhs[:, a, :, q * ext + low:q * ext + high] = (
                        v.reshape(nseq, mblk, size).astype(BF16))

        clip_lhs(0, hb * line)

        def other_clip(o):
            q = peer(o)
            drain(call_.at[q], c_r.at[q])
            clip_stack(q)

        each(1, ndp - 1, other_clip)

        @pl.when(seq > 0)
        def _():
            drain(hrow.at[others, pl.ds(0, line)], e_r.at[0])

        @pl.when(seq < nseq - 1)
        def _():
            drain(hrow.at[others, pl.ds(0, line)], e_r.at[1])

        clip_lhs(hb * line, ext)
        drain(praw.at[pl.ds(0, nseq - 1)], p_r.at[0])
        got = praw[...].reshape(nseq * he * chunk, mid)
        major = got.astype(BF16)
        minor = (got - major.astype(F32)).astype(BF16)
        grad_h = (jnp.dot(gather_of[...], major, preferred_element_type=F32)
                  + jnp.dot(gather_of[...], minor, preferred_element_type=F32))
        grad_z = (grad_h * slope_of[...]).astype(BF16).astype(F32).T
        for d in range(ndp):
            gsend[d] = grad_z[d * cblk:(d + 1) * cblk].astype(BF16)

        def g_copy(o):
            t = lax.rem(dp * nz + chip + o, ndp * nz)
            d = t // nz
            return remote(gsend.at[d], gall.at[dp, core, chip], g_s.at[0], g_r.at[dp], d,
                          2 * lax.rem(t, nz) + core)

        each(1, ndp * nz, lambda o: g_copy(o).start())
        gall[dp, core, chip] = gsend[dp]
        drain(xall.at[0, pl.ds(0, nseq - 1)], xz_r.at[0])

        def xd_copy(o):
            d = peer(o)
            return remote(xall.at[dp], xall.at[dp], xd_s.at[0], xd_r.at[dp], d, seq)

        each(1, ndp, lambda o: xd_copy(o).start())

        other_clip(ndp - 1)

        def half(k, j):
            block = jnp.concatenate(
                [lhs[2 * s + k].reshape(3 * mblk, ndp * ext) for s in range(nz)], axis=0)
            low, size = cuts[j]
            return lax.dot_general(block, stack[low:low + size], NT, preferred_element_type=F32)

        swaps = [remote(qs, qr, q_s.at[j], q_r.at[j], dp, 2 * chip + 1 - core)
                 for j, (qs, qr) in enumerate(zip(qsend, qrecv))]
        for j in range(len(cuts)):
            sent = half(1 - core, j)
            qsend[j][...] = sent.reshape(nk, 2, 3 * mblk, cuts[j][1]).astype(BF16)
            swaps[j].start()
        par, kz = lax.rem(chip, 2), chip // 2

        def near_copy(j, k):
            return remote(asend[j].at[k], arecv[j].at[k], a_s.at[2 * j], a_r.at[2 * j], dp,
                          2 * (chip + 1 - 2 * par) + core)

        def last_copy(j):
            return remote(asend[j].at[kz], arecv[j].at[kz], a_s.at[2 * j + 1], a_r.at[2 * j + 1],
                          dp, 2 * (chip + 1 - 2 * par) + core)

        def far_copy(j, o):
            k = lax.rem(kz + o, nk)
            return remote(bsend[j].at[k], brecv[j].at[kz], b_s.at[j], b_r.at[j], dp,
                          2 * (2 * k + par) + core)

        for j in range(len(cuts)):
            size = cuts[j][1]
            acc2[j][...] = half(core, j).reshape(nk, 2, 3 * mblk, size)
            swaps[j].wait_recv()
            asend[j][...] = (acc2[j][:, 1 - par] + qrecv[j][:, 1 - par].astype(F32)).astype(BF16)
            each(1, nk, lambda o: near_copy(j, lax.rem(kz + o, nk)).start())
            last_copy(j).start()
            acc2[j][:, par] = acc2[j][:, par] + qrecv[j][:, par].astype(F32)
        for j in range(len(cuts)):
            drain(asend[j].at[pl.ds(0, nk - 1)], a_r.at[2 * j])

            def combine(o):
                k = lax.rem(kz + o, nk)
                bsend[j][k] = (acc2[j][k, par] + arecv[j][k].astype(F32)).astype(BF16)
                far_copy(j, o).start()

            each(1, nk, combine)

        lx = lax.broadcasted_iota(jnp.int32, (1, clip_lanes), 1)
        x_low, x_high = (lx >= plane).astype(F32), (lx < clip_lanes - plane).astype(F32)

        def turn_clip(q):
            x = jnp.concatenate([xall[q, s] for s in range(nseq)], axis=1)
            xf = x.astype(F32)
            xs[q, 0:dblk] = (pltpu.roll(xf, plane, axis=1) * x_low).astype(BF16)
            xs[q, dblk:2 * dblk] = x
            xs[q, 2 * dblk:3 * dblk] = (
                pltpu.roll(xf, clip_lanes - plane, axis=1) * x_high).astype(BF16)


        def g_forward(q):
            return remote(gall.at[q, core], gall.at[q, core], f_s.at[0], f_r.at[q], dp,
                          2 * chip + 1 - core)

        def pass_on(o):
            q = peer(o)
            drain(gall.at[0, 0], g_r.at[q])
            g_forward(q).start()

        drain(gall.at[0, 0, pl.ds(0, nz - 1)], g_r.at[dp])
        g_forward(dp).start()
        each(1, ndp, pass_on)

        lh = lax.rem(lx, rows)
        lc = lax.rem(lx, plane)
        g_h = ((lh < rows - 1).astype(F32), None, (lh > 0).astype(F32))
        g_w = ((lc < plane - rows).astype(F32), None, (lc >= rows).astype(F32))
        acc1[...] = jnp.zeros_like(acc1)

        def one_first(q):
            g = jnp.concatenate([gall[q, s % 2, s // 2].astype(F32) for s in range(nseq)], axis=1)
            grid = []
            for b in range(3):
                v = g if b == 1 else pltpu.roll(g, (b - 1) % clip_lanes, axis=1) * g_h[b]
                for c in range(3):
                    u = v if c == 1 else pltpu.roll(
                        v, ((c - 1) * rows) % clip_lanes, axis=1) * g_w[c]
                    grid.append(u.astype(BF16))
            acc1[...] += lax.dot_general(jnp.concatenate(grid, axis=0), xs[q], NT,
                                         preferred_element_type=F32)

        turn_clip(dp)
        drain(gall.at[0, 0], f_r.at[dp])
        one_first(dp)

        def arrived_first(o):
            q = peer(o)
            drain(xall.at[0], xd_r.at[q])
            turn_clip(q)
            drain(gall.at[0, 0], f_r.at[q])
            one_first(q)

        each(1, ndp, arrived_first)
        for a in range(3):
            o1[a * 9 * cblk:(a + 1) * 9 * cblk] = acc1[:, a * dblk:(a + 1) * dblk]

        @pl.when(seq < nseq - 1)
        def _():
            up.wait_send()

        @pl.when(seq > 0)
        def _():
            down.wait_send()

        drain(hsend.at[pl.ds(0, nseq - 1)], h_s.at[0])
        drain(xbuf.at[pl.ds(0, nseq - 1)], xz_s.at[0])
        drain(hrow.at[pl.ds(0, ndp - 1), pl.ds(0, hb * line)], ht_s.at[0])
        drain(csend.at[pl.ds(0, ndp - 1)], c_s.at[0])
        drain(psend.at[pl.ds(0, nseq - 1)], p_s.at[0])
        drain(xall.at[pl.ds(0, ndp - 1)], xd_s.at[0])
        for w in swaps:
            w.wait_send()
        for o in range(ndp):
            drain(gall.at[0, 0, pl.ds(0, nz - 1)] if o == 0 else gall.at[0, 0], g_s.at[0])
        drain(gall.at[:, 0], f_s.at[0])
        @pl.when(seq < nseq - 1)
        def _():
            drain(hrow.at[others, pl.ds(0, line)], e_s.at[0])

        @pl.when(seq > 0)
        def _():
            drain(hrow.at[others, pl.ds(0, line)], e_s.at[1])

        totals = []
        for j in range(len(cuts)):
            drain(asend[j].at[0], a_r.at[2 * j + 1])
            acc2[j][kz, par] = acc2[j][kz, par] + arecv[j][kz].astype(F32)
            drain(brecv[j].at[pl.ds(0, nk - 1)], b_r.at[j])

            def add(o):
                acc2[j][kz, par] = (acc2[j][kz, par]
                                    + brecv[j][lax.rem(kz + o, nk)].astype(F32))

            each(1, nk, add)
            totals.append(acc2[j][kz, par])
        total = jnp.concatenate(totals, axis=1)
        for a in range(3):
            for bc in range(9):
                o2[a * 9 + bc] = total[a * mblk:(a + 1) * mblk, bc * vblk:(bc + 1) * vblk]
        for j in range(len(cuts)):
            drain(asend[j].at[pl.ds(0, nk - 1)], a_s.at[2 * j])
            drain(asend[j].at[0], a_s.at[2 * j + 1])
            drain(brecv[j].at[pl.ds(0, nk - 1)], b_s.at[j])

    return kernel


def flush(a, b, oa, ob, sem):
    moves = (pltpu.make_async_copy(a, oa, sem.at[0]), pltpu.make_async_copy(b, ob, sem.at[1]))
    for m in moves:
        m.start()
    for m in moves:
        m.wait()


def per_device(tokens, conv_first, bias_first, conv_second, bias_second, pixels, mask_index):
    ndp, nseq = lax.axis_size("dp"), lax.axis_size("seq")
    tf, rows, cols, width = tokens.shape[1:]
    frames = tf * nseq
    mid, values = conv_second.shape[1], conv_second.shape[2]
    n = tf * rows * cols
    hb = rows // nseq
    he = hb + 2
    line = frames * cols
    ext = he * line
    chunk = tf * cols
    dims = (ndp, nseq, tf, rows, cols, width, mid, values)
    plane = rows * cols
    dblk, cblk, vblk, mblk = width // nseq, mid // ndp, values // ndp, mid // nseq
    nz = nseq // 2
    cuts = columns(9 * vblk)

    idx = np.arange(n, dtype=np.int32)
    t_of, w_of, h_of = idx // plane, idx // rows % cols, idx % rows
    flat_place = (h_of * cols + w_of)[:plane]
    tperm = jnp.asarray(flat_place[:, None] == idx[None, :plane], BF16)
    msg = np.arange(nseq * he * chunk, dtype=np.int32)
    m_s, m_h = msg // (he * chunk), msg // chunk % he
    m_t, m_w = msg % chunk // cols, msg % cols
    m_row = m_s * hb + m_h - 1
    same = ((m_row[:, None] == h_of[None]) & (m_t[:, None] == t_of[None])
            & (m_w[:, None] == w_of[None]))
    spread_of = jnp.asarray(same, BF16)
    gather_of = jnp.asarray(same.T, BF16)
    vm = pl.BlockSpec(memory_space=pltpu.VMEM)
    hbm = pl.BlockSpec(memory_space=pl.ANY)

    def dma(k):
        return pltpu.SemaphoreType.DMA((k,))

    scratch = [
        pltpu.VMEM((tf, rows, cols, width), BF16),
        pltpu.VMEM((1, mid), F32),
        pltpu.VMEM((values,), F32),
        pltpu.VMEM(mask_index.shape, jnp.int32),
        pltpu.VMEM((plane, plane), BF16),
        pltpu.VMEM((nseq * he * chunk, n), BF16),
        pltpu.VMEM((n, nseq * he * chunk), BF16),
        pltpu.VMEM((9 * width, 3 * mid), BF16),
        pltpu.VMEM((27 * mid, values), BF16),
        pltpu.VMEM((3, 3 * mid, 3 * values), BF16),
        pltpu.VMEM((4, 12 * mid, values), BF16),
        pltpu.VMEM((frames, hb, cols, 4 * values), BF16),
        pltpu.VMEM((nseq, dblk, n), BF16),
        pltpu.VMEM((ndp, nseq, dblk, n), BF16),
        pltpu.VMEM((ndp, 3 * dblk, nseq * n), BF16),
        pltpu.VMEM((2, plane, mid), F32),
        pltpu.VMEM((2, plane, mid), F32),
        pltpu.VMEM((3, tf, cols + 2, rows, width), BF16),
        pltpu.VMEM((n, 9 * width), BF16),
        pltpu.VMEM((n, mid), F32),
        pltpu.VMEM((nseq, he, chunk, mid), BF16),
        pltpu.VMEM((nseq, he, chunk, mid), BF16),
        pltpu.VMEM((9, ext, mid), BF16),
        pltpu.VMEM((4, n, values), F32),
        pltpu.VMEM((3 * n, 3 * values), BF16),
        pltpu.VMEM((nseq, he, chunk, mid), F32),
        pltpu.VMEM((nseq, he, chunk, mid), F32),
        pltpu.VMEM((ndp, ext, mid), BF16),
        pltpu.VMEM((nseq, 3, mblk, ndp * ext), BF16),
        pltpu.VMEM((ndp, 4, vblk, n), BF16),
        pltpu.VMEM((ndp, 4, vblk, n), BF16),
        pltpu.VMEM((9 * vblk, ndp * ext), BF16),
        pltpu.VMEM((ndp, cblk, n), BF16),
        pltpu.VMEM((ndp, 2, nz, cblk, n), BF16),
        pltpu.VMEM((9 * cblk, 3 * dblk), F32),
        [[pltpu.VMEM((nz // 2, 2, 3 * mblk, size), BF16) for _, size in cuts] for _ in range(2)]
        + [[pltpu.VMEM((nz // 2, 3 * mblk, size), BF16) for _, size in cuts] for _ in range(4)]
        + [[pltpu.VMEM((nz // 2, 2, 3 * mblk, size), F32) for _, size in cuts]],
        dma(14), dma(2), dma(2), dma(1), dma(1), dma(1), dma(1), dma(1), dma(1), dma(1), dma(ndp),
        dma(1), dma(1), dma(2), dma(2), dma(1), dma(ndp), dma(1), dma(ndp), dma(1), dma(ndp),
        dma(len(cuts)), dma(len(cuts)), dma(2 * len(cuts)), dma(2 * len(cuts)),
        dma(len(cuts)), dma(len(cuts)),
    ]
    first, second = pl.pallas_call(
        make_kernel(dims),
        out_shape=(pltpu.VMEM((27 * cblk, dblk), F32), pltpu.VMEM((27, mblk, vblk), F32)),
        in_specs=[hbm] * 10,
        out_specs=(vm, vm),
        scratch_shapes=scratch,
        compiler_params=pltpu.CompilerParams(
            collective_id=0, has_side_effects=True, vmem_limit_bytes=60 * 1024 * 1024),
        name="step",
    )(tokens[0], conv_first.reshape(27 * width, mid), bias_first.reshape(1, mid),
      conv_second.reshape(27 * mid, values), bias_second,
      pixels[0], mask_index, tperm, spread_of, gather_of)
    first, second = pl.pallas_call(
        flush,
        out_shape=(jax.ShapeDtypeStruct(first.shape, F32), jax.ShapeDtypeStruct(second.shape, F32)),
        in_specs=[vm, vm],
        out_specs=(hbm, hbm),
        scratch_shapes=[dma(2)],
        compiler_params=pltpu.CompilerParams(vmem_limit_bytes=4 * 1024 * 1024),
        name="flush",
    )(pltpu.with_memory_space_constraint(first, pltpu.VMEM),
      pltpu.with_memory_space_constraint(second, pltpu.VMEM))
    first = first.reshape(27, cblk, dblk).transpose(0, 2, 1)
    return (first, second)


def solution(mesh):
    return jax.shard_map(
        per_device,
        mesh=mesh,
        in_specs=(
            P("dp", "seq", None, None, None),
            P(),
            P(),
            P(),
            P(),
            P("dp", None, "seq", None, None),
            P("dp", None),
        ),
        out_specs=(P(None, "seq", "dp"), P(None, "seq", "dp")),
        check_vma=False,
    )
```

```python
import jax
import jax.numpy as jnp
import numpy as np
from jax import lax
from jax.experimental import pallas as pl
from jax.experimental.pallas import tpu as pltpu
from jax.sharding import PartitionSpec as P

F32 = jnp.float32
BF16 = jnp.bfloat16
NT = (((1,), (1,)), ((), ()))
GELU_ROOT = 0.7978845608028654
GELU_CUBE = 0.044715


def floor_half(v):
    return v // 2 if v >= 0 else -1


def columns(total):
    half = -(-total // 512) * 256
    return [(0, half), (half, total - half)] if total > half else [(0, total)]


def make_kernel(dims):
    ndp, nseq, tf, rows, cols, width, mid, values = dims
    n = tf * cols * rows
    plane = cols * rows
    frames = tf * nseq
    hb = rows // nseq
    he = hb + 2
    line = frames * cols
    ext = he * line
    chunk = tf * cols
    dblk = width // nseq
    cblk = mid // ndp
    vblk = values // ndp
    mblk = mid // nseq
    ndev = ndp * nseq
    nz = nseq // 2
    clip_lanes = nseq * n
    nk = nz // 2
    cuts = columns(9 * vblk)

    def kernel(tok_hbm, w1_hbm, b1_hbm, w2_hbm, b2_hbm, pix_hbm, marks_hbm, tperm_hbm, spread_hbm,
               gather_hbm, o1, o2,
               tok, b1, b2, marks, tperm, spread_of, gather_of,
               w1, w2, w2b, weff, pixv, xbuf, xall, xs, tsend, thalo, tfield, im1, slope_of,
               hsend, hraw, vfield, tgt, cell, psend, praw,
               hrow, lhs, csend, call_, stack, gsend, gall, acc1, rsend, rall, asend, arecv, bsend, brecv,
               chunks,
               wsem, th_s, th_r, h_s, h_r, p_s, p_r, xz_s, xz_r, xd_s, xd_r, ht_s, ht_r, e_s, e_r,
               c_s, c_r, g_s, g_r, f_s, f_r, q_s, q_r, r_s, r_r, a_s, a_r, b_s, b_r):
        dp = lax.axis_index("dp")
        seq = lax.axis_index("seq")
        me = dp * nseq + seq
        chip, core = seq // 2, lax.rem(seq, 2)
        qsend, qrecv, acc2, acc3 = chunks

        def remote(src, dst, ss, rs, d, s):
            return pltpu.make_async_remote_copy(
                src_ref=src, dst_ref=dst, send_sem=ss, recv_sem=rs,
                device_id=(d, s), device_id_type=pl.DeviceIdType.MESH)

        def drain(ref, sem):
            pltpu.make_async_copy(ref, ref, sem).wait()

        def each(low, count, act):
            def body(o, c):
                act(o)
                return c
            lax.fori_loop(low, count, body, 0)

        def differ(at, o, size):
            d, bit = 0, 1
            while bit < size:
                mine_, other = lax.rem(at // bit, 2), (o // bit) % 2
                d = d + bit * (mine_ + other - 2 * mine_ * other)
                bit = bit * 2
            return d

        def peer(o):
            return differ(dp, o, ndp)

        barrier = pltpu.get_barrier_semaphore()

        def greet(o):
            s, d = lax.div(o, ndp), lax.rem(o, ndp)

            @pl.when(jnp.logical_or(s != seq, d != dp))
            def _():
                pl.semaphore_signal(barrier, inc=1, device_id=(d, s),
                                    device_id_type=pl.DeviceIdType.MESH)

        loads = [pltpu.make_async_copy(src, dst, wsem.at[k]) for k, (src, dst) in enumerate((
            (tok_hbm, tok), (tperm_hbm, tperm), (b1_hbm, b1), (b2_hbm, b2), (marks_hbm, marks),
            (spread_hbm, spread_of), (gather_hbm, gather_of), (pix_hbm, pixv), (w2_hbm, w2)))]
        loads[0].start()
        loads[1].start()
        def w1_part(b, a, at):
            rows_ = 3 * width
            return pltpu.make_async_copy(
                w1_hbm.at[pl.ds((a * 9 + b * 3) * width, rows_)],
                w1.at[pl.ds(b * rows_, rows_), pl.ds(at * mid, mid)],
                wsem.at[13 if at == 2 else 9 + b])

        for b in range(3):
            w1_part(b, 0, 0).start()
            w1_part(b, 2, 1).start()
        for b in range(3):
            w1_part(b, 1, 2).start()
        each(0, ndev, greet)
        for m in loads[2:]:
            m.start()
        def ordered(frame):
            raw = frame.astype(F32).reshape(plane, width).astype(BF16)
            return jnp.dot(tperm[...], raw, preferred_element_type=F32)

        loads[0].wait()
        loads[1].wait()
        flat = jnp.concatenate([ordered(tok[t]) for t in range(tf)], axis=0)
        lr = lax.broadcasted_iota(jnp.int32, (rows, width), 0)
        edge = ((lr > 0).astype(F32), None, (lr < rows - 1).astype(F32))
        zero = jnp.zeros((3, tf, 1, rows, width), BF16)
        tfield[:, :, 0:1] = zero
        tfield[:, :, cols + 1:cols + 2] = zero
        for b in range(3):
            v = flat.reshape(tf, cols, rows, width)
            if b != 1:
                v = pltpu.roll(flat, 1 if b == 0 else n - 1, axis=0).reshape(
                    tf * cols, rows, width) * edge[b][None]
            tfield[b, :, 1:cols + 1] = v.reshape(tf, cols, rows, width).astype(BF16)
        for bc in range(9):
            im1[:, bc * width:(bc + 1) * width] = (
                tfield[bc // 3, :, bc % 3:bc % 3 + cols].reshape(n, width))
        parts = None
        for b in range(3):
            span = slice(b * 3 * width, (b + 1) * 3 * width)
            drain(w1.at[pl.ds(b * 3 * width, 3 * width), pl.ds(0, 2 * mid)], wsem.at[9 + b])
            part = jnp.dot(im1[:, span], w1[span, 0:2 * mid], preferred_element_type=F32)
            parts = part if parts is None else parts + part
        to_next, to_prev = parts[:, :mid], parts[:, mid:]
        tsend[0] = to_next[n - plane:]
        tsend[1] = to_prev[:plane]
        pl.semaphore_wait(barrier, ndev - 1)

        up = remote(tsend.at[0], thalo.at[0], th_s.at[0], th_r.at[0], dp,
                    jnp.minimum(seq + 1, nseq - 1))
        down = remote(tsend.at[1], thalo.at[1], th_s.at[1], th_r.at[1], dp,
                      jnp.maximum(seq - 1, 0))

        @pl.when(seq < nseq - 1)
        def _():
            up.start()

        @pl.when(seq > 0)
        def _():
            down.start()

        @pl.when(seq == 0)
        def _():
            thalo[0] = jnp.zeros((plane, mid), F32)

        @pl.when(seq == nseq - 1)
        def _():
            thalo[1] = jnp.zeros((plane, mid), F32)

        for m in loads[2:7]:
            m.wait()
        drain(w1.at[:, pl.ds(2 * mid, mid)], wsem.at[13])
        slope_of[...] = jnp.dot(im1[...], w1[:, 2 * mid:3 * mid],
                                preferred_element_type=F32) + b1[...]
        xt = flat.T
        for s in range(nseq):
            xbuf[s] = xt[s * dblk:(s + 1) * dblk].astype(BF16)

        @pl.when(seq > 0)
        def _():
            up.wait_recv()

        @pl.when(seq < nseq - 1)
        def _():
            down.wait_recv()

        if tf > 1:
            late = jnp.concatenate([thalo[0], to_next[:n - plane]], axis=0)
            early = jnp.concatenate([to_prev[plane:], thalo[1]], axis=0)
        else:
            late, early = thalo[0], thalo[1]
        z = slope_of[...] + late + early
        th_ = jnp.tanh(GELU_ROOT * (z + GELU_CUBE * z * z * z))
        hid = (0.5 * z * (1.0 + th_)).astype(BF16)
        hsend[...] = jnp.dot(spread_of[...], hid, preferred_element_type=F32).reshape(
            nseq, he, chunk, mid).astype(BF16)

        def h_copy(o):
            s = lax.rem(seq + o, nseq)
            return remote(hsend.at[s], hraw.at[seq], h_s.at[0], h_r.at[0], dp, s)

        each(1, nseq, lambda o: h_copy(o).start())
        hraw[seq] = hsend[seq]
        slope_of[...] = 0.5 * (1.0 + th_) + 0.5 * z * (1.0 - th_ * th_) * GELU_ROOT * (
            1.0 + 3.0 * GELU_CUBE * z * z)

        for m in loads[7:]:
            m.wait()
        raw = [pixv[:, h].astype(F32).reshape(line, 4 * values) for h in range(hb)]
        px = jnp.concatenate(raw, axis=0)
        center = px - jnp.mean(px, axis=-1, keepdims=True)
        spread = jnp.mean(center * center, axis=-1, keepdims=True)
        normed = center * lax.rsqrt(spread + 1e-06)
        for ij in range(4):
            tgt[ij] = normed[:, ij * values:(ij + 1) * values] - b2[...].reshape(1, values)
        le = lax.broadcasted_iota(jnp.int32, (n, 1), 0)
        spot = lax.div(le, line) * cols + lax.rem(le, cols) + seq * (hb * cols)
        matches = (spot == marks[...]).astype(F32)
        scale = 2.0 / (4 * values) * jnp.sum(matches, axis=1, keepdims=True)

        step = 16 if mid % 16 == 0 else mid

        def sum_taps(o):
            a, r = lax.div(o, mid // step), lax.rem(o, mid // step)
            w = []
            for bc in range(9):
                part = w2[pl.ds(pl.multiple_of((a * 9 + bc) * mid + r * step, step), step)]
                w2b[bc // 3, pl.ds(pl.multiple_of(a * mid + r * step, step), step),
                    (bc % 3) * values:(bc % 3 + 1) * values] = part
                w.append(part.astype(F32))
            wide = []
            for b in range(3):
                x, y, z_ = w[b * 3:b * 3 + 3]
                wide.append((x, y + z_, x + y, z_))
            for i in range(2):
                for e in range(4):
                    x, y, z_ = wide[0][e], wide[1][e], wide[2][e]
                    for rh, v in enumerate((x, y + z_) if i == 0 else (x + y, z_)):
                        at = (a * 4 + rh * 2 + e % 2) * mid + r * step
                        weff[i * 2 + e // 2, pl.ds(pl.multiple_of(at, step), step)] = v.astype(BF16)

        each(0, 3 * (mid // step), sum_taps)

        def band(size):
            li = lax.broadcasted_iota(jnp.int32, (line, size), 0)
            lw = lax.rem(li, cols)
            return ((lw > 0).astype(F32), (lw < cols - 1).astype(F32),
                    (li >= cols).astype(F32), (li < line - cols).astype(F32))

        w_low, w_high, t_low, t_high = band(mid)
        p_low, p_high, _, _ = band(values)
        le = lax.broadcasted_iota(jnp.int32, (1, ext), 1)
        lw = lax.rem(le, cols)
        lt = lax.rem(le, line)
        s_low, s_high = (lt >= cols).astype(F32), (lt < line - cols).astype(F32)

        def shifted(v, by, mask):
            m = v.shape[0]
            rolled = pltpu.roll(v, (-by) % m, axis=0)
            return (rolled.reshape(m // line, line, v.shape[1]) * mask[None]).reshape(v.shape)

        drain(hraw.at[pl.ds(0, nseq - 1)], h_r.at[0])

        def xz_copy(o):
            s = lax.rem(seq + o, nseq)
            return remote(xbuf.at[s], xall.at[dp, seq], xz_s.at[0], xz_r.at[0], dp, s)

        each(1, nseq, lambda o: xz_copy(o).start())
        xall[dp, seq] = xbuf[seq]

        hin = hraw[...].astype(F32)
        hext = jnp.concatenate(
            [hin[:, hh].reshape(line, mid) for hh in range(he)], axis=0)
        for a in range(3):
            late = hext if a == 1 else shifted(
                hext, cols * (a - 1), t_low if a == 0 else t_high)
            for e in range(3):
                v = late if e == 1 else shifted(late, e - 1, w_low if e == 0 else w_high)
                vfield[a * 3 + e] = v.astype(BF16)
        hrow[dp, 0:hb * line] = hext[line:(hb + 1) * line].astype(BF16)
        hrow[dp, hb * line:(hb + 1) * line] = hext[0:line].astype(BF16)
        hrow[dp, (hb + 1) * line:ext] = hext[(hb + 1) * line:ext].astype(BF16)
        mine = hrow.at[dp, pl.ds(0, hb * line)]

        def ht_copy(o):
            d = peer(o)
            return remote(mine, mine, ht_s.at[0], ht_r.at[0], d, seq)

        each(1, ndp, lambda o: ht_copy(o).start())

        cots = []
        for ij in range(4):
            i, j = ij // 2, ij % 2
            near = []
            for k in range(12):
                low = (i + k // 2 % 2) * line
                near.append(vfield[k // 4 * 3 + j + k % 2, low:low + hb * line])
            predict = jnp.dot(jnp.concatenate(near, axis=1), weff[ij], preferred_element_type=F32)
            cot = (scale * (predict - tgt[ij])).astype(BF16).astype(F32)
            cots.append(cot)
            turned = cot.T
            for d in range(ndp):
                csend[d, ij] = turned[d * vblk:(d + 1) * vblk].astype(BF16)

        def c_copy(o):
            d = peer(o)
            return remote(csend.at[d], call_.at[dp], c_s.at[0], c_r.at[dp], d, seq)

        each(1, ndp, lambda o: c_copy(o).start())
        call_[dp] = csend[dp]

        def pair_sums(low, high, after, before):
            return (high + after(low), low + high, before(high) + low)

        def after_row(v):
            return shifted(v, 1, p_high)

        def before_row(v):
            return shifted(v, -1, p_low)

        for u, (low, high) in enumerate((
                (cots[0], cots[1]), (cots[2], cots[3]),
                (cots[0] + cots[2], cots[1] + cots[3]))):
            for c, s in enumerate(pair_sums(low, high, after_row, before_row)):
                cell[u * n:(u + 1) * n, c * values:(c + 1) * values] = s.astype(BF16)

        both = cell[0:2 * n]
        first = lax.dot_general(both, w2b[0], NT, preferred_element_type=F32)
        third = lax.dot_general(both, w2b[2], NT, preferred_element_type=F32)
        second = lax.dot_general(cell[2 * n:3 * n], w2b[1], NT, preferred_element_type=F32)
        same = first[n:] + second + third[:n]
        pieces = []
        for hh in range(he):
            total = None
            for v, dh in ((first[:n], -1), (same, 0), (third[n:], 1)):
                h = hh - 1 - dh
                if 0 <= h < hb:
                    part = v[h * line:(h + 1) * line]
                    total = part if total is None else total + part
            back = total[:, mid:2 * mid]
            back = back + shifted(total[:, :mid], cols, t_high)
            back = back + shifted(total[:, 2 * mid:], -cols, t_low)
            pieces.append(back)
        for hh in range(he):
            psend[:, hh] = pieces[hh].reshape(nseq, chunk, mid)

        def p_copy(o):
            s = lax.rem(seq + o, nseq)
            return remote(psend.at[s], praw.at[seq], p_s.at[0], p_r.at[0], dp, s)

        each(1, nseq, lambda o: p_copy(o).start())
        praw[seq] = psend[seq]

        drain(hrow.at[pl.ds(0, ndp - 1), pl.ds(0, hb * line)], ht_r.at[0])
        others = pl.ds(0, ndp - 1)

        def edge_copy(o, k):
            q = peer(o)
            if k == 0:
                return remote(hrow.at[q, pl.ds((hb - 1) * line, line)],
                              hrow.at[q, pl.ds(hb * line, line)], e_s.at[0], e_r.at[0], dp,
                              jnp.minimum(seq + 1, nseq - 1))
            return remote(hrow.at[q, pl.ds(0, line)],
                          hrow.at[q, pl.ds((hb + 1) * line, line)], e_s.at[1], e_r.at[1], dp,
                          jnp.maximum(seq - 1, 0))

        def no_edge(k):
            def put(o):
                q = peer(o)
                hrow[q, (hb + k) * line:(hb + k + 1) * line] = jnp.zeros((line, mid), BF16)
            each(1, ndp, put)

        @pl.when(seq < nseq - 1)
        def _():
            each(1, ndp, lambda o: edge_copy(o, 0).start())

        @pl.when(seq > 0)
        def _():
            each(1, ndp, lambda o: edge_copy(o, 1).start())

        @pl.when(seq == 0)
        def _():
            no_edge(0)

        @pl.when(seq == nseq - 1)
        def _():
            no_edge(1)

        lo = lax.broadcasted_iota(jnp.int32, (1, hb * line), 1)
        lw = lax.rem(lo, cols)
        e_low, e_high = (lw > 0).astype(F32), (lw < cols - 1).astype(F32)
        early_rows, late_rows = (lo < (hb - 1) * line).astype(F32), (lo >= line).astype(F32)

        def lane_after(v):
            return pltpu.roll(v, hb * line - 1, axis=1) * e_high

        def lane_before(v):
            return pltpu.roll(v, 1, axis=1) * e_low

        stack[3 * vblk:6 * vblk] = jnp.zeros((3 * vblk, ndp * ext), BF16)

        tile = hb * line

        def clip_stack(q, inner_at, outer_at):
            by_col, by_edge = [], []
            for j in range(2):
                low, high = call_[q, j].astype(F32), call_[q, 2 + j].astype(F32)
                by_col.append((high + pltpu.roll(low, (hb - 1) * line, axis=1) * early_rows,
                               low + high, low + pltpu.roll(high, line, axis=1) * late_rows))
                by_edge.append((low * early_rows, None, high * late_rows))
            at, rim = pl.ds(inner_at, tile), pl.ds(outer_at, 2 * line)
            k = 0
            for b in range(3):
                inner = pair_sums(by_col[0][b], by_col[1][b], lane_after, lane_before)
                outer = (None,) * 3 if b == 1 else pair_sums(
                    by_edge[0][b], by_edge[1][b], lane_after, lane_before)
                for s, r in zip(inner, outer):
                    stack[k * vblk:(k + 1) * vblk, at] = s.astype(BF16)
                    if r is not None:
                        stack[k * vblk:(k + 1) * vblk, rim] = r.astype(BF16)
                    k += 1

        clip_stack(dp, 0, (ndp - 1) * tile)

        def clip_lhs(o, low, high, at):
            size = high - low
            turned = hrow[peer(o), low:high].astype(F32).T
            for a in range(3):
                v = turned
                if a != 1:
                    v = pltpu.roll(turned, (cols if a == 0 else size - cols), axis=1)
                    v = v * (s_low if a == 0 else s_high)[:, low:high]
                lhs[:, a, :, at:at + size] = v.reshape(nseq, mblk, size).astype(BF16)

        for o in range(ndp):
            clip_lhs(o, 0, tile, (ndp if o == ndp - 1 else o) * tile)
        clip_lhs(0, tile, ext, (ndp - 1) * tile)

        def other_clip(o, inner_at):
            q = peer(o)
            drain(call_.at[q], c_r.at[q])
            clip_stack(q, inner_at, pl.multiple_of((ndp + o) * tile, 128))

        each(1, ndp - 1, lambda o: other_clip(o, pl.multiple_of(o * tile, 128)))

        def half(k, j, part):
            span = slice(part * ndp * tile, (part + 1) * ndp * tile)
            block = jnp.concatenate(
                [lhs[2 * s + k, :, :, span].reshape(3 * mblk, ndp * tile) for s in range(nz)],
                axis=0)
            low, size = cuts[j]
            return lax.dot_general(block, stack[low:low + size, span], NT,
                                   preferred_element_type=F32).reshape(nk, 2, 3 * mblk, size)

        for j in range(len(cuts)):
            acc3[j][...] = half(1 - core, j, 0)
            acc2[j][...] = half(core, j, 0)

        drain(praw.at[pl.ds(0, nseq - 1)], p_r.at[0])
        got = praw[...].reshape(nseq * he * chunk, mid)
        major = got.astype(BF16)
        minor = (got - major.astype(F32)).astype(BF16)
        grad_h = (jnp.dot(gather_of[...], major, preferred_element_type=F32)
                  + jnp.dot(gather_of[...], minor, preferred_element_type=F32))
        grad_z = (grad_h * slope_of[...]).astype(BF16).astype(F32).T
        for d in range(ndp):
            gsend[d] = grad_z[d * cblk:(d + 1) * cblk].astype(BF16)

        def g_copy(o):
            t = lax.rem(dp * nz + chip + o, ndp * nz)
            d = t // nz
            return remote(gsend.at[d], gall.at[dp, core, chip], g_s.at[0], g_r.at[dp], d,
                          2 * lax.rem(t, nz) + core)

        each(1, ndp * nz, lambda o: g_copy(o).start())
        gall[dp, core, chip] = gsend[dp]
        drain(xall.at[0, pl.ds(0, nseq - 1)], xz_r.at[0])

        def xd_copy(o):
            d = peer(o)
            return remote(xall.at[dp], xall.at[dp], xd_s.at[0], xd_r.at[dp], d, seq)

        each(1, ndp, lambda o: xd_copy(o).start())

        @pl.when(seq > 0)
        def _():
            drain(hrow.at[others, pl.ds(0, line)], e_r.at[0])

        @pl.when(seq < nseq - 1)
        def _():
            drain(hrow.at[others, pl.ds(0, line)], e_r.at[1])

        for o in range(1, ndp):
            clip_lhs(o, tile, ext, (ndp + o) * tile)
        other_clip(ndp - 1, ndp * tile)

        swaps = [remote(qs, qr, q_s.at[j], q_r.at[j], dp, 2 * chip + 1 - core)
                 for j, (qs, qr) in enumerate(zip(qsend, qrecv))]
        for j in range(len(cuts)):
            qsend[j][...] = (acc3[j][...] + half(1 - core, j, 1)).astype(BF16)
            swaps[j].start()
        par, kz = lax.rem(chip, 2), chip // 2

        def g_forward(q):
            return remote(gall.at[q, core], gall.at[q, core], f_s.at[0], f_r.at[q], dp,
                          2 * chip + 1 - core)

        def pass_on(o):
            q = peer(o)
            drain(gall.at[0, 0], g_r.at[q])
            g_forward(q).start()

        def forward_all():
            drain(gall.at[0, 0, pl.ds(0, nz - 1)], g_r.at[dp])
            g_forward(dp).start()
            each(1, ndp, pass_on)

        def near_copy(k):
            return remote(asend.at[k], arecv.at[k], a_s.at[0], a_r.at[0], dp,
                          2 * (chip + 1 - 2 * par) + core)

        def last_copy():
            return remote(asend.at[kz], arecv.at[kz], a_s.at[1], a_r.at[1],
                          dp, 2 * (chip + 1 - 2 * par) + core)

        def far_copy(o):
            k = lax.rem(kz + o, nk)
            return remote(bsend.at[k], brecv.at[kz], b_s.at[0], b_r.at[0], dp,
                          2 * (2 * k + par) + core)

        def r_copy(o):
            t = differ(chip, nz - o, nz)
            return remote(rsend.at[t // 2, lax.rem(t, 2)], rall.at[chip], r_s.at[0], r_r.at[0],
                          dp, 2 * t + core)

        for j in range(len(cuts)):
            acc2[j][...] = acc2[j][...] + half(core, j, 1)
            swaps[j].wait_recv()
            if j > 0:
                rsend[...] = (acc2[j][...] + qrecv[j][...].astype(F32)).astype(BF16)
                each(1, nz, lambda o: r_copy(o).start())
                acc2[j][kz, par] = acc2[j][kz, par] + qrecv[j][kz, par].astype(F32)
                continue
            asend[...] = (acc2[j][:, 1 - par] + qrecv[j][:, 1 - par].astype(F32)).astype(BF16)
            each(1, nk, lambda o: near_copy(lax.rem(kz + o, nk)).start())
            last_copy().start()
            acc2[j][:, par] = acc2[j][:, par] + qrecv[j][:, par].astype(F32)
        drain(asend.at[pl.ds(0, nk - 1)], a_r.at[0])

        def combine(o):
            k = lax.rem(kz + o, nk)
            bsend[k] = (acc2[0][k, par] + arecv[k].astype(F32)).astype(BF16)
            far_copy(o).start()

        each(1, nk, combine)
        forward_all()

        lx = lax.broadcasted_iota(jnp.int32, (1, clip_lanes), 1)
        x_low, x_high = (lx >= plane).astype(F32), (lx < clip_lanes - plane).astype(F32)

        def turn_clip(q):
            x = jnp.concatenate([xall[q, s] for s in range(nseq)], axis=1)
            xf = x.astype(F32)
            xs[q, 0:dblk] = (pltpu.roll(xf, plane, axis=1) * x_low).astype(BF16)
            xs[q, dblk:2 * dblk] = x
            xs[q, 2 * dblk:3 * dblk] = (
                pltpu.roll(xf, clip_lanes - plane, axis=1) * x_high).astype(BF16)


        lh = lax.rem(lx, rows)
        lc = lax.rem(lx, plane)
        g_h = ((lh < rows - 1).astype(F32), None, (lh > 0).astype(F32))
        g_w = ((lc < plane - rows).astype(F32), None, (lc >= rows).astype(F32))
        acc1[...] = jnp.zeros_like(acc1)

        def one_first(q):
            g = jnp.concatenate([gall[q, s % 2, s // 2].astype(F32) for s in range(nseq)], axis=1)
            grid = []
            for b in range(3):
                v = g if b == 1 else pltpu.roll(g, (b - 1) % clip_lanes, axis=1) * g_h[b]
                for c in range(3):
                    u = v if c == 1 else pltpu.roll(
                        v, ((c - 1) * rows) % clip_lanes, axis=1) * g_w[c]
                    grid.append(u.astype(BF16))
            acc1[...] += lax.dot_general(jnp.concatenate(grid, axis=0), xs[q], NT,
                                         preferred_element_type=F32)

        turn_clip(dp)
        drain(gall.at[0, 0], f_r.at[dp])
        one_first(dp)

        def arrived_first(o):
            q = peer(o)
            drain(xall.at[0], xd_r.at[q])
            turn_clip(q)
            drain(gall.at[0, 0], f_r.at[q])
            one_first(q)

        each(1, ndp, arrived_first)
        for a in range(3):
            o1[a * 9 * cblk:(a + 1) * 9 * cblk] = acc1[:, a * dblk:(a + 1) * dblk]

        @pl.when(seq < nseq - 1)
        def _():
            up.wait_send()

        @pl.when(seq > 0)
        def _():
            down.wait_send()

        drain(hsend.at[pl.ds(0, nseq - 1)], h_s.at[0])
        drain(xbuf.at[pl.ds(0, nseq - 1)], xz_s.at[0])
        drain(hrow.at[pl.ds(0, ndp - 1), pl.ds(0, hb * line)], ht_s.at[0])
        drain(csend.at[pl.ds(0, ndp - 1)], c_s.at[0])
        drain(psend.at[pl.ds(0, nseq - 1)], p_s.at[0])
        drain(xall.at[pl.ds(0, ndp - 1)], xd_s.at[0])
        for w in swaps:
            w.wait_send()
        for o in range(ndp):
            drain(gall.at[0, 0, pl.ds(0, nz - 1)] if o == 0 else gall.at[0, 0], g_s.at[0])
        drain(gall.at[:, 0], f_s.at[0])
        @pl.when(seq < nseq - 1)
        def _():
            drain(hrow.at[others, pl.ds(0, line)], e_s.at[0])

        @pl.when(seq > 0)
        def _():
            drain(hrow.at[others, pl.ds(0, line)], e_s.at[1])

        totals = []
        drain(asend.at[0], a_r.at[1])
        acc2[0][kz, par] = acc2[0][kz, par] + arecv[kz].astype(F32)
        drain(brecv.at[pl.ds(0, nk - 1)], b_r.at[0])

        def add(o):
            acc2[0][kz, par] = (acc2[0][kz, par]
                                     + brecv[lax.rem(kz + o, nk)].astype(F32))

        each(1, nk, add)
        totals.append(acc2[0][kz, par])
        if len(cuts) > 1:
            drain(rall.at[pl.ds(0, nz - 1)], r_r.at[0])
            total = acc2[1][kz, par]
            for o in range(1, nz):
                total = total + rall[differ(chip, o, nz)].astype(F32)
            totals.append(total)
        total = jnp.concatenate(totals, axis=1)
        for a in range(3):
            for bc in range(9):
                o2[a * 9 + bc] = total[a * mblk:(a + 1) * mblk, bc * vblk:(bc + 1) * vblk]
        if len(cuts) > 1:
            drain(rall.at[pl.ds(0, nz - 1)], r_s.at[0])
        drain(asend.at[pl.ds(0, nk - 1)], a_s.at[0])
        drain(asend.at[0], a_s.at[1])
        drain(brecv.at[pl.ds(0, nk - 1)], b_s.at[0])

    return kernel


def flush(a, b, oa, ob, sem):
    moves = (pltpu.make_async_copy(a, oa, sem.at[0]), pltpu.make_async_copy(b, ob, sem.at[1]))
    for m in moves:
        m.start()
    for m in moves:
        m.wait()


def per_device(tokens, conv_first, bias_first, conv_second, bias_second, pixels, mask_index):
    ndp, nseq = lax.axis_size("dp"), lax.axis_size("seq")
    tf, rows, cols, width = tokens.shape[1:]
    frames = tf * nseq
    mid, values = conv_second.shape[1], conv_second.shape[2]
    n = tf * rows * cols
    hb = rows // nseq
    he = hb + 2
    line = frames * cols
    ext = he * line
    chunk = tf * cols
    dims = (ndp, nseq, tf, rows, cols, width, mid, values)
    plane = rows * cols
    dblk, cblk, vblk, mblk = width // nseq, mid // ndp, values // ndp, mid // nseq
    nz = nseq // 2
    cuts = columns(9 * vblk)

    idx = np.arange(n, dtype=np.int32)
    t_of, w_of, h_of = idx // plane, idx // rows % cols, idx % rows
    flat_place = (h_of * cols + w_of)[:plane]
    tperm = jnp.asarray(flat_place[:, None] == idx[None, :plane], BF16)
    msg = np.arange(nseq * he * chunk, dtype=np.int32)
    m_s, m_h = msg // (he * chunk), msg // chunk % he
    m_t, m_w = msg % chunk // cols, msg % cols
    m_row = m_s * hb + m_h - 1
    same = ((m_row[:, None] == h_of[None]) & (m_t[:, None] == t_of[None])
            & (m_w[:, None] == w_of[None]))
    spread_of = jnp.asarray(same, BF16)
    gather_of = jnp.asarray(same.T, BF16)
    vm = pl.BlockSpec(memory_space=pltpu.VMEM)
    hbm = pl.BlockSpec(memory_space=pl.ANY)

    def dma(k):
        return pltpu.SemaphoreType.DMA((k,))

    scratch = [
        pltpu.VMEM((tf, rows, cols, width), BF16),
        pltpu.VMEM((1, mid), F32),
        pltpu.VMEM((values,), F32),
        pltpu.VMEM(mask_index.shape, jnp.int32),
        pltpu.VMEM((plane, plane), BF16),
        pltpu.VMEM((nseq * he * chunk, n), BF16),
        pltpu.VMEM((n, nseq * he * chunk), BF16),
        pltpu.VMEM((9 * width, 3 * mid), BF16),
        pltpu.VMEM((27 * mid, values), BF16),
        pltpu.VMEM((3, 3 * mid, 3 * values), BF16),
        pltpu.VMEM((4, 12 * mid, values), BF16),
        pltpu.VMEM((frames, hb, cols, 4 * values), BF16),
        pltpu.VMEM((nseq, dblk, n), BF16),
        pltpu.VMEM((ndp, nseq, dblk, n), BF16),
        pltpu.VMEM((ndp, 3 * dblk, nseq * n), BF16),
        pltpu.VMEM((2, plane, mid), F32),
        pltpu.VMEM((2, plane, mid), F32),
        pltpu.VMEM((3, tf, cols + 2, rows, width), BF16),
        pltpu.VMEM((n, 9 * width), BF16),
        pltpu.VMEM((n, mid), F32),
        pltpu.VMEM((nseq, he, chunk, mid), BF16),
        pltpu.VMEM((nseq, he, chunk, mid), BF16),
        pltpu.VMEM((9, ext, mid), BF16),
        pltpu.VMEM((4, n, values), F32),
        pltpu.VMEM((3 * n, 3 * values), BF16),
        pltpu.VMEM((nseq, he, chunk, mid), F32),
        pltpu.VMEM((nseq, he, chunk, mid), F32),
        pltpu.VMEM((ndp, ext, mid), BF16),
        pltpu.VMEM((nseq, 3, mblk, ndp * ext), BF16),
        pltpu.VMEM((ndp, 4, vblk, n), BF16),
        pltpu.VMEM((ndp, 4, vblk, n), BF16),
        pltpu.VMEM((9 * vblk, ndp * ext), BF16),
        pltpu.VMEM((ndp, cblk, n), BF16),
        pltpu.VMEM((ndp, 2, nz, cblk, n), BF16),
        pltpu.VMEM((9 * cblk, 3 * dblk), F32),
        pltpu.VMEM((nz // 2, 2, 3 * mblk, cuts[-1][1]), BF16),
        pltpu.VMEM((nz, 3 * mblk, cuts[-1][1]), BF16),
    ] + [pltpu.VMEM((nz // 2, 3 * mblk, cuts[0][1]), BF16)] * 4 + [
        [[pltpu.VMEM((nz // 2, 2, 3 * mblk, size), kind) for _, size in cuts]
         for kind in (BF16, BF16, F32, F32)],
        dma(14), dma(2), dma(2), dma(1), dma(1), dma(1), dma(1), dma(1), dma(1), dma(1), dma(ndp),
        dma(1), dma(1), dma(2), dma(2), dma(1), dma(ndp), dma(1), dma(ndp), dma(1), dma(ndp),
        dma(len(cuts)), dma(len(cuts)), dma(1), dma(1), dma(2), dma(2), dma(1), dma(1),
    ]
    first, second = pl.pallas_call(
        make_kernel(dims),
        out_shape=(pltpu.VMEM((27 * cblk, dblk), F32), pltpu.VMEM((27, mblk, vblk), F32)),
        in_specs=[hbm] * 10,
        out_specs=(vm, vm),
        scratch_shapes=scratch,
        compiler_params=pltpu.CompilerParams(
            collective_id=0, has_side_effects=True, vmem_limit_bytes=60 * 1024 * 1024),
        name="step",
    )(tokens[0], conv_first.reshape(27 * width, mid), bias_first.reshape(1, mid),
      conv_second.reshape(27 * mid, values), bias_second,
      pixels[0], mask_index, tperm, spread_of, gather_of)
    first, second = pl.pallas_call(
        flush,
        out_shape=(jax.ShapeDtypeStruct(first.shape, F32), jax.ShapeDtypeStruct(second.shape, F32)),
        in_specs=[vm, vm],
        out_specs=(hbm, hbm),
        scratch_shapes=[dma(2)],
        compiler_params=pltpu.CompilerParams(vmem_limit_bytes=4 * 1024 * 1024),
        name="flush",
    )(pltpu.with_memory_space_constraint(first, pltpu.VMEM),
      pltpu.with_memory_space_constraint(second, pltpu.VMEM))
    first = first.reshape(27, cblk, dblk).transpose(0, 2, 1)
    return (first, second)


def solution(mesh):
    return jax.shard_map(
        per_device,
        mesh=mesh,
        in_specs=(
            P("dp", "seq", None, None, None),
            P(),
            P(),
            P(),
            P(),
            P("dp", None, "seq", None, None),
            P("dp", None),
        ),
        out_specs=(P(None, "seq", "dp"), P(None, "seq", "dp")),
        check_vma=False,
    )
```

```python
import jax
import jax.numpy as jnp
import numpy as np
from jax import lax
from jax.experimental import pallas as pl
from jax.experimental.pallas import tpu as pltpu
from jax.sharding import PartitionSpec as P

F32 = jnp.float32
BF16 = jnp.bfloat16
NT = (((1,), (1,)), ((), ()))
GELU_ROOT = 0.7978845608028654
GELU_CUBE = 0.044715


def floor_half(v):
    return v // 2 if v >= 0 else -1


def columns(total):
    half = -(-total // 512) * 256
    return [(0, half), (half, total - half)] if total > half else [(0, total)]


def make_kernel(dims):
    ndp, nseq, tf, rows, cols, width, mid, values = dims
    n = tf * cols * rows
    plane = cols * rows
    frames = tf * nseq
    hb = rows // nseq
    he = hb + 2
    line = frames * cols
    ext = he * line
    chunk = tf * cols
    dblk = width // nseq
    cblk = mid // ndp
    vblk = values // ndp
    mblk = mid // nseq
    ndev = ndp * nseq
    nz = nseq // 2
    clip_lanes = nseq * n
    nk = nz // 2
    cuts = columns(9 * vblk)

    def kernel(tok_hbm, w1_hbm, b1_hbm, w2_hbm, b2_hbm, pix_hbm, marks_hbm, tperm_hbm, spread_hbm,
               gather_hbm, o1, o2,
               tok, b1, b2, marks, tperm, spread_of, gather_of,
               w1, w2, w2b, weff, pixv, xbuf, xall, xs, tsend, thalo, tfield, im1, slope_of,
               hsend, hraw, vfield, tgt, cell, psend, praw,
               hrow, lhs, csend, call_, stack, gsend, gall, acc1, rsend, rall, asend, arecv, bsend, brecv,
               chunks,
               wsem, th_s, th_r, h_s, h_r, p_r, xz_r, xd_r, ht_r, e_r,
               c_r, g_r, f_r, q_r, r_r, a_r, b_r):
        dp = lax.axis_index("dp")
        seq = lax.axis_index("seq")
        me = dp * nseq + seq
        chip, core = seq // 2, lax.rem(seq, 2)
        p_s, xz_s, xd_s, ht_s, c_s, g_s, f_s, r_s, b_s = [
            wsem.at[pl.ds(k, 1)] for k in range(9)]
        e_s, q_s, a_s = [wsem.at[pl.ds(k, 2)] for k in (9, 11, 13)]
        qsend, qrecv, acc2, acc3 = chunks

        def remote(src, dst, ss, rs, d, s):
            return pltpu.make_async_remote_copy(
                src_ref=src, dst_ref=dst, send_sem=ss, recv_sem=rs,
                device_id=(d, s), device_id_type=pl.DeviceIdType.MESH)

        def drain(ref, sem):
            pltpu.make_async_copy(ref, ref, sem).wait()

        def each(low, count, act):
            def body(o, c):
                act(o)
                return c
            lax.fori_loop(low, count, body, 0)

        def differ(at, o, size):
            d, bit = 0, 1
            while bit < size:
                mine_, other = lax.rem(at // bit, 2), (o // bit) % 2
                d = d + bit * (mine_ + other - 2 * mine_ * other)
                bit = bit * 2
            return d

        def peer(o):
            return differ(dp, o, ndp)

        barrier = pltpu.get_barrier_semaphore()

        def greet(o):
            s, d = lax.div(o, ndp), lax.rem(o, ndp)

            @pl.when(jnp.logical_or(s != seq, d != dp))
            def _():
                pl.semaphore_signal(barrier, inc=1, device_id=(d, s),
                                    device_id_type=pl.DeviceIdType.MESH)

        loads = [pltpu.make_async_copy(src, dst, wsem.at[k]) for k, (src, dst) in enumerate((
            (tok_hbm, tok), (tperm_hbm, tperm), (b1_hbm, b1), (b2_hbm, b2), (marks_hbm, marks),
            (spread_hbm, spread_of), (gather_hbm, gather_of), (pix_hbm, pixv), (w2_hbm, w2)))]
        loads[0].start()
        loads[1].start()
        def w1_part(b, a, at):
            rows_ = 3 * width
            return pltpu.make_async_copy(
                w1_hbm.at[pl.ds((a * 9 + b * 3) * width, rows_)],
                w1.at[pl.ds(b * rows_, rows_), pl.ds(at * mid, mid)],
                wsem.at[13 if at == 2 else 9 + b])

        for b in range(3):
            w1_part(b, 0, 0).start()
            w1_part(b, 2, 1).start()
        for b in range(3):
            w1_part(b, 1, 2).start()
        each(0, ndev, greet)
        for m in loads[2:]:
            m.start()
        def ordered(frame):
            raw = frame.astype(F32).reshape(plane, width).astype(BF16)
            return jnp.dot(tperm[...], raw, preferred_element_type=F32)

        loads[0].wait()
        loads[1].wait()
        flat = jnp.concatenate([ordered(tok[t]) for t in range(tf)], axis=0)
        lr = lax.broadcasted_iota(jnp.int32, (rows, width), 0)
        edge = ((lr > 0).astype(F32), None, (lr < rows - 1).astype(F32))
        zero = jnp.zeros((3, tf, 1, rows, width), BF16)
        tfield[:, :, 0:1] = zero
        tfield[:, :, cols + 1:cols + 2] = zero
        for b in range(3):
            v = flat.reshape(tf, cols, rows, width)
            if b != 1:
                v = pltpu.roll(flat, 1 if b == 0 else n - 1, axis=0).reshape(
                    tf * cols, rows, width) * edge[b][None]
            tfield[b, :, 1:cols + 1] = v.reshape(tf, cols, rows, width).astype(BF16)
        for bc in range(9):
            im1[:, bc * width:(bc + 1) * width] = (
                tfield[bc // 3, :, bc % 3:bc % 3 + cols].reshape(n, width))
        parts = None
        for b in range(3):
            span = slice(b * 3 * width, (b + 1) * 3 * width)
            drain(w1.at[pl.ds(b * 3 * width, 3 * width), pl.ds(0, 2 * mid)], wsem.at[9 + b])
            part = jnp.dot(im1[:, span], w1[span, 0:2 * mid], preferred_element_type=F32)
            parts = part if parts is None else parts + part
        to_next, to_prev = parts[:, :mid], parts[:, mid:]
        tsend[0] = to_next[n - plane:]
        tsend[1] = to_prev[:plane]
        pl.semaphore_wait(barrier, ndev - 1)

        up = remote(tsend.at[0], thalo.at[0], th_s.at[0], th_r.at[0], dp,
                    jnp.minimum(seq + 1, nseq - 1))
        down = remote(tsend.at[1], thalo.at[1], th_s.at[1], th_r.at[1], dp,
                      jnp.maximum(seq - 1, 0))

        @pl.when(seq < nseq - 1)
        def _():
            up.start()

        @pl.when(seq > 0)
        def _():
            down.start()

        @pl.when(seq == 0)
        def _():
            thalo[0] = jnp.zeros((plane, mid), F32)

        @pl.when(seq == nseq - 1)
        def _():
            thalo[1] = jnp.zeros((plane, mid), F32)

        for m in loads[2:7]:
            m.wait()
        drain(w1.at[:, pl.ds(2 * mid, mid)], wsem.at[13])
        slope_of[...] = jnp.dot(im1[...], w1[:, 2 * mid:3 * mid],
                                preferred_element_type=F32) + b1[...]
        xt = flat.T
        for s in range(nseq):
            xbuf[s] = xt[s * dblk:(s + 1) * dblk].astype(BF16)

        @pl.when(seq > 0)
        def _():
            up.wait_recv()

        @pl.when(seq < nseq - 1)
        def _():
            down.wait_recv()

        if tf > 1:
            late = jnp.concatenate([thalo[0], to_next[:n - plane]], axis=0)
            early = jnp.concatenate([to_prev[plane:], thalo[1]], axis=0)
        else:
            late, early = thalo[0], thalo[1]
        z = slope_of[...] + late + early
        th_ = jnp.tanh(GELU_ROOT * (z + GELU_CUBE * z * z * z))
        hid = (0.5 * z * (1.0 + th_)).astype(BF16)
        hsend[...] = jnp.dot(spread_of[...], hid, preferred_element_type=F32).reshape(
            nseq, he, chunk, mid).astype(BF16)

        def h_copy(o):
            s = lax.rem(seq + o, nseq)
            return remote(hsend.at[s], hraw.at[seq], h_s.at[0], h_r.at[0], dp, s)

        each(1, nseq, lambda o: h_copy(o).start())
        hraw[seq] = hsend[seq]
        slope_of[...] = 0.5 * (1.0 + th_) + 0.5 * z * (1.0 - th_ * th_) * GELU_ROOT * (
            1.0 + 3.0 * GELU_CUBE * z * z)

        for m in loads[7:]:
            m.wait()
        raw = [pixv[:, h].astype(F32).reshape(line, 4 * values) for h in range(hb)]
        px = jnp.concatenate(raw, axis=0)
        center = px - jnp.mean(px, axis=-1, keepdims=True)
        spread = jnp.mean(center * center, axis=-1, keepdims=True)
        normed = center * lax.rsqrt(spread + 1e-06)
        for ij in range(4):
            tgt[ij] = normed[:, ij * values:(ij + 1) * values] - b2[...].reshape(1, values)
        le = lax.broadcasted_iota(jnp.int32, (n, 1), 0)
        spot = lax.div(le, line) * cols + lax.rem(le, cols) + seq * (hb * cols)
        matches = (spot == marks[...]).astype(F32)
        scale = 2.0 / (4 * values) * jnp.sum(matches, axis=1, keepdims=True)

        step = 16 if mid % 16 == 0 else mid

        def sum_taps(o):
            a, r = lax.div(o, mid // step), lax.rem(o, mid // step)
            w = []
            for bc in range(9):
                part = w2[pl.ds(pl.multiple_of((a * 9 + bc) * mid + r * step, step), step)]
                w2b[bc // 3, pl.ds(pl.multiple_of(a * mid + r * step, step), step),
                    (bc % 3) * values:(bc % 3 + 1) * values] = part
                w.append(part.astype(F32))
            wide = []
            for b in range(3):
                x, y, z_ = w[b * 3:b * 3 + 3]
                wide.append((x, y + z_, x + y, z_))
            for i in range(2):
                for e in range(4):
                    x, y, z_ = wide[0][e], wide[1][e], wide[2][e]
                    for rh, v in enumerate((x, y + z_) if i == 0 else (x + y, z_)):
                        at = (a * 4 + rh * 2 + e % 2) * mid + r * step
                        weff[i * 2 + e // 2, pl.ds(pl.multiple_of(at, step), step)] = v.astype(BF16)

        each(0, 3 * (mid // step), sum_taps)

        def band(size):
            li = lax.broadcasted_iota(jnp.int32, (line, size), 0)
            lw = lax.rem(li, cols)
            return ((lw > 0).astype(F32), (lw < cols - 1).astype(F32),
                    (li >= cols).astype(F32), (li < line - cols).astype(F32))

        w_low, w_high, t_low, t_high = band(mid)
        p_low, p_high, _, _ = band(values)
        le = lax.broadcasted_iota(jnp.int32, (1, ext), 1)
        lw = lax.rem(le, cols)
        lt = lax.rem(le, line)
        s_low, s_high = (lt >= cols).astype(F32), (lt < line - cols).astype(F32)

        def shifted(v, by, mask):
            m = v.shape[0]
            rolled = pltpu.roll(v, (-by) % m, axis=0)
            return (rolled.reshape(m // line, line, v.shape[1]) * mask[None]).reshape(v.shape)

        drain(hraw.at[pl.ds(0, nseq - 1)], h_r.at[0])

        def xz_copy(o):
            s = lax.rem(seq + o, nseq)
            return remote(xbuf.at[s], xall.at[dp, seq], xz_s.at[0], xz_r.at[0], dp, s)

        each(1, nseq, lambda o: xz_copy(o).start())
        xall[dp, seq] = xbuf[seq]

        hin = hraw[...].astype(F32)
        hext = jnp.concatenate(
            [hin[:, hh].reshape(line, mid) for hh in range(he)], axis=0)
        for a in range(3):
            late = hext if a == 1 else shifted(
                hext, cols * (a - 1), t_low if a == 0 else t_high)
            for e in range(3):
                v = late if e == 1 else shifted(late, e - 1, w_low if e == 0 else w_high)
                vfield[a * 3 + e] = v.astype(BF16)
        hrow[dp, 0:hb * line] = hext[line:(hb + 1) * line].astype(BF16)
        hrow[dp, hb * line:(hb + 1) * line] = hext[0:line].astype(BF16)
        hrow[dp, (hb + 1) * line:ext] = hext[(hb + 1) * line:ext].astype(BF16)
        mine = hrow.at[dp, pl.ds(0, hb * line)]

        def ht_copy(o):
            d = peer(o)
            return remote(mine, mine, ht_s.at[0], ht_r.at[0], d, seq)

        each(1, ndp, lambda o: ht_copy(o).start())

        cots = []
        for ij in range(4):
            i, j = ij // 2, ij % 2
            near = []
            for k in range(12):
                low = (i + k // 2 % 2) * line
                near.append(vfield[k // 4 * 3 + j + k % 2, low:low + hb * line])
            predict = jnp.dot(jnp.concatenate(near, axis=1), weff[ij], preferred_element_type=F32)
            cot = (scale * (predict - tgt[ij])).astype(BF16).astype(F32)
            cots.append(cot)
            turned = cot.T
            for d in range(ndp):
                csend[d, ij] = turned[d * vblk:(d + 1) * vblk].astype(BF16)

        def c_copy(o):
            d = peer(o)
            return remote(csend.at[d], call_.at[dp], c_s.at[0], c_r.at[dp], d, seq)

        each(1, ndp, lambda o: c_copy(o).start())
        call_[dp] = csend[dp]

        def pair_sums(low, high, after, before):
            return (high + after(low), low + high, before(high) + low)

        def after_row(v):
            return shifted(v, 1, p_high)

        def before_row(v):
            return shifted(v, -1, p_low)

        for u, (low, high) in enumerate((
                (cots[0], cots[1]), (cots[2], cots[3]),
                (cots[0] + cots[2], cots[1] + cots[3]))):
            for c, s in enumerate(pair_sums(low, high, after_row, before_row)):
                cell[u * n:(u + 1) * n, c * values:(c + 1) * values] = s.astype(BF16)

        both = cell[0:2 * n]
        first = lax.dot_general(both, w2b[0], NT, preferred_element_type=F32)
        third = lax.dot_general(both, w2b[2], NT, preferred_element_type=F32)
        second = lax.dot_general(cell[2 * n:3 * n], w2b[1], NT, preferred_element_type=F32)
        same = first[n:] + second + third[:n]
        pieces = []
        for hh in range(he):
            total = None
            for v, dh in ((first[:n], -1), (same, 0), (third[n:], 1)):
                h = hh - 1 - dh
                if 0 <= h < hb:
                    part = v[h * line:(h + 1) * line]
                    total = part if total is None else total + part
            back = total[:, mid:2 * mid]
            back = back + shifted(total[:, :mid], cols, t_high)
            back = back + shifted(total[:, 2 * mid:], -cols, t_low)
            pieces.append(back)
        for hh in range(he):
            psend[:, hh] = pieces[hh].reshape(nseq, chunk, mid)

        def p_copy(o):
            s = lax.rem(seq + o, nseq)
            return remote(psend.at[s], praw.at[seq], p_s.at[0], p_r.at[0], dp, s)

        each(1, nseq, lambda o: p_copy(o).start())
        praw[seq] = psend[seq]

        drain(hrow.at[pl.ds(0, ndp - 1), pl.ds(0, hb * line)], ht_r.at[0])
        others = pl.ds(0, ndp - 1)

        def edge_copy(o, k):
            q = peer(o)
            if k == 0:
                return remote(hrow.at[q, pl.ds((hb - 1) * line, line)],
                              hrow.at[q, pl.ds(hb * line, line)], e_s.at[0], e_r.at[0], dp,
                              jnp.minimum(seq + 1, nseq - 1))
            return remote(hrow.at[q, pl.ds(0, line)],
                          hrow.at[q, pl.ds((hb + 1) * line, line)], e_s.at[1], e_r.at[1], dp,
                          jnp.maximum(seq - 1, 0))

        def no_edge(k):
            def put(o):
                q = peer(o)
                hrow[q, (hb + k) * line:(hb + k + 1) * line] = jnp.zeros((line, mid), BF16)
            each(1, ndp, put)

        @pl.when(seq < nseq - 1)
        def _():
            each(1, ndp, lambda o: edge_copy(o, 0).start())

        @pl.when(seq > 0)
        def _():
            each(1, ndp, lambda o: edge_copy(o, 1).start())

        @pl.when(seq == 0)
        def _():
            no_edge(0)

        @pl.when(seq == nseq - 1)
        def _():
            no_edge(1)

        lo = lax.broadcasted_iota(jnp.int32, (1, hb * line), 1)
        lw = lax.rem(lo, cols)
        e_low, e_high = (lw > 0).astype(F32), (lw < cols - 1).astype(F32)
        early_rows, late_rows = (lo < (hb - 1) * line).astype(F32), (lo >= line).astype(F32)

        def lane_after(v):
            return pltpu.roll(v, hb * line - 1, axis=1) * e_high

        def lane_before(v):
            return pltpu.roll(v, 1, axis=1) * e_low

        stack[3 * vblk:6 * vblk] = jnp.zeros((3 * vblk, ndp * ext), BF16)

        tile = hb * line

        def clip_stack(q, inner_at, outer_at):
            by_col, by_edge = [], []
            for j in range(2):
                low, high = call_[q, j].astype(F32), call_[q, 2 + j].astype(F32)
                by_col.append((high + pltpu.roll(low, (hb - 1) * line, axis=1) * early_rows,
                               low + high, low + pltpu.roll(high, line, axis=1) * late_rows))
                by_edge.append((low * early_rows, None, high * late_rows))
            at, rim = pl.ds(inner_at, tile), pl.ds(outer_at, 2 * line)
            k = 0
            for b in range(3):
                inner = pair_sums(by_col[0][b], by_col[1][b], lane_after, lane_before)
                outer = (None,) * 3 if b == 1 else pair_sums(
                    by_edge[0][b], by_edge[1][b], lane_after, lane_before)
                for s, r in zip(inner, outer):
                    stack[k * vblk:(k + 1) * vblk, at] = s.astype(BF16)
                    if r is not None:
                        stack[k * vblk:(k + 1) * vblk, rim] = r.astype(BF16)
                    k += 1

        clip_stack(dp, 0, (ndp - 1) * tile)

        def clip_lhs(o, low, high, at):
            size = high - low
            turned = hrow[peer(o), low:high].astype(F32).T
            for a in range(3):
                v = turned
                if a != 1:
                    v = pltpu.roll(turned, (cols if a == 0 else size - cols), axis=1)
                    v = v * (s_low if a == 0 else s_high)[:, low:high]
                lhs[:, a, :, at:at + size] = v.reshape(nseq, mblk, size).astype(BF16)

        for o in range(ndp):
            clip_lhs(o, 0, tile, (ndp if o == ndp - 1 else o) * tile)
        clip_lhs(0, tile, ext, (ndp - 1) * tile)

        def other_clip(o, inner_at):
            q = peer(o)
            drain(call_.at[q], c_r.at[q])
            clip_stack(q, inner_at, pl.multiple_of((ndp + o) * tile, 128))

        each(1, ndp - 1, lambda o: other_clip(o, pl.multiple_of(o * tile, 128)))

        def half(k, j, part):
            span = slice(part * ndp * tile, (part + 1) * ndp * tile)
            block = jnp.concatenate(
                [lhs[2 * s + k, :, :, span].reshape(3 * mblk, ndp * tile) for s in range(nz)],
                axis=0)
            low, size = cuts[j]
            return lax.dot_general(block, stack[low:low + size, span], NT,
                                   preferred_element_type=F32).reshape(nk, 2, 3 * mblk, size)

        for j in range(len(cuts)):
            acc3[j][...] = half(1 - core, j, 0)
            acc2[j][...] = half(core, j, 0)

        drain(praw.at[pl.ds(0, nseq - 1)], p_r.at[0])
        got = praw[...].reshape(nseq * he * chunk, mid)
        major = got.astype(BF16)
        minor = (got - major.astype(F32)).astype(BF16)
        grad_h = (jnp.dot(gather_of[...], major, preferred_element_type=F32)
                  + jnp.dot(gather_of[...], minor, preferred_element_type=F32))
        grad_z = (grad_h * slope_of[...]).astype(BF16).astype(F32).T
        for d in range(ndp):
            gsend[d] = grad_z[d * cblk:(d + 1) * cblk].astype(BF16)

        def g_copy(o):
            t = lax.rem(dp * nz + chip + o, ndp * nz)
            d = t // nz
            return remote(gsend.at[d], gall.at[dp, core, chip], g_s.at[0], g_r.at[dp], d,
                          2 * lax.rem(t, nz) + core)

        each(1, ndp * nz, lambda o: g_copy(o).start())
        gall[dp, core, chip] = gsend[dp]
        drain(xall.at[0, pl.ds(0, nseq - 1)], xz_r.at[0])

        def xd_copy(o):
            d = peer(o)
            return remote(xall.at[dp], xall.at[dp], xd_s.at[0], xd_r.at[dp], d, seq)

        each(1, ndp, lambda o: xd_copy(o).start())

        @pl.when(seq > 0)
        def _():
            drain(hrow.at[others, pl.ds(0, line)], e_r.at[0])

        @pl.when(seq < nseq - 1)
        def _():
            drain(hrow.at[others, pl.ds(0, line)], e_r.at[1])

        for o in range(1, ndp):
            clip_lhs(o, tile, ext, (ndp + o) * tile)
        other_clip(ndp - 1, ndp * tile)

        swaps = [remote(qs, qr, q_s.at[j], q_r.at[j], dp, 2 * chip + 1 - core)
                 for j, (qs, qr) in enumerate(zip(qsend, qrecv))]
        for j in range(len(cuts)):
            qsend[j][...] = (acc3[j][...] + half(1 - core, j, 1)).astype(BF16)
            swaps[j].start()
        par, kz = lax.rem(chip, 2), chip // 2

        def g_forward(q):
            return remote(gall.at[q, core], gall.at[q, core], f_s.at[0], f_r.at[q], dp,
                          2 * chip + 1 - core)

        def pass_on(o):
            q = peer(o)
            drain(gall.at[0, 0], g_r.at[q])
            g_forward(q).start()

        def forward_all():
            drain(gall.at[0, 0, pl.ds(0, nz - 1)], g_r.at[dp])
            g_forward(dp).start()
            each(1, ndp, pass_on)

        def near_copy(k):
            return remote(asend.at[k], arecv.at[k], a_s.at[0], a_r.at[0], dp,
                          2 * (chip + 1 - 2 * par) + core)

        def last_copy():
            return remote(asend.at[kz], arecv.at[kz], a_s.at[1], a_r.at[1],
                          dp, 2 * (chip + 1 - 2 * par) + core)

        def far_copy(o):
            k = lax.rem(kz + o, nk)
            return remote(bsend.at[k], brecv.at[kz], b_s.at[0], b_r.at[0], dp,
                          2 * (2 * k + par) + core)

        def r_copy(o):
            t = differ(chip, nz - o, nz)
            return remote(rsend.at[t // 2, lax.rem(t, 2)], rall.at[chip], r_s.at[0], r_r.at[0],
                          dp, 2 * t + core)

        for j in range(len(cuts)):
            acc2[j][...] = acc2[j][...] + half(core, j, 1)
            swaps[j].wait_recv()
            if j > 0:
                rsend[...] = (acc2[j][...] + qrecv[j][...].astype(F32)).astype(BF16)
                each(1, nz, lambda o: r_copy(o).start())
                acc2[j][kz, par] = acc2[j][kz, par] + qrecv[j][kz, par].astype(F32)
                continue
            asend[...] = (acc2[j][:, 1 - par] + qrecv[j][:, 1 - par].astype(F32)).astype(BF16)
            each(1, nk, lambda o: near_copy(lax.rem(kz + o, nk)).start())
            acc2[j][:, par] = acc2[j][:, par] + qrecv[j][:, par].astype(F32)
        lx = lax.broadcasted_iota(jnp.int32, (1, clip_lanes), 1)
        x_low, x_high = (lx >= plane).astype(F32), (lx < clip_lanes - plane).astype(F32)

        def turn_clip(q):
            x = jnp.concatenate([xall[q, s] for s in range(nseq)], axis=1)
            xf = x.astype(F32)
            xs[q, 0:dblk] = (pltpu.roll(xf, plane, axis=1) * x_low).astype(BF16)
            xs[q, dblk:2 * dblk] = x
            xs[q, 2 * dblk:3 * dblk] = (
                pltpu.roll(xf, clip_lanes - plane, axis=1) * x_high).astype(BF16)

        turn_clip(dp)
        acc1[...] = jnp.zeros_like(acc1)
        forward_all()
        drain(asend.at[pl.ds(0, nk - 1)], a_r.at[0])

        def combine(o):
            k = lax.rem(kz + o, nk)
            bsend[k] = (acc2[0][k, par] + arecv[k].astype(F32)).astype(BF16)
            far_copy(o).start()

        each(1, nk, combine)
        last_copy().start()

        lh = lax.rem(lx, rows)
        lc = lax.rem(lx, plane)
        g_h = ((lh < rows - 1).astype(F32), None, (lh > 0).astype(F32))
        g_w = ((lc < plane - rows).astype(F32), None, (lc >= rows).astype(F32))

        def one_first(q):
            g = jnp.concatenate([gall[q, s % 2, s // 2].astype(F32) for s in range(nseq)], axis=1)
            grid = []
            for b in range(3):
                v = g if b == 1 else pltpu.roll(g, (b - 1) % clip_lanes, axis=1) * g_h[b]
                for c in range(3):
                    u = v if c == 1 else pltpu.roll(
                        v, ((c - 1) * rows) % clip_lanes, axis=1) * g_w[c]
                    grid.append(u.astype(BF16))
            acc1[...] += lax.dot_general(jnp.concatenate(grid, axis=0), xs[q], NT,
                                         preferred_element_type=F32)

        drain(gall.at[0, 0], f_r.at[dp])
        one_first(dp)

        def arrived_first(o):
            q = peer(o)
            drain(xall.at[0], xd_r.at[q])
            turn_clip(q)
            drain(gall.at[0, 0], f_r.at[q])
            one_first(q)

        each(1, ndp, arrived_first)
        for a in range(3):
            o1[a * 9 * cblk:(a + 1) * 9 * cblk] = acc1[:, a * dblk:(a + 1) * dblk]

        @pl.when(seq < nseq - 1)
        def _():
            up.wait_send()

        @pl.when(seq > 0)
        def _():
            down.wait_send()

        drain(hsend.at[pl.ds(0, nseq - 1)], h_s.at[0])
        drain(xbuf.at[pl.ds(0, nseq - 1)], xz_s.at[0])
        drain(hrow.at[pl.ds(0, ndp - 1), pl.ds(0, hb * line)], ht_s.at[0])
        drain(csend.at[pl.ds(0, ndp - 1)], c_s.at[0])
        drain(psend.at[pl.ds(0, nseq - 1)], p_s.at[0])
        drain(xall.at[pl.ds(0, ndp - 1)], xd_s.at[0])
        for w in swaps:
            w.wait_send()
        for o in range(ndp):
            drain(gall.at[0, 0, pl.ds(0, nz - 1)] if o == 0 else gall.at[0, 0], g_s.at[0])
        drain(gall.at[:, 0], f_s.at[0])
        @pl.when(seq < nseq - 1)
        def _():
            drain(hrow.at[others, pl.ds(0, line)], e_s.at[0])

        @pl.when(seq > 0)
        def _():
            drain(hrow.at[others, pl.ds(0, line)], e_s.at[1])

        totals = []
        drain(asend.at[0], a_r.at[1])
        acc2[0][kz, par] = acc2[0][kz, par] + arecv[kz].astype(F32)
        drain(brecv.at[pl.ds(0, nk - 1)], b_r.at[0])

        def add(o):
            acc2[0][kz, par] = (acc2[0][kz, par]
                                     + brecv[lax.rem(kz + o, nk)].astype(F32))

        each(1, nk, add)
        totals.append(acc2[0][kz, par])
        if len(cuts) > 1:
            drain(rall.at[pl.ds(0, nz - 1)], r_r.at[0])
            total = acc2[1][kz, par]
            for o in range(1, nz):
                total = total + rall[differ(chip, o, nz)].astype(F32)
            totals.append(total)
        total = jnp.concatenate(totals, axis=1)
        for a in range(3):
            for bc in range(9):
                o2[a * 9 + bc] = total[a * mblk:(a + 1) * mblk, bc * vblk:(bc + 1) * vblk]
        if len(cuts) > 1:
            drain(rall.at[pl.ds(0, nz - 1)], r_s.at[0])
        drain(asend.at[pl.ds(0, nk - 1)], a_s.at[0])
        drain(asend.at[0], a_s.at[1])
        drain(brecv.at[pl.ds(0, nk - 1)], b_s.at[0])

    return kernel


def flush(a, b, oa, ob, sem):
    moves = (pltpu.make_async_copy(a, oa, sem.at[0]), pltpu.make_async_copy(b, ob, sem.at[1]))
    for m in moves:
        m.start()
    for m in moves:
        m.wait()


def per_device(tokens, conv_first, bias_first, conv_second, bias_second, pixels, mask_index):
    ndp, nseq = lax.axis_size("dp"), lax.axis_size("seq")
    tf, rows, cols, width = tokens.shape[1:]
    frames = tf * nseq
    mid, values = conv_second.shape[1], conv_second.shape[2]
    n = tf * rows * cols
    hb = rows // nseq
    he = hb + 2
    line = frames * cols
    ext = he * line
    chunk = tf * cols
    dims = (ndp, nseq, tf, rows, cols, width, mid, values)
    plane = rows * cols
    dblk, cblk, vblk, mblk = width // nseq, mid // ndp, values // ndp, mid // nseq
    nz = nseq // 2
    cuts = columns(9 * vblk)

    idx = np.arange(n, dtype=np.int32)
    t_of, w_of, h_of = idx // plane, idx // rows % cols, idx % rows
    flat_place = (h_of * cols + w_of)[:plane]
    tperm = jnp.asarray(flat_place[:, None] == idx[None, :plane], BF16)
    msg = np.arange(nseq * he * chunk, dtype=np.int32)
    m_s, m_h = msg // (he * chunk), msg // chunk % he
    m_t, m_w = msg % chunk // cols, msg % cols
    m_row = m_s * hb + m_h - 1
    same = ((m_row[:, None] == h_of[None]) & (m_t[:, None] == t_of[None])
            & (m_w[:, None] == w_of[None]))
    spread_of = jnp.asarray(same, BF16)
    gather_of = jnp.asarray(same.T, BF16)
    vm = pl.BlockSpec(memory_space=pltpu.VMEM)
    hbm = pl.BlockSpec(memory_space=pl.ANY)

    def dma(k):
        return pltpu.SemaphoreType.DMA((k,))

    scratch = [
        pltpu.VMEM((tf, rows, cols, width), BF16),
        pltpu.VMEM((1, mid), F32),
        pltpu.VMEM((values,), F32),
        pltpu.VMEM(mask_index.shape, jnp.int32),
        pltpu.VMEM((plane, plane), BF16),
        pltpu.VMEM((nseq * he * chunk, n), BF16),
        pltpu.VMEM((n, nseq * he * chunk), BF16),
        pltpu.VMEM((9 * width, 3 * mid), BF16),
        pltpu.VMEM((27 * mid, values), BF16),
        pltpu.VMEM((3, 3 * mid, 3 * values), BF16),
        pltpu.VMEM((4, 12 * mid, values), BF16),
        pltpu.VMEM((frames, hb, cols, 4 * values), BF16),
        pltpu.VMEM((nseq, dblk, n), BF16),
        pltpu.VMEM((ndp, nseq, dblk, n), BF16),
        pltpu.VMEM((ndp, 3 * dblk, nseq * n), BF16),
        pltpu.VMEM((2, plane, mid), F32),
        pltpu.VMEM((2, plane, mid), F32),
        pltpu.VMEM((3, tf, cols + 2, rows, width), BF16),
        pltpu.VMEM((n, 9 * width), BF16),
        pltpu.VMEM((n, mid), F32),
        pltpu.VMEM((nseq, he, chunk, mid), BF16),
        pltpu.VMEM((nseq, he, chunk, mid), BF16),
        pltpu.VMEM((9, ext, mid), BF16),
        pltpu.VMEM((4, n, values), F32),
        pltpu.VMEM((3 * n, 3 * values), BF16),
        pltpu.VMEM((nseq, he, chunk, mid), F32),
        pltpu.VMEM((nseq, he, chunk, mid), F32),
        pltpu.VMEM((ndp, ext, mid), BF16),
        pltpu.VMEM((nseq, 3, mblk, ndp * ext), BF16),
        pltpu.VMEM((ndp, 4, vblk, n), BF16),
        pltpu.VMEM((ndp, 4, vblk, n), BF16),
        pltpu.VMEM((9 * vblk, ndp * ext), BF16),
        pltpu.VMEM((ndp, cblk, n), BF16),
        pltpu.VMEM((ndp, 2, nz, cblk, n), BF16),
        pltpu.VMEM((9 * cblk, 3 * dblk), F32),
        pltpu.VMEM((nz // 2, 2, 3 * mblk, cuts[-1][1]), BF16),
        pltpu.VMEM((nz, 3 * mblk, cuts[-1][1]), BF16),
    ] + [pltpu.VMEM((nz // 2, 3 * mblk, cuts[0][1]), BF16)] * 4 + [
        [[pltpu.VMEM((nz // 2, 2, 3 * mblk, size), kind) for _, size in cuts]
         for kind in (BF16, BF16, F32, F32)],
        dma(15), dma(2), dma(2), dma(1), dma(1), dma(1), dma(1), dma(ndp), dma(1), dma(2),
        dma(ndp), dma(ndp), dma(ndp), dma(len(cuts)), dma(1), dma(2), dma(1),
    ]
    first, second = pl.pallas_call(
        make_kernel(dims),
        out_shape=(pltpu.VMEM((27 * cblk, dblk), F32), pltpu.VMEM((27, mblk, vblk), F32)),
        in_specs=[hbm] * 10,
        out_specs=(vm, vm),
        scratch_shapes=scratch,
        compiler_params=pltpu.CompilerParams(
            collective_id=0, has_side_effects=True, vmem_limit_bytes=60 * 1024 * 1024),
        name="step",
    )(tokens[0], conv_first.reshape(27 * width, mid), bias_first.reshape(1, mid),
      conv_second.reshape(27 * mid, values), bias_second,
      pixels[0], mask_index, tperm, spread_of, gather_of)
    first, second = pl.pallas_call(
        flush,
        out_shape=(jax.ShapeDtypeStruct(first.shape, F32), jax.ShapeDtypeStruct(second.shape, F32)),
        in_specs=[vm, vm],
        out_specs=(hbm, hbm),
        scratch_shapes=[dma(2)],
        compiler_params=pltpu.CompilerParams(vmem_limit_bytes=4 * 1024 * 1024),
        name="flush",
    )(pltpu.with_memory_space_constraint(first, pltpu.VMEM),
      pltpu.with_memory_space_constraint(second, pltpu.VMEM))
    first = first.reshape(27, cblk, dblk).transpose(0, 2, 1)
    return (first, second)


def solution(mesh):
    return jax.shard_map(
        per_device,
        mesh=mesh,
        in_specs=(
            P("dp", "seq", None, None, None),
            P(),
            P(),
            P(),
            P(),
            P("dp", None, "seq", None, None),
            P("dp", None),
        ),
        out_specs=(P(None, "seq", "dp"), P(None, "seq", "dp")),
        check_vma=False,
    )
```

```python
import jax
import jax.numpy as jnp
import numpy as np
from jax import lax
from jax.experimental import pallas as pl
from jax.experimental.pallas import tpu as pltpu
from jax.sharding import PartitionSpec as P

F32 = jnp.float32
BF16 = jnp.bfloat16
NT = (((1,), (1,)), ((), ()))
GELU_ROOT = 0.7978845608028654
GELU_CUBE = 0.044715


def floor_half(v):
    return v // 2 if v >= 0 else -1


def columns(total):
    half = -(-total // 512) * 256
    return [(0, half), (half, total - half)] if total > half else [(0, total)]


def make_kernel(dims):
    ndp, nseq, tf, rows, cols, width, mid, values = dims
    n = tf * cols * rows
    plane = cols * rows
    frames = tf * nseq
    hb = rows // nseq
    he = hb + 2
    line = frames * cols
    ext = he * line
    chunk = tf * cols
    dblk = width // nseq
    cblk = mid // ndp
    vblk = values // ndp
    mblk = mid // nseq
    ndev = ndp * nseq
    nz = nseq // 2
    clip_lanes = nseq * n
    nk = nz // 2
    cuts = columns(9 * vblk)

    def kernel(tok_hbm, w1_hbm, b1_hbm, w2_hbm, b2_hbm, pix_hbm, marks_hbm, tperm_hbm, spread_hbm,
               gather_hbm, o1, o2,
               tok, b1, b2, marks, tperm, spread_of, gather_of,
               w1, w2, w2b, weff, pixv, xbuf, xall, xs, tsend, thalo, tfield, im1, slope_of,
               hsend, hraw, vfield, tgt, cell, psend, praw,
               hrow, lhs, csend, call_, stack, gsend, gall, acc1, rsend, rall, asend, arecv, bsend, brecv,
               chunks,
               wsem, th_s, th_r, h_s, h_r, p_r, xz_r, xd_r, ht_r, e_r,
               c_r, g_r, f_r, q_r, r_r, a_r, b_r):
        dp = lax.axis_index("dp")
        seq = lax.axis_index("seq")
        me = dp * nseq + seq
        chip, core = seq // 2, lax.rem(seq, 2)
        p_s, xz_s, xd_s, ht_s, c_s, g_s, f_s, r_s, b_s = [
            wsem.at[pl.ds(k, 1)] for k in range(9)]
        e_s, q_s, a_s = [wsem.at[pl.ds(k, 2)] for k in (9, 11, 13)]
        qsend, qrecv, acc2, acc3 = chunks

        def remote(src, dst, ss, rs, d, s):
            return pltpu.make_async_remote_copy(
                src_ref=src, dst_ref=dst, send_sem=ss, recv_sem=rs,
                device_id=(d, s), device_id_type=pl.DeviceIdType.MESH)

        def drain(ref, sem):
            pltpu.make_async_copy(ref, ref, sem).wait()

        def each(low, count, act):
            def body(o, c):
                act(o)
                return c
            lax.fori_loop(low, count, body, 0)

        def differ(at, o, size):
            d, bit = 0, 1
            while bit < size:
                mine_, other = lax.rem(at // bit, 2), (o // bit) % 2
                d = d + bit * (mine_ + other - 2 * mine_ * other)
                bit = bit * 2
            return d

        def peer(o):
            return differ(dp, o, ndp)

        barrier = pltpu.get_barrier_semaphore()

        def greet(o):
            s, d = lax.div(o, ndp), lax.rem(o, ndp)

            @pl.when(jnp.logical_or(s != seq, d != dp))
            def _():
                pl.semaphore_signal(barrier, inc=1, device_id=(d, s),
                                    device_id_type=pl.DeviceIdType.MESH)

        loads = [pltpu.make_async_copy(src, dst, wsem.at[k]) for k, (src, dst) in enumerate((
            (tok_hbm, tok), (tperm_hbm, tperm), (b1_hbm, b1), (b2_hbm, b2), (marks_hbm, marks),
            (spread_hbm, spread_of), (gather_hbm, gather_of), (pix_hbm, pixv), (w2_hbm, w2)))]
        loads[0].start()
        loads[1].start()
        def w1_part(b, a, at):
            rows_ = 3 * width
            return pltpu.make_async_copy(
                w1_hbm.at[pl.ds((a * 9 + b * 3) * width, rows_)],
                w1.at[pl.ds(b * rows_, rows_), pl.ds(at * mid, mid)],
                wsem.at[13 if at == 2 else 9 + b])

        for b in range(3):
            w1_part(b, 0, 0).start()
            w1_part(b, 2, 1).start()
        for b in range(3):
            w1_part(b, 1, 2).start()
        each(0, ndev, greet)
        for m in loads[2:]:
            m.start()
        def ordered(frame):
            raw = frame.astype(F32).reshape(plane, width).astype(BF16)
            return jnp.dot(tperm[...], raw, preferred_element_type=F32)

        loads[0].wait()
        loads[1].wait()
        flat = jnp.concatenate([ordered(tok[t]) for t in range(tf)], axis=0)
        lr = lax.broadcasted_iota(jnp.int32, (rows, width), 0)
        edge = ((lr > 0).astype(F32), None, (lr < rows - 1).astype(F32))
        zero = jnp.zeros((3, tf, 1, rows, width), BF16)
        tfield[:, :, 0:1] = zero
        tfield[:, :, cols + 1:cols + 2] = zero
        for b in range(3):
            v = flat.reshape(tf, cols, rows, width)
            if b != 1:
                v = pltpu.roll(flat, 1 if b == 0 else n - 1, axis=0).reshape(
                    tf * cols, rows, width) * edge[b][None]
            tfield[b, :, 1:cols + 1] = v.reshape(tf, cols, rows, width).astype(BF16)
        for bc in range(9):
            im1[:, bc * width:(bc + 1) * width] = (
                tfield[bc // 3, :, bc % 3:bc % 3 + cols].reshape(n, width))
        parts = None
        for b in range(3):
            span = slice(b * 3 * width, (b + 1) * 3 * width)
            drain(w1.at[pl.ds(b * 3 * width, 3 * width), pl.ds(0, 2 * mid)], wsem.at[9 + b])
            part = jnp.dot(im1[:, span], w1[span, 0:2 * mid], preferred_element_type=F32)
            parts = part if parts is None else parts + part
        to_next, to_prev = parts[:, :mid], parts[:, mid:]
        tsend[0] = to_next[n - plane:]
        tsend[1] = to_prev[:plane]
        pl.semaphore_wait(barrier, ndev - 1)

        up = remote(tsend.at[0], thalo.at[0], th_s.at[0], th_r.at[0], dp,
                    jnp.minimum(seq + 1, nseq - 1))
        down = remote(tsend.at[1], thalo.at[1], th_s.at[1], th_r.at[1], dp,
                      jnp.maximum(seq - 1, 0))

        @pl.when(seq < nseq - 1)
        def _():
            up.start()

        @pl.when(seq > 0)
        def _():
            down.start()

        @pl.when(seq == 0)
        def _():
            thalo[0] = jnp.zeros((plane, mid), F32)

        @pl.when(seq == nseq - 1)
        def _():
            thalo[1] = jnp.zeros((plane, mid), F32)

        for m in loads[2:7]:
            m.wait()
        drain(w1.at[:, pl.ds(2 * mid, mid)], wsem.at[13])
        slope_of[...] = jnp.dot(im1[...], w1[:, 2 * mid:3 * mid],
                                preferred_element_type=F32) + b1[...]
        xt = flat.T
        for s in range(nseq):
            xbuf[s] = xt[s * dblk:(s + 1) * dblk].astype(BF16)

        @pl.when(seq > 0)
        def _():
            up.wait_recv()

        @pl.when(seq < nseq - 1)
        def _():
            down.wait_recv()

        if tf > 1:
            late = jnp.concatenate([thalo[0], to_next[:n - plane]], axis=0)
            early = jnp.concatenate([to_prev[plane:], thalo[1]], axis=0)
        else:
            late, early = thalo[0], thalo[1]
        z = slope_of[...] + late + early
        th_ = jnp.tanh(GELU_ROOT * (z + GELU_CUBE * z * z * z))
        hid = (0.5 * z * (1.0 + th_)).astype(BF16)
        hsend[...] = jnp.dot(spread_of[...], hid, preferred_element_type=F32).reshape(
            nseq, he, chunk, mid).astype(BF16)

        def h_copy(o):
            s = lax.rem(seq + o, nseq)
            return remote(hsend.at[s], hraw.at[seq], h_s.at[0], h_r.at[0], dp, s)

        each(1, nseq, lambda o: h_copy(o).start())
        hraw[seq] = hsend[seq]
        slope_of[...] = 0.5 * (1.0 + th_) + 0.5 * z * (1.0 - th_ * th_) * GELU_ROOT * (
            1.0 + 3.0 * GELU_CUBE * z * z)

        for m in loads[7:]:
            m.wait()
        raw = [pixv[:, h].astype(F32).reshape(line, 4 * values) for h in range(hb)]
        px = jnp.concatenate(raw, axis=0)
        center = px - jnp.mean(px, axis=-1, keepdims=True)
        spread = jnp.mean(center * center, axis=-1, keepdims=True)
        normed = center * lax.rsqrt(spread + 1e-06)
        for ij in range(4):
            tgt[ij] = normed[:, ij * values:(ij + 1) * values] - b2[...].reshape(1, values)
        le = lax.broadcasted_iota(jnp.int32, (n, 1), 0)
        spot = lax.div(le, line) * cols + lax.rem(le, cols) + seq * (hb * cols)
        matches = (spot == marks[...]).astype(F32)
        scale = 2.0 / (4 * values) * jnp.sum(matches, axis=1, keepdims=True)

        step = 16 if mid % 16 == 0 else mid

        def sum_taps(o):
            a, r = lax.div(o, mid // step), lax.rem(o, mid // step)
            w = []
            for bc in range(9):
                part = w2[pl.ds(pl.multiple_of((a * 9 + bc) * mid + r * step, step), step)]
                w2b[bc // 3, pl.ds(pl.multiple_of(a * mid + r * step, step), step),
                    (bc % 3) * values:(bc % 3 + 1) * values] = part
                w.append(part.astype(F32))
            wide = []
            for b in range(3):
                x, y, z_ = w[b * 3:b * 3 + 3]
                wide.append((x, y + z_, x + y, z_))
            for i in range(2):
                for e in range(4):
                    x, y, z_ = wide[0][e], wide[1][e], wide[2][e]
                    for rh, v in enumerate((x, y + z_) if i == 0 else (x + y, z_)):
                        at = (a * 4 + rh * 2 + e % 2) * mid + r * step
                        weff[i * 2 + e // 2, pl.ds(pl.multiple_of(at, step), step)] = v.astype(BF16)

        each(0, 3 * (mid // step), sum_taps)

        def band(size):
            li = lax.broadcasted_iota(jnp.int32, (line, size), 0)
            lw = lax.rem(li, cols)
            return ((lw > 0).astype(F32), (lw < cols - 1).astype(F32),
                    (li >= cols).astype(F32), (li < line - cols).astype(F32))

        w_low, w_high, t_low, t_high = band(mid)
        p_low, p_high, _, _ = band(values)
        le = lax.broadcasted_iota(jnp.int32, (1, ext), 1)
        lw = lax.rem(le, cols)
        lt = lax.rem(le, line)
        s_low, s_high = (lt >= cols).astype(F32), (lt < line - cols).astype(F32)

        def shifted(v, by, mask):
            m = v.shape[0]
            rolled = pltpu.roll(v, (-by) % m, axis=0)
            return (rolled.reshape(m // line, line, v.shape[1]) * mask[None]).reshape(v.shape)

        drain(hraw.at[pl.ds(0, nseq - 1)], h_r.at[0])

        def xz_copy(o):
            s = lax.rem(seq + o, nseq)
            return remote(xbuf.at[s], xall.at[dp, seq], xz_s.at[0], xz_r.at[0], dp, s)

        each(1, nseq, lambda o: xz_copy(o).start())
        xall[dp, seq] = xbuf[seq]

        hin = hraw[...].astype(F32)
        hext = jnp.concatenate(
            [hin[:, hh].reshape(line, mid) for hh in range(he)], axis=0)
        for a in range(3):
            late = hext if a == 1 else shifted(
                hext, cols * (a - 1), t_low if a == 0 else t_high)
            for e in range(3):
                v = late if e == 1 else shifted(late, e - 1, w_low if e == 0 else w_high)
                vfield[a * 3 + e] = v.astype(BF16)
        hrow[dp, 0:hb * line] = hext[line:(hb + 1) * line].astype(BF16)
        hrow[dp, hb * line:(hb + 1) * line] = hext[0:line].astype(BF16)
        hrow[dp, (hb + 1) * line:ext] = hext[(hb + 1) * line:ext].astype(BF16)
        mine = hrow.at[dp, pl.ds(0, hb * line)]

        def ht_copy(o):
            d = peer(o)
            return remote(mine, mine, ht_s.at[0], ht_r.at[0], d, seq)

        each(1, ndp, lambda o: ht_copy(o).start())

        cots = []
        for ij in range(4):
            i, j = ij // 2, ij % 2
            near = []
            for k in range(12):
                low = (i + k // 2 % 2) * line
                near.append(vfield[k // 4 * 3 + j + k % 2, low:low + hb * line])
            predict = jnp.dot(jnp.concatenate(near, axis=1), weff[ij], preferred_element_type=F32)
            cot = (scale * (predict - tgt[ij])).astype(BF16).astype(F32)
            cots.append(cot)
            turned = cot.T
            for d in range(ndp):
                csend[d, ij] = turned[d * vblk:(d + 1) * vblk].astype(BF16)

        def c_copy(o):
            d = peer(o)
            return remote(csend.at[d], call_.at[dp], c_s.at[0], c_r.at[dp], d, seq)

        each(1, ndp, lambda o: c_copy(o).start())
        call_[dp] = csend[dp]

        def pair_sums(low, high, after, before):
            return (high + after(low), low + high, before(high) + low)

        def after_row(v):
            return shifted(v, 1, p_high)

        def before_row(v):
            return shifted(v, -1, p_low)

        for u, (low, high) in enumerate((
                (cots[0], cots[1]), (cots[2], cots[3]),
                (cots[0] + cots[2], cots[1] + cots[3]))):
            for c, s in enumerate(pair_sums(low, high, after_row, before_row)):
                cell[u * n:(u + 1) * n, c * values:(c + 1) * values] = s.astype(BF16)

        both = cell[0:2 * n]
        first = lax.dot_general(both, w2b[0], NT, preferred_element_type=F32)
        third = lax.dot_general(both, w2b[2], NT, preferred_element_type=F32)
        second = lax.dot_general(cell[2 * n:3 * n], w2b[1], NT, preferred_element_type=F32)
        same = first[n:] + second + third[:n]
        pieces = []
        for hh in range(he):
            total = None
            for v, dh in ((first[:n], -1), (same, 0), (third[n:], 1)):
                h = hh - 1 - dh
                if 0 <= h < hb:
                    part = v[h * line:(h + 1) * line]
                    total = part if total is None else total + part
            back = total[:, mid:2 * mid]
            back = back + shifted(total[:, :mid], cols, t_high)
            back = back + shifted(total[:, 2 * mid:], -cols, t_low)
            pieces.append(back)
        for hh in range(he):
            psend[:, hh] = pieces[hh].reshape(nseq, chunk, mid)

        def p_copy(o):
            s = lax.rem(seq + o, nseq)
            return remote(psend.at[s], praw.at[seq], p_s.at[0], p_r.at[0], dp, s)

        each(1, nseq, lambda o: p_copy(o).start())
        praw[seq] = psend[seq]

        drain(hrow.at[pl.ds(0, ndp - 1), pl.ds(0, hb * line)], ht_r.at[0])
        others = pl.ds(0, ndp - 1)

        def edge_copy(o, k):
            q = peer(o)
            if k == 0:
                return remote(hrow.at[q, pl.ds((hb - 1) * line, line)],
                              hrow.at[q, pl.ds(hb * line, line)], e_s.at[0], e_r.at[0], dp,
                              jnp.minimum(seq + 1, nseq - 1))
            return remote(hrow.at[q, pl.ds(0, line)],
                          hrow.at[q, pl.ds((hb + 1) * line, line)], e_s.at[1], e_r.at[1], dp,
                          jnp.maximum(seq - 1, 0))

        def no_edge(k):
            def put(o):
                q = peer(o)
                hrow[q, (hb + k) * line:(hb + k + 1) * line] = jnp.zeros((line, mid), BF16)
            each(1, ndp, put)

        @pl.when(seq < nseq - 1)
        def _():
            each(1, ndp, lambda o: edge_copy(o, 0).start())

        @pl.when(seq > 0)
        def _():
            each(1, ndp, lambda o: edge_copy(o, 1).start())

        @pl.when(seq == 0)
        def _():
            no_edge(0)

        @pl.when(seq == nseq - 1)
        def _():
            no_edge(1)

        lo = lax.broadcasted_iota(jnp.int32, (1, hb * line), 1)
        lw = lax.rem(lo, cols)
        e_low, e_high = (lw > 0).astype(F32), (lw < cols - 1).astype(F32)
        early_rows, late_rows = (lo < (hb - 1) * line).astype(F32), (lo >= line).astype(F32)

        def lane_after(v):
            return pltpu.roll(v, hb * line - 1, axis=1) * e_high

        def lane_before(v):
            return pltpu.roll(v, 1, axis=1) * e_low

        stack[3 * vblk:6 * vblk] = jnp.zeros((3 * vblk, ndp * ext), BF16)

        tile = hb * line

        def clip_stack(q, inner_at, outer_at):
            by_col, by_edge = [], []
            for j in range(2):
                low, high = call_[q, j].astype(F32), call_[q, 2 + j].astype(F32)
                by_col.append((high + pltpu.roll(low, (hb - 1) * line, axis=1) * early_rows,
                               low + high, low + pltpu.roll(high, line, axis=1) * late_rows))
                by_edge.append((low * early_rows, None, high * late_rows))
            at, rim = pl.ds(inner_at, tile), pl.ds(outer_at, 2 * line)
            k = 0
            for b in range(3):
                inner = pair_sums(by_col[0][b], by_col[1][b], lane_after, lane_before)
                outer = (None,) * 3 if b == 1 else pair_sums(
                    by_edge[0][b], by_edge[1][b], lane_after, lane_before)
                for s, r in zip(inner, outer):
                    stack[k * vblk:(k + 1) * vblk, at] = s.astype(BF16)
                    if r is not None:
                        stack[k * vblk:(k + 1) * vblk, rim] = r.astype(BF16)
                    k += 1

        clip_stack(dp, 0, (ndp - 1) * tile)

        def clip_lhs(o, low, high, at):
            size = high - low
            turned = hrow[peer(o), low:high].astype(F32).T
            for a in range(3):
                v = turned
                if a != 1:
                    v = pltpu.roll(turned, (cols if a == 0 else size - cols), axis=1)
                    v = v * (s_low if a == 0 else s_high)[:, low:high]
                lhs[:, a, :, at:at + size] = v.reshape(nseq, mblk, size).astype(BF16)

        for o in range(ndp):
            clip_lhs(o, 0, tile, (ndp if o == ndp - 1 else o) * tile)
        clip_lhs(0, tile, ext, (ndp - 1) * tile)

        def other_clip(o, inner_at):
            q = peer(o)
            drain(call_.at[q], c_r.at[q])
            clip_stack(q, inner_at, pl.multiple_of((ndp + o) * tile, 128))

        each(1, ndp - 1, lambda o: other_clip(o, pl.multiple_of(o * tile, 128)))

        def half(k, j, first_part, last_part):
            depth = (last_part - first_part) * ndp * tile
            span = slice(first_part * ndp * tile, last_part * ndp * tile)
            block = jnp.concatenate(
                [lhs[2 * s + k, :, :, span].reshape(3 * mblk, depth) for s in range(nz)],
                axis=0)
            low, size = cuts[j]
            return lax.dot_general(block, stack[low:low + size, span], NT,
                                   preferred_element_type=F32).reshape(nk, 2, 3 * mblk, size)

        for j in range(len(cuts)):
            acc3[j][...] = half(1 - core, j, 0, 1)

        drain(praw.at[pl.ds(0, nseq - 1)], p_r.at[0])
        got = praw[...].reshape(nseq * he * chunk, mid)
        major = got.astype(BF16)
        minor = (got - major.astype(F32)).astype(BF16)
        grad_h = (jnp.dot(gather_of[...], major, preferred_element_type=F32)
                  + jnp.dot(gather_of[...], minor, preferred_element_type=F32))
        grad_z = (grad_h * slope_of[...]).astype(BF16).astype(F32).T
        for d in range(ndp):
            gsend[d] = grad_z[d * cblk:(d + 1) * cblk].astype(BF16)

        def g_copy(o):
            t = lax.rem(dp * nz + chip + o, ndp * nz)
            d = t // nz
            return remote(gsend.at[d], gall.at[dp, core, chip], g_s.at[0], g_r.at[dp], d,
                          2 * lax.rem(t, nz) + core)

        each(1, ndp * nz, lambda o: g_copy(o).start())
        gall[dp, core, chip] = gsend[dp]
        drain(xall.at[0, pl.ds(0, nseq - 1)], xz_r.at[0])

        def xd_copy(o):
            d = peer(o)
            return remote(xall.at[dp], xall.at[dp], xd_s.at[0], xd_r.at[dp], d, seq)

        each(1, ndp, lambda o: xd_copy(o).start())

        @pl.when(seq > 0)
        def _():
            drain(hrow.at[others, pl.ds(0, line)], e_r.at[0])

        @pl.when(seq < nseq - 1)
        def _():
            drain(hrow.at[others, pl.ds(0, line)], e_r.at[1])

        for o in range(1, ndp):
            clip_lhs(o, tile, ext, (ndp + o) * tile)
        other_clip(ndp - 1, ndp * tile)

        swaps = [remote(qs, qr, q_s.at[j], q_r.at[j], dp, 2 * chip + 1 - core)
                 for j, (qs, qr) in enumerate(zip(qsend, qrecv))]
        for j in range(len(cuts)):
            qsend[j][...] = (acc3[j][...] + half(1 - core, j, 1, 2)).astype(BF16)
            swaps[j].start()
        par, kz = lax.rem(chip, 2), chip // 2

        def g_forward(q):
            return remote(gall.at[q, core], gall.at[q, core], f_s.at[0], f_r.at[q], dp,
                          2 * chip + 1 - core)

        def pass_on(o):
            q = peer(o)
            drain(gall.at[0, 0], g_r.at[q])
            g_forward(q).start()

        def forward_all():
            drain(gall.at[0, 0, pl.ds(0, nz - 1)], g_r.at[dp])
            g_forward(dp).start()
            each(1, ndp, pass_on)

        def near_copy(k):
            return remote(asend.at[k], arecv.at[k], a_s.at[0], a_r.at[0], dp,
                          2 * (chip + 1 - 2 * par) + core)

        def last_copy():
            return remote(asend.at[kz], arecv.at[kz], a_s.at[1], a_r.at[1],
                          dp, 2 * (chip + 1 - 2 * par) + core)

        def far_copy(o):
            k = lax.rem(kz + o, nk)
            return remote(bsend.at[k], brecv.at[kz], b_s.at[0], b_r.at[0], dp,
                          2 * (2 * k + par) + core)

        def r_copy(o):
            t = differ(chip, nz - o, nz)
            return remote(rsend.at[t // 2, lax.rem(t, 2)], rall.at[chip], r_s.at[0], r_r.at[0],
                          dp, 2 * t + core)

        for j in range(len(cuts)):
            acc2[j][...] = half(core, j, 0, 2)
            swaps[j].wait_recv()
            if j > 0:
                rsend[...] = (acc2[j][...] + qrecv[j][...].astype(F32)).astype(BF16)
                each(1, nz, lambda o: r_copy(o).start())
                acc2[j][kz, par] = acc2[j][kz, par] + qrecv[j][kz, par].astype(F32)
                continue
            asend[...] = (acc2[j][:, 1 - par] + qrecv[j][:, 1 - par].astype(F32)).astype(BF16)
            each(1, nk, lambda o: near_copy(lax.rem(kz + o, nk)).start())
            acc2[j][:, par] = acc2[j][:, par] + qrecv[j][:, par].astype(F32)
        lx = lax.broadcasted_iota(jnp.int32, (1, clip_lanes), 1)
        x_low, x_high = (lx >= plane).astype(F32), (lx < clip_lanes - plane).astype(F32)

        def turn_clip(q):
            x = jnp.concatenate([xall[q, s] for s in range(nseq)], axis=1)
            xf = x.astype(F32)
            xs[q, 0:dblk] = (pltpu.roll(xf, plane, axis=1) * x_low).astype(BF16)
            xs[q, dblk:2 * dblk] = x
            xs[q, 2 * dblk:3 * dblk] = (
                pltpu.roll(xf, clip_lanes - plane, axis=1) * x_high).astype(BF16)

        turn_clip(dp)
        acc1[...] = jnp.zeros_like(acc1)
        forward_all()
        drain(asend.at[pl.ds(0, nk - 1)], a_r.at[0])

        def combine(o):
            k = lax.rem(kz + o, nk)
            bsend[k] = (acc2[0][k, par] + arecv[k].astype(F32)).astype(BF16)
            far_copy(o).start()

        each(1, nk, combine)
        last_copy().start()

        lh = lax.rem(lx, rows)
        lc = lax.rem(lx, plane)
        g_h = ((lh < rows - 1).astype(F32), None, (lh > 0).astype(F32))
        g_w = ((lc < plane - rows).astype(F32), None, (lc >= rows).astype(F32))

        def one_first(q):
            g = jnp.concatenate([gall[q, s % 2, s // 2].astype(F32) for s in range(nseq)], axis=1)
            grid = []
            for b in range(3):
                v = g if b == 1 else pltpu.roll(g, (b - 1) % clip_lanes, axis=1) * g_h[b]
                for c in range(3):
                    u = v if c == 1 else pltpu.roll(
                        v, ((c - 1) * rows) % clip_lanes, axis=1) * g_w[c]
                    grid.append(u.astype(BF16))
            acc1[...] += lax.dot_general(jnp.concatenate(grid, axis=0), xs[q], NT,
                                         preferred_element_type=F32)

        drain(gall.at[0, 0], f_r.at[dp])
        one_first(dp)

        def arrived_first(o):
            q = peer(o)
            drain(xall.at[0], xd_r.at[q])
            turn_clip(q)
            drain(gall.at[0, 0], f_r.at[q])
            one_first(q)

        each(1, ndp, arrived_first)
        for a in range(3):
            o1[a * 9 * cblk:(a + 1) * 9 * cblk] = acc1[:, a * dblk:(a + 1) * dblk]

        @pl.when(seq < nseq - 1)
        def _():
            up.wait_send()

        @pl.when(seq > 0)
        def _():
            down.wait_send()

        drain(hsend.at[pl.ds(0, nseq - 1)], h_s.at[0])
        drain(xbuf.at[pl.ds(0, nseq - 1)], xz_s.at[0])
        drain(hrow.at[pl.ds(0, ndp - 1), pl.ds(0, hb * line)], ht_s.at[0])
        drain(csend.at[pl.ds(0, ndp - 1)], c_s.at[0])
        drain(psend.at[pl.ds(0, nseq - 1)], p_s.at[0])
        drain(xall.at[pl.ds(0, ndp - 1)], xd_s.at[0])
        for w in swaps:
            w.wait_send()
        for o in range(ndp):
            drain(gall.at[0, 0, pl.ds(0, nz - 1)] if o == 0 else gall.at[0, 0], g_s.at[0])
        drain(gall.at[:, 0], f_s.at[0])
        @pl.when(seq < nseq - 1)
        def _():
            drain(hrow.at[others, pl.ds(0, line)], e_s.at[0])

        @pl.when(seq > 0)
        def _():
            drain(hrow.at[others, pl.ds(0, line)], e_s.at[1])

        totals = []
        drain(asend.at[0], a_r.at[1])
        acc2[0][kz, par] = acc2[0][kz, par] + arecv[kz].astype(F32)
        drain(brecv.at[pl.ds(0, nk - 1)], b_r.at[0])

        def add(o):
            acc2[0][kz, par] = (acc2[0][kz, par]
                                     + brecv[lax.rem(kz + o, nk)].astype(F32))

        each(1, nk, add)
        totals.append(acc2[0][kz, par])
        if len(cuts) > 1:
            drain(rall.at[pl.ds(0, nz - 1)], r_r.at[0])
            total = acc2[1][kz, par]
            for o in range(1, nz):
                total = total + rall[differ(chip, o, nz)].astype(F32)
            totals.append(total)
        total = jnp.concatenate(totals, axis=1)
        for a in range(3):
            for bc in range(9):
                o2[a * 9 + bc] = total[a * mblk:(a + 1) * mblk, bc * vblk:(bc + 1) * vblk]
        if len(cuts) > 1:
            drain(rall.at[pl.ds(0, nz - 1)], r_s.at[0])
        drain(asend.at[pl.ds(0, nk - 1)], a_s.at[0])
        drain(asend.at[0], a_s.at[1])
        drain(brecv.at[pl.ds(0, nk - 1)], b_s.at[0])

    return kernel


def flush(a, b, oa, ob, sem):
    moves = (pltpu.make_async_copy(a, oa, sem.at[0]), pltpu.make_async_copy(b, ob, sem.at[1]))
    for m in moves:
        m.start()
    for m in moves:
        m.wait()


def per_device(tokens, conv_first, bias_first, conv_second, bias_second, pixels, mask_index):
    ndp, nseq = lax.axis_size("dp"), lax.axis_size("seq")
    tf, rows, cols, width = tokens.shape[1:]
    frames = tf * nseq
    mid, values = conv_second.shape[1], conv_second.shape[2]
    n = tf * rows * cols
    hb = rows // nseq
    he = hb + 2
    line = frames * cols
    ext = he * line
    chunk = tf * cols
    dims = (ndp, nseq, tf, rows, cols, width, mid, values)
    plane = rows * cols
    dblk, cblk, vblk, mblk = width // nseq, mid // ndp, values // ndp, mid // nseq
    nz = nseq // 2
    cuts = columns(9 * vblk)

    idx = np.arange(n, dtype=np.int32)
    t_of, w_of, h_of = idx // plane, idx // rows % cols, idx % rows
    flat_place = (h_of * cols + w_of)[:plane]
    tperm = jnp.asarray(flat_place[:, None] == idx[None, :plane], BF16)
    msg = np.arange(nseq * he * chunk, dtype=np.int32)
    m_s, m_h = msg // (he * chunk), msg // chunk % he
    m_t, m_w = msg % chunk // cols, msg % cols
    m_row = m_s * hb + m_h - 1
    same = ((m_row[:, None] == h_of[None]) & (m_t[:, None] == t_of[None])
            & (m_w[:, None] == w_of[None]))
    spread_of = jnp.asarray(same, BF16)
    gather_of = jnp.asarray(same.T, BF16)
    vm = pl.BlockSpec(memory_space=pltpu.VMEM)
    hbm = pl.BlockSpec(memory_space=pl.ANY)

    def dma(k):
        return pltpu.SemaphoreType.DMA((k,))

    scratch = [
        pltpu.VMEM((tf, rows, cols, width), BF16),
        pltpu.VMEM((1, mid), F32),
        pltpu.VMEM((values,), F32),
        pltpu.VMEM(mask_index.shape, jnp.int32),
        pltpu.VMEM((plane, plane), BF16),
        pltpu.VMEM((nseq * he * chunk, n), BF16),
        pltpu.VMEM((n, nseq * he * chunk), BF16),
        pltpu.VMEM((9 * width, 3 * mid), BF16),
        pltpu.VMEM((27 * mid, values), BF16),
        pltpu.VMEM((3, 3 * mid, 3 * values), BF16),
        pltpu.VMEM((4, 12 * mid, values), BF16),
        pltpu.VMEM((frames, hb, cols, 4 * values), BF16),
        pltpu.VMEM((nseq, dblk, n), BF16),
        pltpu.VMEM((ndp, nseq, dblk, n), BF16),
        pltpu.VMEM((ndp, 3 * dblk, nseq * n), BF16),
        pltpu.VMEM((2, plane, mid), F32),
        pltpu.VMEM((2, plane, mid), F32),
        pltpu.VMEM((3, tf, cols + 2, rows, width), BF16),
        pltpu.VMEM((n, 9 * width), BF16),
        pltpu.VMEM((n, mid), F32),
        pltpu.VMEM((nseq, he, chunk, mid), BF16),
        pltpu.VMEM((nseq, he, chunk, mid), BF16),
        pltpu.VMEM((9, ext, mid), BF16),
        pltpu.VMEM((4, n, values), F32),
        pltpu.VMEM((3 * n, 3 * values), BF16),
        pltpu.VMEM((nseq, he, chunk, mid), F32),
        pltpu.VMEM((nseq, he, chunk, mid), F32),
        pltpu.VMEM((ndp, ext, mid), BF16),
        pltpu.VMEM((nseq, 3, mblk, ndp * ext), BF16),
        pltpu.VMEM((ndp, 4, vblk, n), BF16),
        pltpu.VMEM((ndp, 4, vblk, n), BF16),
        pltpu.VMEM((9 * vblk, ndp * ext), BF16),
        pltpu.VMEM((ndp, cblk, n), BF16),
        pltpu.VMEM((ndp, 2, nz, cblk, n), BF16),
        pltpu.VMEM((9 * cblk, 3 * dblk), F32),
        pltpu.VMEM((nz // 2, 2, 3 * mblk, cuts[-1][1]), BF16),
        pltpu.VMEM((nz, 3 * mblk, cuts[-1][1]), BF16),
    ] + [pltpu.VMEM((nz // 2, 3 * mblk, cuts[0][1]), BF16)] * 4 + [
        [[pltpu.VMEM((nz // 2, 2, 3 * mblk, size), kind) for _, size in cuts]
         for kind in (BF16, BF16, F32, F32)],
        dma(15), dma(2), dma(2), dma(1), dma(1), dma(1), dma(1), dma(ndp), dma(1), dma(2),
        dma(ndp), dma(ndp), dma(ndp), dma(len(cuts)), dma(1), dma(2), dma(1),
    ]
    first, second = pl.pallas_call(
        make_kernel(dims),
        out_shape=(pltpu.VMEM((27 * cblk, dblk), F32), pltpu.VMEM((27, mblk, vblk), F32)),
        in_specs=[hbm] * 10,
        out_specs=(vm, vm),
        scratch_shapes=scratch,
        compiler_params=pltpu.CompilerParams(
            collective_id=0, has_side_effects=True, vmem_limit_bytes=60 * 1024 * 1024),
        name="step",
    )(tokens[0], conv_first.reshape(27 * width, mid), bias_first.reshape(1, mid),
      conv_second.reshape(27 * mid, values), bias_second,
      pixels[0], mask_index, tperm, spread_of, gather_of)
    first, second = pl.pallas_call(
        flush,
        out_shape=(jax.ShapeDtypeStruct(first.shape, F32), jax.ShapeDtypeStruct(second.shape, F32)),
        in_specs=[vm, vm],
        out_specs=(hbm, hbm),
        scratch_shapes=[dma(2)],
        compiler_params=pltpu.CompilerParams(vmem_limit_bytes=4 * 1024 * 1024),
        name="flush",
    )(pltpu.with_memory_space_constraint(first, pltpu.VMEM),
      pltpu.with_memory_space_constraint(second, pltpu.VMEM))
    first = first.reshape(27, cblk, dblk).transpose(0, 2, 1)
    return (first, second)


def solution(mesh):
    return jax.shard_map(
        per_device,
        mesh=mesh,
        in_specs=(
            P("dp", "seq", None, None, None),
            P(),
            P(),
            P(),
            P(),
            P("dp", None, "seq", None, None),
            P("dp", None),
        ),
        out_specs=(P(None, "seq", "dp"), P(None, "seq", "dp")),
        check_vma=False,
    )
```

```python
import jax
import jax.numpy as jnp
import numpy as np
from jax import lax
from jax.experimental import pallas as pl
from jax.experimental.pallas import tpu as pltpu
from jax.sharding import PartitionSpec as P

F32 = jnp.float32
BF16 = jnp.bfloat16
NT = (((1,), (1,)), ((), ()))
GELU_ROOT = 0.7978845608028654
GELU_CUBE = 0.044715


def floor_half(v):
    return v // 2 if v >= 0 else -1


def columns(total):
    half = -(-total // 512) * 256
    return [(0, half), (half, total - half)] if total > half else [(0, total)]


def make_kernel(dims):
    ndp, nseq, tf, rows, cols, width, mid, values = dims
    n = tf * cols * rows
    plane = cols * rows
    frames = tf * nseq
    hb = rows // nseq
    he = hb + 2
    line = frames * cols
    ext = he * line
    chunk = tf * cols
    dblk = width // nseq
    cblk = mid // ndp
    vblk = values // ndp
    mblk = mid // nseq
    ndev = ndp * nseq
    nz = nseq // 2
    clip_lanes = nseq * n
    nk = nz // 2
    cuts = columns(9 * vblk)

    def kernel(tok_hbm, w1_hbm, b1_hbm, w2_hbm, b2_hbm, pix_hbm, marks_hbm, tperm_hbm, spread_hbm,
               gather_hbm, o1, o2,
               tok, b1, b2, marks, tperm, spread_of, gather_of,
               w1, w2, w2b, weff, pixv, xbuf, xall, xs, tsend, thalo, tfield, im1, slope_of,
               hsend, hraw, vfield, tgt, cell, psend, praw,
               hrow, lhs, csend, call_, stack, gsend, gall, acc1, rsend, rall, asend, arecv, bsend, brecv,
               chunks,
               wsem, th_s, th_r, h_s, h_r, p_r, xz_r, xd_r, ht_r, e_r,
               c_r, g_r, f_r, q_r, r_r, a_r, b_r):
        dp = lax.axis_index("dp")
        seq = lax.axis_index("seq")
        me = dp * nseq + seq
        chip, core = seq // 2, lax.rem(seq, 2)
        p_s, xz_s, xd_s, ht_s, c_s, g_s, f_s, r_s, b_s = [
            wsem.at[pl.ds(k, 1)] for k in range(9)]
        e_s, q_s, a_s = [wsem.at[pl.ds(k, 2)] for k in (9, 11, 13)]
        qsend, qrecv, acc2, acc3 = chunks

        def remote(src, dst, ss, rs, d, s):
            return pltpu.make_async_remote_copy(
                src_ref=src, dst_ref=dst, send_sem=ss, recv_sem=rs,
                device_id=(d, s), device_id_type=pl.DeviceIdType.MESH)

        def drain(ref, sem):
            pltpu.make_async_copy(ref, ref, sem).wait()

        def each(low, count, act):
            def body(o, c):
                act(o)
                return c
            lax.fori_loop(low, count, body, 0)

        def differ(at, o, size):
            d, bit = 0, 1
            while bit < size:
                mine_, other = lax.rem(at // bit, 2), (o // bit) % 2
                d = d + bit * (mine_ + other - 2 * mine_ * other)
                bit = bit * 2
            return d

        def peer(o):
            return differ(dp, o, ndp)

        barrier = pltpu.get_barrier_semaphore()

        def greet(o):
            s, d = lax.div(o, ndp), lax.rem(o, ndp)

            @pl.when(jnp.logical_or(s != seq, d != dp))
            def _():
                pl.semaphore_signal(barrier, inc=1, device_id=(d, s),
                                    device_id_type=pl.DeviceIdType.MESH)

        loads = [pltpu.make_async_copy(src, dst, wsem.at[k]) for k, (src, dst) in enumerate((
            (tok_hbm, tok), (tperm_hbm, tperm), (b1_hbm, b1), (b2_hbm, b2), (marks_hbm, marks),
            (spread_hbm, spread_of), (gather_hbm, gather_of), (pix_hbm, pixv), (w2_hbm, w2)))]
        loads[0].start()
        loads[1].start()
        def w1_part(b, a, at):
            rows_ = 3 * width
            return pltpu.make_async_copy(
                w1_hbm.at[pl.ds((a * 9 + b * 3) * width, rows_)],
                w1.at[pl.ds(b * rows_, rows_), pl.ds(at * mid, mid)],
                wsem.at[13 if at == 2 else 9 + b])

        for b in range(3):
            w1_part(b, 0, 0).start()
            w1_part(b, 2, 1).start()
        for b in range(3):
            w1_part(b, 1, 2).start()
        each(0, ndev, greet)
        for m in loads[2:]:
            m.start()
        def ordered(frame):
            raw = frame.astype(F32).reshape(plane, width).astype(BF16)
            return jnp.dot(tperm[...], raw, preferred_element_type=F32)

        loads[0].wait()
        loads[1].wait()
        flat = jnp.concatenate([ordered(tok[t]) for t in range(tf)], axis=0)
        lr = lax.broadcasted_iota(jnp.int32, (rows, width), 0)
        edge = ((lr > 0).astype(F32), None, (lr < rows - 1).astype(F32))
        zero = jnp.zeros((3, tf, 1, rows, width), BF16)
        tfield[:, :, 0:1] = zero
        tfield[:, :, cols + 1:cols + 2] = zero
        for b in range(3):
            v = flat.reshape(tf, cols, rows, width)
            if b != 1:
                v = pltpu.roll(flat, 1 if b == 0 else n - 1, axis=0).reshape(
                    tf * cols, rows, width) * edge[b][None]
            tfield[b, :, 1:cols + 1] = v.reshape(tf, cols, rows, width).astype(BF16)
        for bc in range(9):
            im1[:, bc * width:(bc + 1) * width] = (
                tfield[bc // 3, :, bc % 3:bc % 3 + cols].reshape(n, width))
        parts = None
        for b in range(3):
            span = slice(b * 3 * width, (b + 1) * 3 * width)
            drain(w1.at[pl.ds(b * 3 * width, 3 * width), pl.ds(0, 2 * mid)], wsem.at[9 + b])
            part = jnp.dot(im1[:, span], w1[span, 0:2 * mid], preferred_element_type=F32)
            parts = part if parts is None else parts + part
        to_next, to_prev = parts[:, :mid], parts[:, mid:]
        tsend[0] = to_next[n - plane:]
        tsend[1] = to_prev[:plane]
        pl.semaphore_wait(barrier, ndev - 1)

        up = remote(tsend.at[0], thalo.at[0], th_s.at[0], th_r.at[0], dp,
                    jnp.minimum(seq + 1, nseq - 1))
        down = remote(tsend.at[1], thalo.at[1], th_s.at[1], th_r.at[1], dp,
                      jnp.maximum(seq - 1, 0))

        @pl.when(seq < nseq - 1)
        def _():
            up.start()

        @pl.when(seq > 0)
        def _():
            down.start()

        @pl.when(seq == 0)
        def _():
            thalo[0] = jnp.zeros((plane, mid), F32)

        @pl.when(seq == nseq - 1)
        def _():
            thalo[1] = jnp.zeros((plane, mid), F32)

        for m in loads[2:7]:
            m.wait()
        drain(w1.at[:, pl.ds(2 * mid, mid)], wsem.at[13])
        slope_of[...] = jnp.dot(im1[...], w1[:, 2 * mid:3 * mid],
                                preferred_element_type=F32) + b1[...]
        xt = flat.T
        for s in range(nseq):
            xbuf[s] = xt[s * dblk:(s + 1) * dblk].astype(BF16)

        @pl.when(seq > 0)
        def _():
            up.wait_recv()

        @pl.when(seq < nseq - 1)
        def _():
            down.wait_recv()

        if tf > 1:
            late = jnp.concatenate([thalo[0], to_next[:n - plane]], axis=0)
            early = jnp.concatenate([to_prev[plane:], thalo[1]], axis=0)
        else:
            late, early = thalo[0], thalo[1]
        z = slope_of[...] + late + early
        th_ = jnp.tanh(GELU_ROOT * (z + GELU_CUBE * z * z * z))
        hid = (0.5 * z * (1.0 + th_)).astype(BF16)
        hsend[...] = jnp.dot(spread_of[...], hid, preferred_element_type=F32).reshape(
            nseq, he, chunk, mid).astype(BF16)

        def h_copy(o):
            s = lax.rem(seq + o, nseq)
            return remote(hsend.at[s], hraw.at[seq], h_s.at[0], h_r.at[0], dp, s)

        each(1, nseq, lambda o: h_copy(o).start())
        hraw[seq] = hsend[seq]
        slope_of[...] = 0.5 * (1.0 + th_) + 0.5 * z * (1.0 - th_ * th_) * GELU_ROOT * (
            1.0 + 3.0 * GELU_CUBE * z * z)

        for m in loads[7:]:
            m.wait()
        raw = [pixv[:, h].astype(F32).reshape(line, 4 * values) for h in range(hb)]
        px = jnp.concatenate(raw, axis=0)
        center = px - jnp.mean(px, axis=-1, keepdims=True)
        spread = jnp.mean(center * center, axis=-1, keepdims=True)
        normed = center * lax.rsqrt(spread + 1e-06)
        for ij in range(4):
            tgt[ij] = normed[:, ij * values:(ij + 1) * values] - b2[...].reshape(1, values)
        le = lax.broadcasted_iota(jnp.int32, (n, 1), 0)
        spot = lax.div(le, line) * cols + lax.rem(le, cols) + seq * (hb * cols)
        matches = (spot == marks[...]).astype(F32)
        scale = 2.0 / (4 * values) * jnp.sum(matches, axis=1, keepdims=True)

        step = 16 if mid % 16 == 0 else mid

        def sum_taps(o):
            a, r = lax.div(o, mid // step), lax.rem(o, mid // step)
            w = []
            for bc in range(9):
                part = w2[pl.ds(pl.multiple_of((a * 9 + bc) * mid + r * step, step), step)]
                w2b[bc // 3, pl.ds(pl.multiple_of(a * mid + r * step, step), step),
                    (bc % 3) * values:(bc % 3 + 1) * values] = part
                w.append(part.astype(F32))
            wide = []
            for b in range(3):
                x, y, z_ = w[b * 3:b * 3 + 3]
                wide.append((x, y + z_, x + y, z_))
            for i in range(2):
                for e in range(4):
                    x, y, z_ = wide[0][e], wide[1][e], wide[2][e]
                    for rh, v in enumerate((x, y + z_) if i == 0 else (x + y, z_)):
                        at = (a * 4 + rh * 2 + e % 2) * mid + r * step
                        weff[i * 2 + e // 2, pl.ds(pl.multiple_of(at, step), step)] = v.astype(BF16)

        each(0, 3 * (mid // step), sum_taps)

        def band(size):
            li = lax.broadcasted_iota(jnp.int32, (line, size), 0)
            lw = lax.rem(li, cols)
            return ((lw > 0).astype(F32), (lw < cols - 1).astype(F32),
                    (li >= cols).astype(F32), (li < line - cols).astype(F32))

        w_low, w_high, t_low, t_high = band(mid)
        p_low, p_high, _, _ = band(values)
        le = lax.broadcasted_iota(jnp.int32, (1, ext), 1)
        lw = lax.rem(le, cols)
        lt = lax.rem(le, line)
        s_low, s_high = (lt >= cols).astype(F32), (lt < line - cols).astype(F32)

        def shifted(v, by, mask):
            m = v.shape[0]
            rolled = pltpu.roll(v, (-by) % m, axis=0)
            return (rolled.reshape(m // line, line, v.shape[1]) * mask[None]).reshape(v.shape)

        drain(hraw.at[pl.ds(0, nseq - 1)], h_r.at[0])

        hin = hraw[...].astype(F32)
        hext = jnp.concatenate(
            [hin[:, hh].reshape(line, mid) for hh in range(he)], axis=0)
        for a in range(3):
            late = hext if a == 1 else shifted(
                hext, cols * (a - 1), t_low if a == 0 else t_high)
            for e in range(3):
                v = late if e == 1 else shifted(late, e - 1, w_low if e == 0 else w_high)
                vfield[a * 3 + e] = v.astype(BF16)
        hrow[dp, 0:hb * line] = hext[line:(hb + 1) * line].astype(BF16)
        hrow[dp, hb * line:(hb + 1) * line] = hext[0:line].astype(BF16)
        hrow[dp, (hb + 1) * line:ext] = hext[(hb + 1) * line:ext].astype(BF16)
        mine = hrow.at[dp, pl.ds(0, hb * line)]

        def ht_copy(o):
            d = peer(o)
            return remote(mine, mine, ht_s.at[0], ht_r.at[0], d, seq)

        each(1, ndp, lambda o: ht_copy(o).start())

        def xz_copy(o):
            s = lax.rem(seq + o, nseq)
            return remote(xbuf.at[s], xall.at[dp, seq], xz_s.at[0], xz_r.at[0], dp, s)

        each(1, nseq, lambda o: xz_copy(o).start())
        xall[dp, seq] = xbuf[seq]

        cots = []
        for ij in range(4):
            i, j = ij // 2, ij % 2
            near = []
            for k in range(12):
                low = (i + k // 2 % 2) * line
                near.append(vfield[k // 4 * 3 + j + k % 2, low:low + hb * line])
            predict = jnp.dot(jnp.concatenate(near, axis=1), weff[ij], preferred_element_type=F32)
            cot = (scale * (predict - tgt[ij])).astype(BF16).astype(F32)
            cots.append(cot)
            turned = cot.T
            for d in range(ndp):
                csend[d, ij] = turned[d * vblk:(d + 1) * vblk].astype(BF16)

        def c_copy(o):
            d = peer(o)
            return remote(csend.at[d], call_.at[dp], c_s.at[0], c_r.at[dp], d, seq)

        each(1, ndp, lambda o: c_copy(o).start())
        call_[dp] = csend[dp]

        def pair_sums(low, high, after, before):
            return (high + after(low), low + high, before(high) + low)

        def after_row(v):
            return shifted(v, 1, p_high)

        def before_row(v):
            return shifted(v, -1, p_low)

        for u, (low, high) in enumerate((
                (cots[0], cots[1]), (cots[2], cots[3]),
                (cots[0] + cots[2], cots[1] + cots[3]))):
            for c, s in enumerate(pair_sums(low, high, after_row, before_row)):
                cell[u * n:(u + 1) * n, c * values:(c + 1) * values] = s.astype(BF16)

        both = cell[0:2 * n]
        first = lax.dot_general(both, w2b[0], NT, preferred_element_type=F32)
        third = lax.dot_general(both, w2b[2], NT, preferred_element_type=F32)
        second = lax.dot_general(cell[2 * n:3 * n], w2b[1], NT, preferred_element_type=F32)
        same = first[n:] + second + third[:n]
        pieces = []
        for hh in range(he):
            total = None
            for v, dh in ((first[:n], -1), (same, 0), (third[n:], 1)):
                h = hh - 1 - dh
                if 0 <= h < hb:
                    part = v[h * line:(h + 1) * line]
                    total = part if total is None else total + part
            back = total[:, mid:2 * mid]
            back = back + shifted(total[:, :mid], cols, t_high)
            back = back + shifted(total[:, 2 * mid:], -cols, t_low)
            pieces.append(back)
        for hh in range(he):
            psend[:, hh] = pieces[hh].reshape(nseq, chunk, mid)

        def p_copy(o):
            s = lax.rem(seq + o, nseq)
            return remote(psend.at[s], praw.at[seq], p_s.at[0], p_r.at[0], dp, s)

        each(1, nseq, lambda o: p_copy(o).start())
        praw[seq] = psend[seq]

        drain(hrow.at[pl.ds(0, ndp - 1), pl.ds(0, hb * line)], ht_r.at[0])
        others = pl.ds(0, ndp - 1)

        def edge_copy(o, k):
            q = peer(o)
            if k == 0:
                return remote(hrow.at[q, pl.ds((hb - 1) * line, line)],
                              hrow.at[q, pl.ds(hb * line, line)], e_s.at[0], e_r.at[0], dp,
                              jnp.minimum(seq + 1, nseq - 1))
            return remote(hrow.at[q, pl.ds(0, line)],
                          hrow.at[q, pl.ds((hb + 1) * line, line)], e_s.at[1], e_r.at[1], dp,
                          jnp.maximum(seq - 1, 0))

        def no_edge(k):
            def put(o):
                q = peer(o)
                hrow[q, (hb + k) * line:(hb + k + 1) * line] = jnp.zeros((line, mid), BF16)
            each(1, ndp, put)

        @pl.when(seq < nseq - 1)
        def _():
            each(1, ndp, lambda o: edge_copy(o, 0).start())

        @pl.when(seq > 0)
        def _():
            each(1, ndp, lambda o: edge_copy(o, 1).start())

        @pl.when(seq == 0)
        def _():
            no_edge(0)

        @pl.when(seq == nseq - 1)
        def _():
            no_edge(1)

        lo = lax.broadcasted_iota(jnp.int32, (1, hb * line), 1)
        lw = lax.rem(lo, cols)
        e_low, e_high = (lw > 0).astype(F32), (lw < cols - 1).astype(F32)
        early_rows, late_rows = (lo < (hb - 1) * line).astype(F32), (lo >= line).astype(F32)

        def lane_after(v):
            return pltpu.roll(v, hb * line - 1, axis=1) * e_high

        def lane_before(v):
            return pltpu.roll(v, 1, axis=1) * e_low

        stack[3 * vblk:6 * vblk] = jnp.zeros((3 * vblk, ndp * ext), BF16)

        tile = hb * line

        def clip_stack(q, inner_at, outer_at):
            by_col, by_edge = [], []
            for j in range(2):
                low, high = call_[q, j].astype(F32), call_[q, 2 + j].astype(F32)
                by_col.append((high + pltpu.roll(low, (hb - 1) * line, axis=1) * early_rows,
                               low + high, low + pltpu.roll(high, line, axis=1) * late_rows))
                by_edge.append((low * early_rows, None, high * late_rows))
            at, rim = pl.ds(inner_at, tile), pl.ds(outer_at, 2 * line)
            k = 0
            for b in range(3):
                inner = pair_sums(by_col[0][b], by_col[1][b], lane_after, lane_before)
                outer = (None,) * 3 if b == 1 else pair_sums(
                    by_edge[0][b], by_edge[1][b], lane_after, lane_before)
                for s, r in zip(inner, outer):
                    stack[k * vblk:(k + 1) * vblk, at] = s.astype(BF16)
                    if r is not None:
                        stack[k * vblk:(k + 1) * vblk, rim] = r.astype(BF16)
                    k += 1

        clip_stack(dp, 0, (ndp - 1) * tile)

        def clip_lhs(o, low, high, at):
            size = high - low
            turned = hrow[peer(o), low:high].astype(F32).T
            for a in range(3):
                v = turned
                if a != 1:
                    v = pltpu.roll(turned, (cols if a == 0 else size - cols), axis=1)
                    v = v * (s_low if a == 0 else s_high)[:, low:high]
                lhs[:, a, :, at:at + size] = v.reshape(nseq, mblk, size).astype(BF16)

        for o in range(ndp):
            clip_lhs(o, 0, tile, (ndp if o == ndp - 1 else o) * tile)
        clip_lhs(0, tile, ext, (ndp - 1) * tile)

        def other_clip(o, inner_at):
            q = peer(o)
            drain(call_.at[q], c_r.at[q])
            clip_stack(q, inner_at, pl.multiple_of((ndp + o) * tile, 128))

        each(1, ndp - 1, lambda o: other_clip(o, pl.multiple_of(o * tile, 128)))

        def half(k, j, first_part, last_part):
            depth = (last_part - first_part) * ndp * tile
            span = slice(first_part * ndp * tile, last_part * ndp * tile)
            block = jnp.concatenate(
                [lhs[2 * s + k, :, :, span].reshape(3 * mblk, depth) for s in range(nz)],
                axis=0)
            low, size = cuts[j]
            return lax.dot_general(block, stack[low:low + size, span], NT,
                                   preferred_element_type=F32).reshape(nk, 2, 3 * mblk, size)

        for j in range(len(cuts)):
            acc3[j][...] = half(1 - core, j, 0, 1)

        drain(praw.at[pl.ds(0, nseq - 1)], p_r.at[0])
        got = praw[...].reshape(nseq * he * chunk, mid)
        major = got.astype(BF16)
        minor = (got - major.astype(F32)).astype(BF16)
        grad_h = (jnp.dot(gather_of[...], major, preferred_element_type=F32)
                  + jnp.dot(gather_of[...], minor, preferred_element_type=F32))
        grad_z = (grad_h * slope_of[...]).astype(BF16).astype(F32).T
        for d in range(ndp):
            gsend[d] = grad_z[d * cblk:(d + 1) * cblk].astype(BF16)

        def g_copy(o):
            t = lax.rem(dp * nz + chip + o, ndp * nz)
            d = t // nz
            return remote(gsend.at[d], gall.at[dp, core, chip], g_s.at[0], g_r.at[dp], d,
                          2 * lax.rem(t, nz) + core)

        each(1, ndp * nz, lambda o: g_copy(o).start())
        gall[dp, core, chip] = gsend[dp]
        drain(xall.at[0, pl.ds(0, nseq - 1)], xz_r.at[0])

        def xd_copy(o):
            d = peer(o)
            return remote(xall.at[dp], xall.at[dp], xd_s.at[0], xd_r.at[dp], d, seq)

        each(1, ndp, lambda o: xd_copy(o).start())

        @pl.when(seq > 0)
        def _():
            drain(hrow.at[others, pl.ds(0, line)], e_r.at[0])

        @pl.when(seq < nseq - 1)
        def _():
            drain(hrow.at[others, pl.ds(0, line)], e_r.at[1])

        for o in range(1, ndp):
            clip_lhs(o, tile, ext, (ndp + o) * tile)
        other_clip(ndp - 1, ndp * tile)

        swaps = [remote(qs, qr, q_s.at[j], q_r.at[j], dp, 2 * chip + 1 - core)
                 for j, (qs, qr) in enumerate(zip(qsend, qrecv))]
        for j in range(len(cuts)):
            qsend[j][...] = (acc3[j][...] + half(1 - core, j, 1, 2)).astype(BF16)
            swaps[j].start()
        par, kz = lax.rem(chip, 2), chip // 2

        def g_forward(q):
            return remote(gall.at[q, core], gall.at[q, core], f_s.at[0], f_r.at[q], dp,
                          2 * chip + 1 - core)

        def pass_on(o):
            q = peer(o)
            drain(gall.at[0, 0], g_r.at[q])
            g_forward(q).start()

        def forward_all():
            drain(gall.at[0, 0, pl.ds(0, nz - 1)], g_r.at[dp])
            g_forward(dp).start()
            each(1, ndp, pass_on)

        def near_copy(k):
            return remote(asend.at[k], arecv.at[k], a_s.at[0], a_r.at[0], dp,
                          2 * (chip + 1 - 2 * par) + core)

        def last_copy():
            return remote(asend.at[kz], arecv.at[kz], a_s.at[1], a_r.at[1],
                          dp, 2 * (chip + 1 - 2 * par) + core)

        def far_copy(o):
            k = lax.rem(kz + o, nk)
            return remote(bsend.at[k], brecv.at[kz], b_s.at[0], b_r.at[0], dp,
                          2 * (2 * k + par) + core)

        def r_copy(o):
            t = differ(chip, nz - o, nz)
            return remote(rsend.at[t // 2, lax.rem(t, 2)], rall.at[chip], r_s.at[0], r_r.at[0],
                          dp, 2 * t + core)

        for j in range(len(cuts)):
            acc2[j][...] = half(core, j, 0, 2)
            swaps[j].wait_recv()
            if j > 0:
                rsend[...] = (acc2[j][...] + qrecv[j][...].astype(F32)).astype(BF16)
                each(1, nz, lambda o: r_copy(o).start())
                acc2[j][kz, par] = acc2[j][kz, par] + qrecv[j][kz, par].astype(F32)
                continue
            asend[...] = (acc2[j][:, 1 - par] + qrecv[j][:, 1 - par].astype(F32)).astype(BF16)
            each(1, nk, lambda o: near_copy(lax.rem(kz + o, nk)).start())
            acc2[j][:, par] = acc2[j][:, par] + qrecv[j][:, par].astype(F32)
        lx = lax.broadcasted_iota(jnp.int32, (1, clip_lanes), 1)
        x_low, x_high = (lx >= plane).astype(F32), (lx < clip_lanes - plane).astype(F32)

        def turn_clip(q):
            x = jnp.concatenate([xall[q, s] for s in range(nseq)], axis=1)
            xf = x.astype(F32)
            xs[q, 0:dblk] = (pltpu.roll(xf, plane, axis=1) * x_low).astype(BF16)
            xs[q, dblk:2 * dblk] = x
            xs[q, 2 * dblk:3 * dblk] = (
                pltpu.roll(xf, clip_lanes - plane, axis=1) * x_high).astype(BF16)

        turn_clip(dp)
        acc1[...] = jnp.zeros_like(acc1)
        forward_all()
        drain(asend.at[pl.ds(0, nk - 1)], a_r.at[0])

        def combine(o):
            k = lax.rem(kz + o, nk)
            bsend[k] = (acc2[0][k, par] + arecv[k].astype(F32)).astype(BF16)
            far_copy(o).start()

        each(1, nk, combine)
        last_copy().start()

        lh = lax.rem(lx, rows)
        lc = lax.rem(lx, plane)
        g_h = ((lh < rows - 1).astype(F32), None, (lh > 0).astype(F32))
        g_w = ((lc < plane - rows).astype(F32), None, (lc >= rows).astype(F32))

        def one_first(q):
            g = jnp.concatenate([gall[q, s % 2, s // 2].astype(F32) for s in range(nseq)], axis=1)
            grid = []
            for b in range(3):
                v = g if b == 1 else pltpu.roll(g, (b - 1) % clip_lanes, axis=1) * g_h[b]
                for c in range(3):
                    u = v if c == 1 else pltpu.roll(
                        v, ((c - 1) * rows) % clip_lanes, axis=1) * g_w[c]
                    grid.append(u.astype(BF16))
            acc1[...] += lax.dot_general(jnp.concatenate(grid, axis=0), xs[q], NT,
                                         preferred_element_type=F32)

        drain(gall.at[0, 0], f_r.at[dp])
        one_first(dp)

        def arrived_first(o):
            q = peer(o)
            drain(xall.at[0], xd_r.at[q])
            turn_clip(q)
            drain(gall.at[0, 0], f_r.at[q])
            one_first(q)

        each(1, ndp, arrived_first)
        for a in range(3):
            o1[a * 9 * cblk:(a + 1) * 9 * cblk] = acc1[:, a * dblk:(a + 1) * dblk]

        @pl.when(seq < nseq - 1)
        def _():
            up.wait_send()

        @pl.when(seq > 0)
        def _():
            down.wait_send()

        drain(hsend.at[pl.ds(0, nseq - 1)], h_s.at[0])
        drain(xbuf.at[pl.ds(0, nseq - 1)], xz_s.at[0])
        drain(hrow.at[pl.ds(0, ndp - 1), pl.ds(0, hb * line)], ht_s.at[0])
        drain(csend.at[pl.ds(0, ndp - 1)], c_s.at[0])
        drain(psend.at[pl.ds(0, nseq - 1)], p_s.at[0])
        drain(xall.at[pl.ds(0, ndp - 1)], xd_s.at[0])
        for w in swaps:
            w.wait_send()
        for o in range(ndp):
            drain(gall.at[0, 0, pl.ds(0, nz - 1)] if o == 0 else gall.at[0, 0], g_s.at[0])
        drain(gall.at[:, 0], f_s.at[0])
        @pl.when(seq < nseq - 1)
        def _():
            drain(hrow.at[others, pl.ds(0, line)], e_s.at[0])

        @pl.when(seq > 0)
        def _():
            drain(hrow.at[others, pl.ds(0, line)], e_s.at[1])

        totals = []
        drain(asend.at[0], a_r.at[1])
        acc2[0][kz, par] = acc2[0][kz, par] + arecv[kz].astype(F32)
        drain(brecv.at[pl.ds(0, nk - 1)], b_r.at[0])

        def add(o):
            acc2[0][kz, par] = (acc2[0][kz, par]
                                     + brecv[lax.rem(kz + o, nk)].astype(F32))

        each(1, nk, add)
        totals.append(acc2[0][kz, par])
        if len(cuts) > 1:
            drain(rall.at[pl.ds(0, nz - 1)], r_r.at[0])
            total = acc2[1][kz, par]
            for o in range(1, nz):
                total = total + rall[differ(chip, o, nz)].astype(F32)
            totals.append(total)
        total = jnp.concatenate(totals, axis=1)
        for a in range(3):
            for bc in range(9):
                o2[a * 9 + bc] = total[a * mblk:(a + 1) * mblk, bc * vblk:(bc + 1) * vblk]
        if len(cuts) > 1:
            drain(rall.at[pl.ds(0, nz - 1)], r_s.at[0])
        drain(asend.at[pl.ds(0, nk - 1)], a_s.at[0])
        drain(asend.at[0], a_s.at[1])
        drain(brecv.at[pl.ds(0, nk - 1)], b_s.at[0])

    return kernel


def flush(a, b, oa, ob, sem):
    moves = (pltpu.make_async_copy(a, oa, sem.at[0]), pltpu.make_async_copy(b, ob, sem.at[1]))
    for m in moves:
        m.start()
    for m in moves:
        m.wait()


def per_device(tokens, conv_first, bias_first, conv_second, bias_second, pixels, mask_index):
    ndp, nseq = lax.axis_size("dp"), lax.axis_size("seq")
    tf, rows, cols, width = tokens.shape[1:]
    frames = tf * nseq
    mid, values = conv_second.shape[1], conv_second.shape[2]
    n = tf * rows * cols
    hb = rows // nseq
    he = hb + 2
    line = frames * cols
    ext = he * line
    chunk = tf * cols
    dims = (ndp, nseq, tf, rows, cols, width, mid, values)
    plane = rows * cols
    dblk, cblk, vblk, mblk = width // nseq, mid // ndp, values // ndp, mid // nseq
    nz = nseq // 2
    cuts = columns(9 * vblk)

    idx = np.arange(n, dtype=np.int32)
    t_of, w_of, h_of = idx // plane, idx // rows % cols, idx % rows
    flat_place = (h_of * cols + w_of)[:plane]
    tperm = jnp.asarray(flat_place[:, None] == idx[None, :plane], BF16)
    msg = np.arange(nseq * he * chunk, dtype=np.int32)
    m_s, m_h = msg // (he * chunk), msg // chunk % he
    m_t, m_w = msg % chunk // cols, msg % cols
    m_row = m_s * hb + m_h - 1
    same = ((m_row[:, None] == h_of[None]) & (m_t[:, None] == t_of[None])
            & (m_w[:, None] == w_of[None]))
    spread_of = jnp.asarray(same, BF16)
    gather_of = jnp.asarray(same.T, BF16)
    vm = pl.BlockSpec(memory_space=pltpu.VMEM)
    hbm = pl.BlockSpec(memory_space=pl.ANY)

    def dma(k):
        return pltpu.SemaphoreType.DMA((k,))

    scratch = [
        pltpu.VMEM((tf, rows, cols, width), BF16),
        pltpu.VMEM((1, mid), F32),
        pltpu.VMEM((values,), F32),
        pltpu.VMEM(mask_index.shape, jnp.int32),
        pltpu.VMEM((plane, plane), BF16),
        pltpu.VMEM((nseq * he * chunk, n), BF16),
        pltpu.VMEM((n, nseq * he * chunk), BF16),
        pltpu.VMEM((9 * width, 3 * mid), BF16),
        pltpu.VMEM((27 * mid, values), BF16),
        pltpu.VMEM((3, 3 * mid, 3 * values), BF16),
        pltpu.VMEM((4, 12 * mid, values), BF16),
        pltpu.VMEM((frames, hb, cols, 4 * values), BF16),
        pltpu.VMEM((nseq, dblk, n), BF16),
        pltpu.VMEM((ndp, nseq, dblk, n), BF16),
        pltpu.VMEM((ndp, 3 * dblk, nseq * n), BF16),
        pltpu.VMEM((2, plane, mid), F32),
        pltpu.VMEM((2, plane, mid), F32),
        pltpu.VMEM((3, tf, cols + 2, rows, width), BF16),
        pltpu.VMEM((n, 9 * width), BF16),
        pltpu.VMEM((n, mid), F32),
        pltpu.VMEM((nseq, he, chunk, mid), BF16),
        pltpu.VMEM((nseq, he, chunk, mid), BF16),
        pltpu.VMEM((9, ext, mid), BF16),
        pltpu.VMEM((4, n, values), F32),
        pltpu.VMEM((3 * n, 3 * values), BF16),
        pltpu.VMEM((nseq, he, chunk, mid), F32),
        pltpu.VMEM((nseq, he, chunk, mid), F32),
        pltpu.VMEM((ndp, ext, mid), BF16),
        pltpu.VMEM((nseq, 3, mblk, ndp * ext), BF16),
        pltpu.VMEM((ndp, 4, vblk, n), BF16),
        pltpu.VMEM((ndp, 4, vblk, n), BF16),
        pltpu.VMEM((9 * vblk, ndp * ext), BF16),
        pltpu.VMEM((ndp, cblk, n), BF16),
        pltpu.VMEM((ndp, 2, nz, cblk, n), BF16),
        pltpu.VMEM((9 * cblk, 3 * dblk), F32),
        pltpu.VMEM((nz // 2, 2, 3 * mblk, cuts[-1][1]), BF16),
        pltpu.VMEM((nz, 3 * mblk, cuts[-1][1]), BF16),
    ] + [pltpu.VMEM((nz // 2, 3 * mblk, cuts[0][1]), BF16)] * 4 + [
        [[pltpu.VMEM((nz // 2, 2, 3 * mblk, size), kind) for _, size in cuts]
         for kind in (BF16, BF16, F32, F32)],
        dma(15), dma(2), dma(2), dma(1), dma(1), dma(1), dma(1), dma(ndp), dma(1), dma(2),
        dma(ndp), dma(ndp), dma(ndp), dma(len(cuts)), dma(1), dma(2), dma(1),
    ]
    first, second = pl.pallas_call(
        make_kernel(dims),
        out_shape=(pltpu.VMEM((27 * cblk, dblk), F32), pltpu.VMEM((27, mblk, vblk), F32)),
        in_specs=[hbm] * 10,
        out_specs=(vm, vm),
        scratch_shapes=scratch,
        compiler_params=pltpu.CompilerParams(
            collective_id=0, has_side_effects=True, vmem_limit_bytes=60 * 1024 * 1024),
        name="step",
    )(tokens[0], conv_first.reshape(27 * width, mid), bias_first.reshape(1, mid),
      conv_second.reshape(27 * mid, values), bias_second,
      pixels[0], mask_index, tperm, spread_of, gather_of)
    first, second = pl.pallas_call(
        flush,
        out_shape=(jax.ShapeDtypeStruct(first.shape, F32), jax.ShapeDtypeStruct(second.shape, F32)),
        in_specs=[vm, vm],
        out_specs=(hbm, hbm),
        scratch_shapes=[dma(2)],
        compiler_params=pltpu.CompilerParams(vmem_limit_bytes=4 * 1024 * 1024),
        name="flush",
    )(pltpu.with_memory_space_constraint(first, pltpu.VMEM),
      pltpu.with_memory_space_constraint(second, pltpu.VMEM))
    first = first.reshape(27, cblk, dblk).transpose(0, 2, 1)
    return (first, second)


def solution(mesh):
    return jax.shard_map(
        per_device,
        mesh=mesh,
        in_specs=(
            P("dp", "seq", None, None, None),
            P(),
            P(),
            P(),
            P(),
            P("dp", None, "seq", None, None),
            P("dp", None),
        ),
        out_specs=(P(None, "seq", "dp"), P(None, "seq", "dp")),
        check_vma=False,
    )
```
